256 devices in a mesh: tm: 64 (over z_hi, y, x), freq: 4 (over z_lo, core).
Axes of the slice: x: 4, y: 4, z: 8 (z_hi: 4, z_lo: 2; z = z_hi * 2 + z_lo), core: 2. Of those that a mesh axis runs over, the one named last changes fastest.
Arguments:
- spectrum: bfloat16 [1024, 49152], P('freq', 'tm'), may hold values from 0.0099487305 to 10
- decay_rate: float32 [1024], P('freq'), may hold values from 1e-07 to 0.03
- init_state: float32 [1024], P('freq'), may hold values from 0.3 to 3
- clip_ids: int32 [49152], P('tm'), may hold values from 0 to 5, never falling along the last dimension, each value on 1 to 16384 neighbouring positions
- encoder: bfloat16 [256, 1024], P(None, 'freq'), may hold values from -0.1875 to 0.1875
- gauss_noise: float32 [256, 49152], P(None, 'tm'), may hold values from -3 to 3
- uniform_noise: float32 [2, 256, 49152], P(None, None, 'tm'), may hold values from 0.02 to 1
- boost_count: int32 [256], replicated, may hold values from 1 to 2
- templates: bfloat16 [1024, 4096], P('freq'), may hold values from 0.0099487305 to 1
Outputs:
- frame_loss: float32 [49152], P('tm')
- template_grad: float32 [4096, 1024], P('tm', 'freq')
The draws below stay inside these ranges and needn't reach their ends.
Inputs may be any that keep to these rules, and one draw needn't show every extreme that they name: `clip_ids`: clip numbers never fall along the frames; each clip holds 1 to 16384 frames, one exactly that many.
All inputs are finite; a program needn't handle non-finite values.
Results may differ from the reference program's by a relative error of at most 0.00033.
Values may be sent and summed in bfloat16 or wider, within the bound.
A program may use at most 64 MiB of HBM per device.

```python
import math
import jax
import jax.numpy as jnp
import numpy as np
from jax import lax

F = 1024
K = 256
L = 16
CLIPS = 6
TIME = 49152


def with_ends(entries, own_key, low, top_value):
    spot = [jax.random.randint(jax.random.fold_in(own_key, axis), (), 0, length) for axis, length in enumerate(entries.shape)]
    widest = entries.shape.index(max(entries.shape))
    beside = spot[:widest] + [(spot[widest] + 1) % entries.shape[widest]] + spot[widest + 1:]
    return entries.at[tuple(spot)].set(low).at[tuple(beside)].set(top_value)


def block_levels(key, extent, pieces, low, top_value):
    level, own = 1.0, jax.random.fold_in(key, 6)
    for dim, blocks in pieces:
        steps = jnp.exp(jax.random.uniform(jax.random.fold_in(own, dim), (blocks,), jnp.float32, low / len(pieces), top_value / len(pieces)))
        level = level * jnp.repeat(steps, extent[dim] // blocks).reshape([-1 if axis == dim else 1 for axis in range(len(extent))])
    return level


def profile(count, total, most, skew):
    weights = [(1 << 20) // math.isqrt(grade ** skew) + 1 for grade in range(2, count + 1)]
    surplus, holding = total - most - (count - 1), [1] * (count - 1)
    while surplus > 0:
        free = [i for i in range(count - 1) if holding[i] < most]
        mass, remaining = sum([weights[i] for i in free]), surplus
        for i in free:
            extra = min(most - holding[i], max(1, remaining * weights[i] // mass), surplus)
            holding[i] = holding[i] + extra
            surplus = surplus - extra
    return np.array([most] + holding)


def uneven(key, count, total, limit, slope):
    if count == 2:
        one = jax.random.randint(key, (), max(1, total - limit), min(limit, total - 1) + 1)
        return jnp.stack([one, total - one])
    sizes = jnp.asarray(profile(count, total, limit, slope), jnp.int32)
    couples = (count - 1) // 2
    donor, receiver = sizes[1:1 + 2 * couples:2], sizes[2:2 + 2 * couples:2]
    room = jnp.minimum(donor - 1, limit - receiver)
    shifted = jax.random.randint(jax.random.fold_in(key, 1), (couples,), 0, 1 << 20) % (room + 1)
    sizes = sizes.at[1:1 + 2 * couples:2].set(donor - shifted).at[2:2 + 2 * couples:2].set(receiver + shifted)
    return sizes[jax.random.permutation(jax.random.fold_in(key, 2), count)]


def normal_values(key, shape, scale, reach, shards=(), held_as=jnp.bfloat16):
    values = scale * jax.random.normal(key, shape, jnp.float32)
    if shards:
        values = values * block_levels(key, shape, shards, -0.22, 0.18)
    return jnp.clip(values, -reach, reach).astype(held_as)


def setup_inputs(seed: int = 0) -> dict:
    arg_keys = jax.random.split(jax.random.key(seed), 10)
    spectrum = jnp.clip(jnp.exp(math.log(10.0) - 6.912895 * jax.random.uniform(arg_keys[0], (F, TIME), jnp.float32) ** block_levels(arg_keys[0], (F, TIME), ((0, 4), (1, 64)), -0.2, 0.2)), 0.0099487305, 10.0).astype(jnp.bfloat16)
    decay_rate = jnp.clip(jnp.exp(math.log(0.03) - 12.611538 * jax.random.uniform(arg_keys[1], (F,), jnp.float32) ** block_levels(arg_keys[1], (F,), ((0, 4),), -0.2, 0.2)), 1.0000000116860974e-07, 0.03)
    init_state = jnp.clip(jnp.exp(math.log(3.0) - 2.3025851 * jax.random.uniform(arg_keys[2], (F,), jnp.float32) ** block_levels(arg_keys[2], (F,), ((0, 4),), -0.2, 0.2)), 0.3, 3.0)
    clip_ids = jnp.searchsorted(jnp.cumsum(uneven(arg_keys[3], CLIPS, TIME, TIME // 3, 0)), jnp.arange(TIME), side="right").astype(jnp.int32)
    encoder = normal_values(arg_keys[4], (K, F), F ** -0.5, 0.1875, ((1, 4),))
    gauss_noise = normal_values(arg_keys[5], (K, TIME), 1.0, 3.0, ((1, 64),), jnp.float32)
    uniform_noise = jnp.clip(0.02 + 0.98 * jax.random.uniform(arg_keys[6], (2, K, TIME), jnp.float32) ** block_levels(arg_keys[6], (2, K, TIME), ((2, 64),), -0.2, 0.2), 0.02, 1.0)
    boost_count = with_ends(jax.random.randint(arg_keys[7], (K,), 1, 3), jax.random.fold_in(arg_keys[7], 1), 1, 2).astype(jnp.int32)
    templates = jnp.clip(jnp.exp(math.log(1.0) - 4.61031033 * jax.random.uniform(arg_keys[8], (F, K * L), jnp.float32) ** block_levels(arg_keys[8], (F, K * L), ((0, 4),), -0.2, 0.2)), 0.0099487305, 1.0).astype(jnp.bfloat16)
    return {"spectrum": spectrum, "decay_rate": decay_rate, "init_state": init_state, "clip_ids": clip_ids, "encoder": encoder, "gauss_noise": gauss_noise, "uniform_noise": uniform_noise, "boost_count": boost_count, "templates": templates}


def compose(former, latter):
    return (former[0] * latter[0], latter[0] * former[1] + latter[1])

def topic_mixture(logits, gaussian, uniforms, boost_count):
    concentration = jax.nn.softplus(logits) + 0.5
    boosted = boost_count[:, None]
    shape_total = concentration + boosted.astype(jnp.float32)
    offset = shape_total - 1.0 / 3.0
    spread = lax.rsqrt(9.0 * offset)
    linear = 1.0 + spread * gaussian
    gamma_draw = offset * linear * linear * linear * jnp.exp(jnp.log(uniforms[0]) / concentration)
    gamma_draw = gamma_draw * jnp.where(boosted >= 2, jnp.exp(jnp.log(uniforms[1]) / (concentration + 1.0)), 1.0)
    return (gamma_draw / lax.optimization_barrier(jnp.sum(gamma_draw, axis=0, keepdims=True))).astype(jnp.bfloat16)

def reference(spectrum, decay_rate, init_state, clip_ids, encoder, gauss_noise, uniform_noise, boost_count, templates):
    spectral = spectrum.astype(jnp.float32)
    changed = clip_ids[1:] != clip_ids[:-1]
    factor_row = jnp.concatenate([jnp.ones((1,), jnp.float32), jnp.where(changed, 0.8, 1.0).astype(jnp.float32)])
    rates = (1.0 - decay_rate)[:, None] * factor_row[None, :]
    inputs = decay_rate[:, None] * spectral
    running, summed = lax.associative_scan(compose, (rates, inputs), axis=1)
    smooth = running * init_state[:, None] + summed
    normed = (spectral * lax.rsqrt(smooth + 0.1)).astype(jnp.bfloat16)
    logits = jnp.dot(encoder, normed, preferred_element_type=jnp.float32)
    proportions = topic_mixture(logits, gauss_noise, uniform_noise, boost_count)
    block_len = math.gcd(TIME, 1024)
    blocks = TIME // block_len
    scale_factor = F * K / TIME
    theta_pad = jnp.concatenate([jnp.zeros((K, L - 1), jnp.bfloat16), proportions], axis=1)
    clip_pad = jnp.concatenate([jnp.full((L - 1,), -1, jnp.int32), clip_ids.astype(jnp.int32)])

    def one_block(total, index):
        start = (index * block_len).astype(jnp.int32)
        extended = lax.dynamic_slice_in_dim(theta_pad, start, block_len + L - 1, 1)
        clip_ext = lax.dynamic_slice_in_dim(clip_pad, start, block_len + L - 1, 0)
        current = clip_ext[L - 1:]
        lag_rows = []
        mask_rows = []
        for lag in range(L):
            begin = L - 1 - lag
            lag_rows.append(extended[:, begin:begin + block_len])
            mask_rows.append(clip_ext[begin:begin + block_len] == current)
        valid = jnp.stack(mask_rows).astype(jnp.bfloat16)
        stacked = (jnp.stack(lag_rows, axis=1) * valid[None]).reshape(K * L, block_len)
        local_spec = lax.dynamic_slice_in_dim(spectral, start, block_len, 1)
        recon = jnp.dot(templates, stacked, preferred_element_type=jnp.float32)
        recon_sum = lax.optimization_barrier(jnp.sum(recon, axis=0))
        spec_sum = lax.optimization_barrier(jnp.sum(local_spec, axis=0))
        log_sum = lax.optimization_barrier(jnp.sum(local_spec * jnp.log(recon), axis=0))
        frame_loss = jnp.log(recon_sum) - log_sum / spec_sum
        ratio = (scale_factor * (1.0 / recon_sum[None, :] - local_spec / (spec_sum[None, :] * recon))).astype(jnp.bfloat16)
        grad_term = lax.dot_general(stacked, ratio, (((1,), (1,)), ((), ())), preferred_element_type=jnp.float32)
        return (total + grad_term, frame_loss)
    indices = jnp.arange(blocks, dtype=jnp.int32)
    template_grad, losses = lax.scan(one_block, jnp.zeros((K * L, F), jnp.float32), indices)
    return (losses.reshape(TIME), template_grad)
```

```python
import jax
import jax.numpy as jnp
from jax import lax
from jax.experimental import pallas as pl
from jax.experimental.pallas import tpu as pltpu
from jax.sharding import PartitionSpec as P

F = 1024
K = 256
L = 16
TIME = 49152
BINS = 256
FRAMES = 768
TILES = 6
TM = 64
NF = 4
MESH = pl.DeviceIdType.MESH
f32 = jnp.float32
bf16 = jnp.bfloat16
LOG_GAIN = 0.22314355131420976
OWNER = (0, 0, 1, 2, 2, 3)
SLOT = (0, 1, 0, 0, 1, 0)


def remote(src, dst, send, recv, tm, fq):
    return pltpu.make_async_remote_copy(
        src_ref=src, dst_ref=dst, send_sem=send, recv_sem=recv,
        device_id={"tm": tm, "freq": fq}, device_id_type=MESH,
    )


def kernel(
    spec_ref, decay_ref, init_ref, ids_ref, enc_ref, boost_ref, gauss_hbm, unif_hbm, tmpl_hbm,
    loss_ref, out_ref,
    tmpl, gbuf, ubuf, encf, grow, cum, normed, nbuf, pbuf, pf, idh, qsend, qbuf, st,
    recon, sbuf, rat, grad, a1, c3, r1, r2, r3,
    load_sem, enc_s, enc_r, q_s, q_r, id_s, id_r, n_s, n_r, p_s, p_r, h_s, h_r, s_s, s_r,
    rs1_s, rs1_r, rs2_s, rs2_r, rs3_s, rs3_r,
):
    tm = lax.axis_index("tm")
    fq = lax.axis_index("freq")
    core = lax.rem(fq, 2)
    zlo = fq // 2
    barrier = pltpu.get_barrier_semaphore()
    nxt = lax.rem(tm + 1, TM)
    prv = lax.rem(tm + TM - 1, TM)

    def greet(i, carry):
        pl.semaphore_signal(
            barrier, inc=1, device_id={"tm": lax.rem(tm + i, TM), "freq": fq}, device_id_type=MESH)
        return carry

    lax.fori_loop(1, TM, greet, 0)
    for i in range(1, NF):
        other = lax.rem(fq + i, NF)
        for place in (tm, nxt, prv):
            pl.semaphore_signal(
                barrier, inc=1, device_id={"tm": place, "freq": other}, device_id_type=MESH)

    first = zlo * 3 + core * 2
    load_t = pltpu.make_async_copy(tmpl_hbm, tmpl, load_sem.at[0])
    load_t.start()

    def tile_loads(slot):
        cols = pl.ds(pl.multiple_of((first + slot) * 128, 128), 128)
        return (
            pltpu.make_async_copy(gauss_hbm.at[:, cols], gbuf.at[slot], load_sem.at[1 + 2 * slot]),
            pltpu.make_async_copy(unif_hbm.at[:, :, cols], ubuf.at[slot], load_sem.at[2 + 2 * slot]),
        )

    for copy in tile_loads(0):
        copy.start()

    @pl.when(core == 0)
    def _():
        for copy in tile_loads(1):
            copy.start()

    rows = lax.broadcasted_iota(jnp.int32, (BINS, BINS), 0)
    cols = lax.broadcasted_iota(jnp.int32, (BINS, BINS), 1)
    eye = rows == cols
    tri = (rows <= cols).astype(bf16)

    def column(row):
        return jnp.sum(jnp.where(eye, jnp.broadcast_to(row, (BINS, BINS)), 0.0), axis=1, keepdims=True)

    def row_of(col):
        return jnp.sum(jnp.where(eye, jnp.broadcast_to(col, (BINS, BINS)), 0.0), axis=0, keepdims=True)

    decay_row = decay_ref[...]
    lost = 1.0 - (1.0 - decay_row)
    log_row = -lost * (1.0 + lost * (1 / 2 + lost * (1 / 3 + lost * (1 / 4 + lost * (1 / 5 + lost * (1 / 6))))))
    log_col = column(log_row)
    decay_col = column(decay_row)
    ids = ids_ref[...].astype(f32)
    lift = jnp.exp(ids * LOG_GAIN)
    carry = jnp.zeros((BINS, 1), f32)
    for b in range(3):
        span = slice(b * 256, b * 256 + 256)
        steps = (cols + (b * 256 + 1)).astype(f32)
        power = steps * log_col
        grow[:, span] = jnp.exp(power)
        v = decay_col * (spec_ref[:, span].astype(f32) * lift[:, span]) * jnp.exp(-power)
        hi = v.astype(bf16)
        rest = v - hi.astype(f32)
        mid = rest.astype(bf16)
        low = (rest - mid.astype(f32)).astype(bf16)
        c = (
            jnp.dot(hi, tri, preferred_element_type=f32)
            + jnp.dot(mid, tri, preferred_element_type=f32)
            + jnp.dot(low, tri, preferred_element_type=f32)
        ) + carry
        cum[:, span] = c
        carry = c[:, 255:256]
    q_col = carry * jnp.exp(log_col * float(FRAMES))
    qsend[...] = row_of(q_col)

    pl.semaphore_wait(barrier, TM - 1 + 3 * (NF - 1))

    def q_copy(place):
        return remote(qsend, qbuf.at[tm], q_s.at[place], q_r.at[tm], place, fq)

    def q_start(i, carry):
        q_copy(i).start()
        return carry

    lax.fori_loop(tm + 1, TM, q_start, 0)

    def enc_copy(i):
        return remote(enc_ref, encf.at[fq], enc_s.at[i], enc_r.at[i], tm, lax.rem(fq + i, NF))

    for i in range(1, NF):
        enc_copy(i).start()
    id_copy = remote(ids_ref.at[:, pl.ds(FRAMES - 128, 128)], idh, id_s, id_r, nxt, fq)

    @pl.when(tm < TM - 1)
    def _():
        id_copy.start()

    encf[fq] = enc_ref[...]

    boost = column(boost_ref[...].astype(f32))

    def ready_noise(slot):
        for copy in tile_loads(slot):
            copy.wait()
        ubuf[slot] = jnp.log(ubuf[slot])

    ready_noise(0)

    @pl.when(core == 0)
    def _():
        ready_noise(1)

    def q_wait(j, carry):
        remote(qsend, qbuf.at[j], q_s.at[j], q_r.at[j], tm, fq).wait_recv()
        return carry

    lax.fori_loop(0, tm, q_wait, 0)
    jump = jnp.exp(log_row * float(FRAMES))
    entry = lax.fori_loop(0, tm, lambda j, e: jump * e + qbuf[j], init_ref[...])
    entry_col = column(entry)
    for t in range(TILES):
        span = slice(t * 128, t * 128 + 128)
        drop = jnp.exp(ids[:, span] * (-LOG_GAIN))
        smooth = grow[:, span] * (entry_col + cum[:, span]) * drop
        normed[t] = (spec_ref[:, span].astype(f32) * lax.rsqrt(smooth + 0.1)).astype(bf16)

    def n_copy(t):
        return remote(
            normed.at[t], nbuf.at[SLOT[t], fq], n_s.at[t], n_r.at[SLOT[t], fq], tm, OWNER[t])

    for t in (3, 4, 5, 0, 1, 2):
        @pl.when(fq != OWNER[t])
        def _(t=t):
            n_copy(t).start()

        @pl.when(fq == OWNER[t])
        def _(t=t):
            nbuf[SLOT[t], fq] = normed[t]

    for i in range(1, NF):
        src = lax.rem(fq + NF - i, NF)
        remote(enc_ref, encf.at[src], enc_s.at[i], enc_r.at[i], tm, fq).wait_recv()

    def p_copy(t, i):
        return remote(pbuf.at[1 + t], pbuf.at[1 + t], p_s.at[t, i], p_r.at[t], tm, lax.rem(fq + i, NF))

    def halo_copy(q):
        return remote(pbuf.at[TILES], pbuf.at[0], h_s.at[q], h_r, nxt, q)

    def sample(slot):
        for i in range(1, NF):
            src = lax.rem(fq + i, NF)
            remote(normed.at[0], nbuf.at[slot, src], n_s.at[0], n_r.at[slot, src], tm, fq).wait_recv()
        logits = jnp.dot(encf[0], nbuf[slot, 0], preferred_element_type=f32)
        for q in range(1, NF):
            logits += jnp.dot(encf[q], nbuf[slot, q], preferred_element_type=f32)
        conc = jnp.maximum(logits, 0.0) + jnp.log(1.0 + jnp.exp(-jnp.abs(logits))) + 0.5
        offset = conc + boost - 1.0 / 3.0
        linear = 1.0 + lax.rsqrt(9.0 * offset) * gbuf[slot]
        second = jnp.where(boost >= 1.5, ubuf[slot, 1], 0.0)
        power = ubuf[slot, 0] / conc + second / (conc + 1.0)
        draw = offset * linear * linear * linear * jnp.exp(power)
        total = jnp.sum(draw, axis=0, keepdims=True)
        pbuf[1 + first + slot] = (draw / total).astype(bf16)

    sample(0)
    for t in range(TILES):
        if SLOT[t] == 0:
            @pl.when(fq == OWNER[t])
            def _(t=t):
                for i in range(1, NF):
                    p_copy(t, i).start()

    @pl.when((fq == NF - 1) & (tm < TM - 1))
    def _():
        for q in range(NF):
            halo_copy(q).start()

    @pl.when(core == 0)
    def _():
        sample(1)

    for t in range(TILES):
        if SLOT[t] == 1:
            @pl.when(fq == OWNER[t])
            def _(t=t):
                for i in range(1, NF):
                    p_copy(t, i).start()

    @pl.when(tm == 0)
    def _():
        pbuf[0] = jnp.zeros((K, 128), bf16)
        idh[...] = jnp.full((1, 128), -1, jnp.int32)

    @pl.when(tm > 0)
    def _():
        id_copy.wait_recv()
        halo_copy(0).wait_recv()

    for t in range(TILES):
        @pl.when(fq != OWNER[t])
        def _(t=t):
            p_copy(t, 1).wait_recv()

    lane = lax.broadcasted_iota(jnp.int32, (L, 128), 1)
    lag = lax.broadcasted_iota(jnp.int32, (L, 128), 0)
    head = lane < lag

    def lagged(row):
        return pltpu.roll(jnp.broadcast_to(row, (L, 128)), 0, 1, stride=1, stride_axis=0)

    id_rows = [idh[...].astype(f32)] + [ids[:, t * 128:t * 128 + 128] for t in range(TILES)]
    rolled = [lagged(r) for r in id_rows]
    keep = []
    for t in range(TILES):
        source = jnp.where(head, rolled[t], rolled[t + 1])
        keep.append(source == jnp.broadcast_to(id_rows[t + 1], (L, 128)))

    for t in range(TILES + 1):
        pf[t] = pbuf[t].astype(f32)

    def build_row(k, carry):
        prior = lagged(pf[0, pl.ds(k, 1), :])
        for t in range(TILES):
            current = lagged(pf[t + 1, pl.ds(k, 1), :])
            value = jnp.where(keep[t], jnp.where(head, prior, current), 0.0)
            st[pl.ds(pl.multiple_of(k * L, L), L), t * 128:t * 128 + 128] = value.astype(bf16)
            prior = current
        return carry

    lax.fori_loop(0, K, build_row, 0, unroll=4)

    load_t.wait()
    for b in range(3):
        span = slice(b * 256, b * 256 + 256)
        rec = jnp.dot(tmpl[...], st[:, span], preferred_element_type=f32)
        x = spec_ref[:, span].astype(f32)
        recon[:, span] = x / rec
        sbuf[fq, 0:1, span] = jnp.sum(rec, axis=0, keepdims=True)
        sbuf[fq, 1:2, span] = jnp.sum(x, axis=0, keepdims=True)
        sbuf[fq, 2:3, span] = jnp.sum(x * jnp.log(rec), axis=0, keepdims=True)

    def s_copy(i):
        return remote(sbuf.at[fq], sbuf.at[fq], s_s.at[i], s_r.at[i], tm, lax.rem(fq + i, NF))

    for i in range(1, NF):
        s_copy(i).start()
    for i in range(1, NF):
        src = lax.rem(fq + NF - i, NF)
        remote(sbuf.at[src], sbuf.at[src], s_s.at[i], s_r.at[i], tm, fq).wait_recv()
    sums = sbuf[0, 0:3, :] + sbuf[1, 0:3, :] + sbuf[2, 0:3, :] + sbuf[3, 0:3, :]
    recon_sum, spec_sum, log_sum = sums[0:1], sums[1:2], sums[2:3]
    loss_ref[...] = jnp.log(recon_sum) - log_sum / spec_sum
    scale = F * K / TIME
    plain = scale / recon_sum
    part = scale / spec_sum
    rat[...] = (plain - part * recon[...]).astype(bf16)

    def grads(z, carry):
        g = lax.dot_general(
            st[pl.ds(pl.multiple_of(z * 1024, 1024), 1024), :], rat[...],
            (((1,), (1,)), ((), ())), preferred_element_type=f32)
        g = g.reshape(4, 4, 64, 256)
        grad[0, z] = g[..., 0:128]
        grad[1, z] = g[..., 128:256]
        return carry

    lax.fori_loop(0, 4, grads, 0)

    px = lax.rem(tm, 4)
    py = lax.rem(tm // 4, 4)
    pz = tm // 16

    def along(axis, step):
        if axis == 0:
            return tm - px + lax.rem(px + step, 4)
        if axis == 1:
            return tm - 4 * py + 4 * lax.rem(py + step, 4)
        return tm - 16 * pz + 16 * lax.rem(pz + step, 4)

    class Stage:
        def __init__(self, view, buf, send, recv, axis, pos):
            self.view, self.buf, self.send, self.recv = view, buf, send, recv
            self.right, self.left = along(axis, 1), along(axis, 3)
            self.p1, self.p2, self.p3 = (lax.rem(pos + i, 4) for i in (1, 2, 3))

        def copy(self, n):
            d, h, to = (
                (self.p2, 0, self.right), (self.p1, 1, self.right), (self.p1, 0, self.right),
                (self.p2, 1, self.left), (self.p3, 0, self.left), (self.p3, 1, self.left),
            )[n]
            return remote(
                self.view(d, h), self.buf.at[n], self.send.at[n], self.recv.at[n], to, fq)

        def begin(self):
            for n in (0, 3, 1, 4):
                self.copy(n).start()

        def relay(self):
            self.copy(0).wait_recv()
            v = self.view(self.p1, 0)
            v[...] = v[...] + self.buf[0]
            self.copy(2).start()
            self.copy(3).wait_recv()
            v = self.view(self.p3, 1)
            v[...] = v[...] + self.buf[3]
            self.copy(5).start()

        def finish(self):
            for n in (1, 4, 2, 5):
                self.copy(n).wait_recv()

        def drain(self):
            for n in range(6):
                self.copy(n).wait_send()

    sx = Stage(lambda d, h: grad.at[0, pl.ds(2 * h, 2), :, d], r1.at[0], rs1_s.at[0], rs1_r.at[0], 0, px)
    sy = Stage(lambda d, h: grad.at[1, pl.ds(2 * h, 2), d, :], r1.at[1], rs1_s.at[1], rs1_r.at[1], 1, py)
    sx.begin()
    sy.begin()
    sx.relay()
    sy.relay()
    sx.finish()
    a1[0, 0:2] = grad[0, 0:2, :, px] + r1[0, 2] + r1[0, 4]
    a1[0, 2:4] = grad[0, 2:4, :, px] + r1[0, 1] + r1[0, 5]
    s2 = [
        Stage(lambda d, h: a1.at[0, pl.ds(2 * h, 2), d], r2.at[0], rs2_s.at[0], rs2_r.at[0], 1, py),
        Stage(lambda d, h: a1.at[1, pl.ds(2 * h, 2), d], r2.at[1], rs2_s.at[1], rs2_r.at[1], 0, px),
    ]
    s2[0].begin()
    sy.finish()
    a1[1, 0:2] = grad[1, 0:2, py] + r1[1, 2] + r1[1, 4]
    a1[1, 2:4] = grad[1, 2:4, py] + r1[1, 1] + r1[1, 5]
    s2[1].begin()
    s2[0].relay()
    s2[1].relay()
    for n, pos in ((0, py), (1, px)):
        s2[n].finish()
        c3[n, 0:2] = a1[n, 0:2, pos] + r2[n, 2] + r2[n, 4]
        c3[n, 2:4] = a1[n, 2:4, pos] + r2[n, 1] + r2[n, 5]
    s3 = Stage(lambda d, h: c3.at[h, d], r3, rs3_s, rs3_r, 2, pz)
    s3.begin()
    s3.relay()
    s3.finish()
    out_ref[:, 0:128] = c3[0, pz] + r3[2] + r3[4]
    out_ref[:, 128:256] = c3[1, pz] + r3[1] + r3[5]

    def q_drain(i, carry):
        q_copy(i).wait_send()
        return carry

    lax.fori_loop(tm + 1, TM, q_drain, 0)
    for i in range(1, NF):
        enc_copy(i).wait_send()
        s_copy(i).wait_send()

    @pl.when(tm < TM - 1)
    def _():
        id_copy.wait_send()

    for t in range(TILES):
        @pl.when(fq != OWNER[t])
        def _(t=t):
            n_copy(t).wait_send()

        @pl.when(fq == OWNER[t])
        def _(t=t):
            for i in range(1, NF):
                p_copy(t, i).wait_send()

    @pl.when((fq == NF - 1) & (tm < TM - 1))
    def _():
        for q in range(NF):
            halo_copy(q).wait_send()

    for stage in (sx, sy, s2[0], s2[1], s3):
        stage.drain()


def on_device(
    spectrum, decay_rate, init_state, clip_ids, encoder, gauss_noise, uniform_noise, boost_count, templates,
):
    vmem = pl.BlockSpec(memory_space=pltpu.VMEM)
    hbm = pl.BlockSpec(memory_space=pl.ANY)
    V = pltpu.VMEM
    dma = pltpu.SemaphoreType.DMA
    loss, grad = pl.pallas_call(
        kernel,
        out_shape=(
            jax.ShapeDtypeStruct((1, FRAMES), f32),
            jax.ShapeDtypeStruct((K * L // TM, BINS), f32),
        ),
        in_specs=[vmem] * 6 + [hbm] * 3,
        out_specs=(vmem, vmem),
        scratch_shapes=[
            V((BINS, K * L), bf16), V((2, K, 128), f32), V((2, 2, K, 128), f32), V((NF, K, BINS), bf16),
            V((BINS, FRAMES), f32), V((BINS, FRAMES), f32), V((TILES, BINS, 128), bf16),
            V((2, NF, BINS, 128), bf16), V((TILES + 1, K, 128), bf16), V((TILES + 1, K, 128), f32),
            V((1, 128), jnp.int32), V((1, BINS), f32), V((TM, 1, BINS), f32), V((K * L, FRAMES), bf16),
            V((BINS, FRAMES), f32), V((NF, 8, FRAMES), f32), V((BINS, FRAMES), bf16),
            V((2, 4, 4, 4, 64, 128), f32), V((2, 4, 4, 64, 128), f32), V((2, 4, 64, 128), f32),
            V((2, 6, 2, 4, 64, 128), f32), V((2, 6, 2, 64, 128), f32), V((6, 64, 128), f32),
            dma((5,)), dma((NF,)), dma((NF,)), dma((TM,)), dma((TM,)), dma, dma,
            dma((TILES,)), dma((2, NF)), dma((TILES, NF)), dma((TILES,)), dma((NF,)), dma,
            dma((NF,)), dma((NF,)),
            dma((2, 6)), dma((2, 6)), dma((2, 6)), dma((2, 6)), dma((6,)), dma((6,)),
        ],
        compiler_params=pltpu.CompilerParams(
            collective_id=0, has_side_effects=True, vmem_limit_bytes=56 * 1024 * 1024),
        name="topic_step",
    )(
        spectrum, decay_rate.reshape(1, BINS), init_state.reshape(1, BINS), clip_ids.reshape(1, FRAMES),
        encoder, boost_count.reshape(1, K), gauss_noise, uniform_noise, templates,
    )
    return loss.reshape(FRAMES), grad


def solution(mesh):
    placed = (
        P("freq", "tm"), P("freq"), P("freq"), P("tm"), P(None, "freq"), P(None, "tm"),
        P(None, None, "tm"), P(), P("freq", None),
    )
    return jax.shard_map(
        on_device, mesh=mesh, in_specs=placed, out_specs=(P("tm"), P("tm", "freq")), check_vma=False
    )
```

```python
import jax
import jax.numpy as jnp
from jax import lax
from jax.experimental import pallas as pl
from jax.experimental.pallas import tpu as pltpu
from jax.sharding import PartitionSpec as P

F = 1024
K = 256
L = 16
TIME = 49152
BINS = 256
FRAMES = 768
TILES = 6
TM = 64
NF = 4
MESH = pl.DeviceIdType.MESH
f32 = jnp.float32
bf16 = jnp.bfloat16
LOG_GAIN = 0.22314355131420976
OWNER = (0, 0, 1, 2, 2, 3)
SLOT = (0, 1, 0, 0, 1, 0)
ORDER = (2, 1, 3, 0)


def remote(src, dst, send, recv, tm, fq):
    return pltpu.make_async_remote_copy(
        src_ref=src, dst_ref=dst, send_sem=send, recv_sem=recv,
        device_id={"tm": tm, "freq": fq}, device_id_type=MESH,
    )


def kernel(
    spec_ref, decay_ref, init_ref, ids_ref, enc_ref, boost_ref, gauss_hbm, unif_hbm, tmpl_hbm,
    loss_ref, out_ref,
    tmpl, gbuf, ubuf, encf, grow, cum, normed, nbuf, pbuf, pf, idh, qbuf, st,
    recon, sbuf, rat, grad, w1, a1, c3, r1, r2, r3,
    load_sem, enc_s, enc_r, q_s, q_r, id_s, id_r, n_s, n_r, p_s, p_r, h_s, h_r, s_s, s_r,
    rs1_s, rs1_r, rs2_s, rs2_r, rs3_s, rs3_r,
):
    tm = lax.axis_index("tm")
    fq = lax.axis_index("freq")
    core = lax.rem(fq, 2)
    zlo = fq // 2
    barrier = pltpu.get_barrier_semaphore()
    nxt = lax.rem(tm + 1, TM)
    prv = lax.rem(tm + TM - 1, TM)

    px = lax.rem(tm, 4)
    py = lax.rem(tm // 4, 4)
    pz = tm // 16

    def along(axis, step):
        if axis == 0:
            return tm - px + lax.rem(px + step, 4)
        if axis == 1:
            return tm - 4 * py + 4 * lax.rem(py + step, 4)
        return tm - 16 * pz + 16 * lax.rem(pz + step, 4)

    peers = [(along(axis, step), fq) for axis in range(3) for step in range(1, 4)]
    peers += [(tm, lax.rem(fq + i, NF)) for i in range(1, NF)]
    peers += [(place, lax.rem(fq + i, NF)) for place in (nxt, prv) for i in range(NF)]
    for place, other in peers:
        pl.semaphore_signal(
            barrier, inc=1, device_id={"tm": place, "freq": other}, device_id_type=MESH)

    first = zlo * 3 + core * 2
    load_t = pltpu.make_async_copy(tmpl_hbm, tmpl, load_sem.at[0])
    load_t.start()

    def tile_loads(slot):
        cols = pl.ds(pl.multiple_of((first + slot) * 128, 128), 128)
        return (
            pltpu.make_async_copy(gauss_hbm.at[:, cols], gbuf.at[slot], load_sem.at[1 + 2 * slot]),
            pltpu.make_async_copy(unif_hbm.at[:, :, cols], ubuf.at[slot], load_sem.at[2 + 2 * slot]),
        )

    for copy in tile_loads(0):
        copy.start()

    @pl.when(core == 0)
    def _():
        for copy in tile_loads(1):
            copy.start()

    rows = lax.broadcasted_iota(jnp.int32, (BINS, BINS), 0)
    cols = lax.broadcasted_iota(jnp.int32, (BINS, BINS), 1)
    eye = rows == cols
    tri = (rows <= cols).astype(bf16)

    def column(row):
        return jnp.sum(jnp.where(eye, jnp.broadcast_to(row, (BINS, BINS)), 0.0), axis=1, keepdims=True)

    def row_of(col):
        return jnp.sum(jnp.where(eye, jnp.broadcast_to(col, (BINS, BINS)), 0.0), axis=0, keepdims=True)

    decay_row = decay_ref[...]
    lost = 1.0 - (1.0 - decay_row)
    log_row = -lost * (1.0 + lost * (1 / 2 + lost * (1 / 3 + lost * (1 / 4 + lost * (1 / 5 + lost * (1 / 6))))))
    log_col = column(log_row)
    decay_col = column(decay_row)
    ids = ids_ref[...].astype(f32)
    lift = jnp.exp(ids * LOG_GAIN)
    carry = jnp.zeros((BINS, 1), f32)
    for b in range(3):
        span = slice(b * 256, b * 256 + 256)
        steps = (cols + (b * 256 + 1)).astype(f32)
        power = steps * log_col
        grow[:, span] = jnp.exp(power)
        v = decay_col * (spec_ref[:, span].astype(f32) * lift[:, span]) * jnp.exp(-power)
        hi = v.astype(bf16)
        rest = v - hi.astype(f32)
        mid = rest.astype(bf16)
        low = (rest - mid.astype(f32)).astype(bf16)
        c = (
            jnp.dot(hi, tri, preferred_element_type=f32)
            + jnp.dot(mid, tri, preferred_element_type=f32)
            + jnp.dot(low, tri, preferred_element_type=f32)
        ) + carry
        cum[:, span] = c
        carry = c[:, 255:256]
    q_col = carry * jnp.exp(log_col * float(FRAMES))
    positions = (px, py, pz)

    def q_copy(axis, step):
        pos = positions[axis]
        return remote(
            qbuf.at[axis, pos], qbuf.at[axis, pos], q_s.at[axis, step], q_r.at[axis, step], along(axis, step), fq)

    def q_send(axis, row):
        qbuf[axis, positions[axis]] = row
        for step in range(1, 4):
            q_copy(axis, step).start()

    def q_take(axis, jump):
        pos = positions[axis]
        for step in range(1, 4):
            slot = qbuf.at[axis, lax.rem(pos + 4 - step, 4)]
            remote(slot, slot, q_s.at[axis, step], q_r.at[axis, step], tm, fq).wait_recv()
        ahead = jnp.zeros((1, BINS), f32)
        total = jnp.zeros((1, BINS), f32)
        for j in range(4):
            ahead = jnp.where(j < pos, jump * ahead + qbuf[axis, j], ahead)
            total = jump * total + qbuf[axis, j]
        return ahead, total

    q_row = row_of(q_col)
    pl.semaphore_wait(barrier, len(peers))
    q_send(0, q_row)

    def enc_copy(i):
        return remote(enc_ref, encf.at[fq], enc_s.at[i], enc_r.at[i], tm, lax.rem(fq + i, NF))

    for i in range(1, NF):
        enc_copy(i).start()
    id_copy = remote(ids_ref.at[:, pl.ds(FRAMES - 128, 128)], idh, id_s, id_r, nxt, fq)

    @pl.when(tm < TM - 1)
    def _():
        id_copy.start()

    encf[fq] = enc_ref[...]

    boost = column(boost_ref[...].astype(f32))

    def ready_noise(slot):
        for copy in tile_loads(slot):
            copy.wait()
        ubuf[slot] = jnp.log(ubuf[slot])

    ready_noise(0)

    @pl.when(core == 0)
    def _():
        ready_noise(1)

    entry = jnp.zeros((1, BINS), f32)
    gain = jnp.ones((1, BINS), f32)
    for axis in range(3):
        frames = float(FRAMES * 4 ** axis)
        ahead, total = q_take(axis, jnp.exp(log_row * frames))
        if axis < 2:
            q_send(axis + 1, total)
        entry += gain * ahead
        gain = gain * jnp.exp(log_row * (frames * positions[axis].astype(f32)))
    entry += gain * init_ref[...]
    entry_col = column(entry)
    for t in range(TILES):
        span = slice(t * 128, t * 128 + 128)
        drop = jnp.exp(ids[:, span] * (-LOG_GAIN))
        smooth = grow[:, span] * (entry_col + cum[:, span]) * drop
        normed[t] = (spec_ref[:, span].astype(f32) * lax.rsqrt(smooth + 0.1)).astype(bf16)

    def n_copy(t):
        return remote(
            normed.at[t], nbuf.at[SLOT[t], fq], n_s.at[t], n_r.at[SLOT[t], fq], tm, OWNER[t])

    for t in (3, 4, 5, 0, 1, 2):
        @pl.when(fq != OWNER[t])
        def _(t=t):
            n_copy(t).start()

        @pl.when(fq == OWNER[t])
        def _(t=t):
            nbuf[SLOT[t], fq] = normed[t]

    for i in range(1, NF):
        src = lax.rem(fq + NF - i, NF)
        remote(enc_ref, encf.at[src], enc_s.at[i], enc_r.at[i], tm, fq).wait_recv()

    def p_copy(t, i):
        return remote(pbuf.at[1 + t], pbuf.at[1 + t], p_s.at[t, i], p_r.at[t], tm, lax.rem(fq + i, NF))

    def halo_copy(q):
        return remote(pbuf.at[TILES], pbuf.at[0], h_s.at[q], h_r, nxt, q)

    def sample(slot):
        for i in range(1, NF):
            src = lax.rem(fq + i, NF)
            remote(normed.at[0], nbuf.at[slot, src], n_s.at[0], n_r.at[slot, src], tm, fq).wait_recv()
        logits = jnp.dot(encf[0], nbuf[slot, 0], preferred_element_type=f32)
        for q in range(1, NF):
            logits += jnp.dot(encf[q], nbuf[slot, q], preferred_element_type=f32)
        conc = jnp.maximum(logits, 0.0) + jnp.log(1.0 + jnp.exp(-jnp.abs(logits))) + 0.5
        offset = conc + boost - 1.0 / 3.0
        linear = 1.0 + lax.rsqrt(9.0 * offset) * gbuf[slot]
        second = jnp.where(boost >= 1.5, ubuf[slot, 1], 0.0)
        power = ubuf[slot, 0] / conc + second / (conc + 1.0)
        draw = offset * linear * linear * linear * jnp.exp(power)
        total = jnp.sum(draw, axis=0, keepdims=True)
        pbuf[1 + first + slot] = (draw / total).astype(bf16)

    sample(0)
    for t in range(TILES):
        if SLOT[t] == 0:
            @pl.when(fq == OWNER[t])
            def _(t=t):
                for i in range(1, NF):
                    p_copy(t, i).start()

    @pl.when((fq == NF - 1) & (tm < TM - 1))
    def _():
        for q in range(NF):
            halo_copy(q).start()

    @pl.when(core == 0)
    def _():
        sample(1)

    for t in range(TILES):
        if SLOT[t] == 1:
            @pl.when(fq == OWNER[t])
            def _(t=t):
                for i in range(1, NF):
                    p_copy(t, i).start()

    @pl.when(tm == 0)
    def _():
        pbuf[0] = jnp.zeros((K, 128), bf16)
        idh[...] = jnp.full((1, 128), -1, jnp.int32)

    @pl.when(tm > 0)
    def _():
        id_copy.wait_recv()
        halo_copy(0).wait_recv()

    for t in range(TILES):
        @pl.when(fq != OWNER[t])
        def _(t=t):
            p_copy(t, 1).wait_recv()

    lane = lax.broadcasted_iota(jnp.int32, (L, 128), 1)
    lag = lax.broadcasted_iota(jnp.int32, (L, 128), 0)
    head = lane < lag

    def lagged(row):
        return pltpu.roll(jnp.broadcast_to(row, (L, 128)), 0, 1, stride=1, stride_axis=0)

    id_rows = [idh[...].astype(f32)] + [ids[:, t * 128:t * 128 + 128] for t in range(TILES)]
    rolled = [lagged(r) for r in id_rows]
    keep = []
    for t in range(TILES):
        source = jnp.where(head, rolled[t], rolled[t + 1])
        keep.append(source == jnp.broadcast_to(id_rows[t + 1], (L, 128)))

    for t in range(TILES + 1):
        pf[t] = pbuf[t].astype(f32)

    def build_row(k, carry):
        prior = lagged(pf[0, pl.ds(k, 1), :])
        for t in range(TILES):
            current = lagged(pf[t + 1, pl.ds(k, 1), :])
            value = jnp.where(keep[t], jnp.where(head, prior, current), 0.0)
            st[pl.ds(pl.multiple_of(k * L, L), L), t * 128:t * 128 + 128] = value.astype(bf16)
            prior = current
        return carry

    lax.fori_loop(0, K, build_row, 0, unroll=4)

    load_t.wait()
    for b in range(3):
        span = slice(b * 256, b * 256 + 256)
        rec = jnp.dot(tmpl[...], st[:, span], preferred_element_type=f32)
        x = spec_ref[:, span].astype(f32)
        recon[:, span] = x / rec
        sbuf[fq, 0:1, span] = jnp.sum(rec, axis=0, keepdims=True)
        sbuf[fq, 1:2, span] = jnp.sum(x, axis=0, keepdims=True)
        sbuf[fq, 2:3, span] = jnp.sum(x * jnp.log(rec), axis=0, keepdims=True)

    def s_copy(i):
        return remote(sbuf.at[fq], sbuf.at[fq], s_s.at[i], s_r.at[i], tm, lax.rem(fq + i, NF))

    for i in range(1, NF):
        s_copy(i).start()
    for i in range(1, NF):
        src = lax.rem(fq + NF - i, NF)
        remote(sbuf.at[src], sbuf.at[src], s_s.at[i], s_r.at[i], tm, fq).wait_recv()
    sums = sbuf[0, 0:3, :] + sbuf[1, 0:3, :] + sbuf[2, 0:3, :] + sbuf[3, 0:3, :]
    recon_sum, spec_sum, log_sum = sums[0:1], sums[1:2], sums[2:3]
    loss_ref[...] = jnp.log(recon_sum) - log_sum / spec_sum
    scale = F * K / TIME
    plain = scale / recon_sum
    part = scale / spec_sum
    rat[...] = (plain - part * recon[...]).astype(bf16)

    def gradient(n):
        z = lax.rem(pz + ORDER[n], 4)
        g = lax.dot_general(
            st[pl.ds(pl.multiple_of(z * 1024, 1024), 1024), :], rat[...],
            (((1,), (1,)), ((), ())), preferred_element_type=f32).reshape(4, 4, 64, 256)
        grad[n, 0] = g[..., 0:128]
        grad[n, 1] = g[..., 128:256]

    class Ring:
        def __init__(self, view, buf, send, recv, axis, staged=None):
            self.view, self.buf, self.send, self.recv, self.staged = view, buf, send, recv, staged
            self.pos = positions[axis]
            to = (along(axis, 1), along(axis, 3))
            far, right, left = (lax.rem(self.pos + i, 4) for i in (2, 1, 3))
            self.parts = (
                (far, 0, to[0]), (right, 1, to[0]), (right, 0, to[0]),
                (far, 1, to[1]), (left, 0, to[1]), (left, 1, to[1]),
            )

        def copy(self, n):
            d, h, to = self.parts[n]
            src = self.view(d, h) if self.staged is None else self.staged.at[n]
            return remote(src, self.buf.at[n], self.send.at[n], self.recv.at[n], to, fq)

        def push(self, n, more=None):
            view = self.view(self.parts[n][0], self.parts[n][1])
            if self.staged is not None:
                value = view[...]
                if more is not None:
                    value = value + self.buf[more].astype(f32)
                self.staged[n] = value.astype(self.staged.dtype)
            elif more is not None:
                view[...] = view[...] + self.buf[more]
            self.copy(n).start()

        def begin(self):
            for n in (0, 3, 1, 4):
                self.push(n)

        def relay(self):
            for n in (0, 3):
                self.copy(n).wait_recv()
                self.push(n + 2, n)

        def result(self):
            for n in (1, 4, 2, 5):
                self.copy(n).wait_recv()
            return tuple(
                self.view(self.pos, h)[...] + self.buf[l].astype(f32) + self.buf[r].astype(f32)
                for h, l, r in ((0, 2, 4), (1, 1, 5)))

        def drain(self):
            for n in range(6):
                self.copy(n).wait_send()

    s1 = [[
        Ring(lambda d, h, n=n: grad.at[n, 0, pl.ds(2 * h, 2), d], r1.at[n, 0], rs1_s.at[n, 0], rs1_r.at[n, 0], 0, w1.at[n, 0]),
        Ring(lambda d, h, n=n: grad.at[n, 1, d, pl.ds(2 * h, 2)], r1.at[n, 1], rs1_s.at[n, 1], rs1_r.at[n, 1], 1, w1.at[n, 1]),
    ] for n in range(4)]
    s2 = [[
        Ring(lambda d, h, n=n, c=c: a1.at[n, c, d, pl.ds(32 * h, 32)], r2.at[n, c], rs2_s.at[n, c], rs2_r.at[n, c], 1 - c)
        for c in range(2)] for n in range(4)]
    z_to = (along(2, 1), along(2, 3))

    def z_copy(n):
        piece, half = ((0, 0), (1, 1), (1, 0), (0, 1), (2, 0), (2, 1))[n]
        return remote(c3.at[piece, half], r3.at[n], rs3_s.at[n], rs3_r.at[n], z_to[n // 3], fq)

    def begin1(n):
        for ring in s1[n]:
            ring.begin()

    def relay1(n):
        for ring in s1[n]:
            ring.relay()

    def begin2(n):
        for c in range(2):
            top, low = s1[n][c].result()
            a1[n, c, 0:2] = top
            a1[n, c, 2:4] = low
            s2[n][c].begin()

    def relay2(n):
        for ring in s2[n]:
            ring.relay()

    def done2(n):
        for c in range(2):
            top, low = s2[n][c].result()
            c3[n, c, 0:32] = top
            c3[n, c, 32:64] = low
        if n == 0:
            z_copy(0).start()
            z_copy(3).start()
        elif n < 3:
            half, plain, held = ((1, 1, 0), (0, 4, 3))[n - 1]
            z_copy(plain).start()
            z_copy(held).wait_recv()
            c3[n, 1 - half] = c3[n, 1 - half] + r3[held]
            z_copy((2, 5)[n - 1]).start()

    gradient(0)
    begin1(0)
    gradient(1)
    begin1(1)
    gradient(2)
    relay1(0)
    begin1(2)
    gradient(3)
    relay1(1)
    begin1(3)
    begin2(0)
    relay1(2)
    begin2(1)
    relay2(0)
    relay1(3)
    begin2(2)
    relay2(1)
    done2(0)
    begin2(3)
    relay2(2)
    done2(1)
    relay2(3)
    done2(2)
    done2(3)
    for n in (1, 4, 2, 5):
        z_copy(n).wait_recv()
    out_ref[:, 0:128] = c3[3, 0] + r3[2] + r3[4]
    out_ref[:, 128:256] = c3[3, 1] + r3[1] + r3[5]

    for axis in range(3):
        for step in range(1, 4):
            q_copy(axis, step).wait_send()
    for i in range(1, NF):
        enc_copy(i).wait_send()
        s_copy(i).wait_send()

    @pl.when(tm < TM - 1)
    def _():
        id_copy.wait_send()

    for t in range(TILES):
        @pl.when(fq != OWNER[t])
        def _(t=t):
            n_copy(t).wait_send()

        @pl.when(fq == OWNER[t])
        def _(t=t):
            for i in range(1, NF):
                p_copy(t, i).wait_send()

    @pl.when((fq == NF - 1) & (tm < TM - 1))
    def _():
        for q in range(NF):
            halo_copy(q).wait_send()

    for n in range(4):
        for ring in s1[n] + s2[n]:
            ring.drain()
    for n in range(6):
        z_copy(n).wait_send()


def on_device(
    spectrum, decay_rate, init_state, clip_ids, encoder, gauss_noise, uniform_noise, boost_count, templates,
):
    vmem = pl.BlockSpec(memory_space=pltpu.VMEM)
    hbm = pl.BlockSpec(memory_space=pl.ANY)
    V = pltpu.VMEM
    dma = pltpu.SemaphoreType.DMA
    loss, grad = pl.pallas_call(
        kernel,
        out_shape=(
            jax.ShapeDtypeStruct((1, FRAMES), f32),
            jax.ShapeDtypeStruct((K * L // TM, BINS), f32),
        ),
        in_specs=[vmem] * 6 + [hbm] * 3,
        out_specs=(vmem, vmem),
        scratch_shapes=[
            V((BINS, K * L), bf16), V((2, K, 128), f32), V((2, 2, K, 128), f32), V((NF, K, BINS), bf16),
            V((BINS, FRAMES), f32), V((BINS, FRAMES), f32), V((TILES, BINS, 128), bf16),
            V((2, NF, BINS, 128), bf16), V((TILES + 1, K, 128), bf16), V((TILES + 1, K, 128), f32),
            V((1, 128), jnp.int32), V((3, 4, 1, BINS), f32), V((K * L, FRAMES), bf16),
            V((BINS, FRAMES), f32), V((NF, 8, FRAMES), f32), V((BINS, FRAMES), bf16),
            V((4, 2, 4, 4, 64, 128), f32), V((4, 2, 6, 2, 64, 128), bf16), V((4, 2, 4, 64, 128), f32),
            V((4, 2, 64, 128), f32), V((4, 2, 6, 2, 64, 128), bf16), V((4, 2, 6, 32, 128), f32), V((6, 64, 128), f32),
            dma((5,)), dma((NF,)), dma((NF,)), dma((3, 4)), dma((3, 4)), dma, dma,
            dma((TILES,)), dma((2, NF)), dma((TILES, NF)), dma((TILES,)), dma((NF,)), dma,
            dma((NF,)), dma((NF,)),
            dma((4, 2, 6)), dma((4, 2, 6)), dma((4, 2, 6)), dma((4, 2, 6)), dma((6,)), dma((6,)),
        ],
        compiler_params=pltpu.CompilerParams(
            collective_id=0, has_side_effects=True, vmem_limit_bytes=56 * 1024 * 1024),
        name="topic_step",
    )(
        spectrum, decay_rate.reshape(1, BINS), init_state.reshape(1, BINS), clip_ids.reshape(1, FRAMES),
        encoder, boost_count.reshape(1, K), gauss_noise, uniform_noise, templates,
    )
    return loss.reshape(FRAMES), grad


def solution(mesh):
    placed = (
        P("freq", "tm"), P("freq"), P("freq"), P("tm"), P(None, "freq"), P(None, "tm"),
        P(None, None, "tm"), P(), P("freq", None),
    )
    return jax.shard_map(
        on_device, mesh=mesh, in_specs=placed, out_specs=(P("tm"), P("tm", "freq")), check_vma=False
    )
```

```python
import jax
import jax.numpy as jnp
from jax import lax
from jax.experimental import pallas as pl
from jax.experimental.pallas import tpu as pltpu
from jax.sharding import PartitionSpec as P

F = 1024
K = 256
L = 16
TIME = 49152
BINS = 256
FRAMES = 768
TILES = 6
TM = 64
NF = 4
MESH = pl.DeviceIdType.MESH
f32 = jnp.float32
bf16 = jnp.bfloat16
LOG_GAIN = 0.22314355131420976
OWNER = (0, 0, 1, 2, 2, 3)
SLOT = (0, 1, 0, 0, 1, 0)
ORDER = (2, 1, 3, 0)


def remote(src, dst, send, recv, tm, fq):
    return pltpu.make_async_remote_copy(
        src_ref=src, dst_ref=dst, send_sem=send, recv_sem=recv,
        device_id={"tm": tm, "freq": fq}, device_id_type=MESH,
    )


def kernel(
    spec_ref, decay_ref, init_ref, ids_ref, enc_ref, boost_ref, gauss_hbm, unif_hbm, tmpl_hbm,
    loss_ref, out_ref,
    tmpl, gbuf, ubuf, encf, grow, cum, normed, nbuf, pbuf, pf, idh, qbuf, st,
    recon, sbuf, rat, grad, w1, a1, c3, r1, r1f, r2, r3,
    load_sem, enc_s, enc_r, q_s, q_r, id_s, id_r, n_s, n_r, p_s, p_r, h_s, h_r, s_s, s_r,
    rs1_s, rs1_r, rs2_s, rs2_r, rs3_s, rs3_r,
):
    tm = lax.axis_index("tm")
    fq = lax.axis_index("freq")
    core = lax.rem(fq, 2)
    zlo = fq // 2
    barrier = pltpu.get_barrier_semaphore()
    nxt = lax.rem(tm + 1, TM)

    px = lax.rem(tm, 4)
    py = lax.rem(tm // 4, 4)
    pz = tm // 16

    def along(axis, step):
        if axis == 0:
            return tm - px + lax.rem(px + step, 4)
        if axis == 1:
            return tm - 4 * py + 4 * lax.rem(py + step, 4)
        return tm - 16 * pz + 16 * lax.rem(pz + step, 4)

    peers = [(along(axis, step), fq) for axis in range(3) for step in range(1, 4)]
    peers += [(tm, lax.rem(fq + i, NF)) for i in range(1, NF)]
    for place, other in peers:
        pl.semaphore_signal(
            barrier, inc=1, device_id={"tm": place, "freq": other}, device_id_type=MESH)

    first = zlo * 3 + core * 2
    load_t = pltpu.make_async_copy(tmpl_hbm, tmpl, load_sem.at[0])
    load_t.start()

    def tile_loads(slot):
        cols = pl.ds(pl.multiple_of((first + slot) * 128, 128), 128)
        return (
            pltpu.make_async_copy(gauss_hbm.at[:, cols], gbuf.at[slot], load_sem.at[1 + 2 * slot]),
            pltpu.make_async_copy(unif_hbm.at[:, :, cols], ubuf.at[slot], load_sem.at[2 + 2 * slot]),
        )

    for copy in tile_loads(0):
        copy.start()

    @pl.when(core == 0)
    def _():
        for copy in tile_loads(1):
            copy.start()

    rows = lax.broadcasted_iota(jnp.int32, (BINS, BINS), 0)
    cols = lax.broadcasted_iota(jnp.int32, (BINS, BINS), 1)
    eye = rows == cols
    tri = (rows <= cols).astype(bf16)

    def column(row):
        return jnp.sum(jnp.where(eye, jnp.broadcast_to(row, (BINS, BINS)), 0.0), axis=1, keepdims=True)

    def row_of(col):
        return jnp.sum(jnp.where(eye, jnp.broadcast_to(col, (BINS, BINS)), 0.0), axis=0, keepdims=True)

    decay_row = decay_ref[...]
    lost = 1.0 - (1.0 - decay_row)
    log_row = -lost * (1.0 + lost * (1 / 2 + lost * (1 / 3 + lost * (1 / 4 + lost * (1 / 5 + lost * (1 / 6))))))
    log_col = column(log_row)
    decay_col = column(decay_row)
    ids = ids_ref[...].astype(f32)
    lift = jnp.exp(ids * LOG_GAIN)
    carry = jnp.zeros((BINS, 1), f32)
    for b in range(3):
        span = slice(b * 256, b * 256 + 256)
        steps = (cols + (b * 256 + 1)).astype(f32)
        power = steps * log_col
        grow[:, span] = jnp.exp(power)
        v = decay_col * (spec_ref[:, span].astype(f32) * lift[:, span]) * jnp.exp(-power)
        hi = v.astype(bf16)
        rest = v - hi.astype(f32)
        mid = rest.astype(bf16)
        low = (rest - mid.astype(f32)).astype(bf16)
        c = (
            jnp.dot(hi, tri, preferred_element_type=f32)
            + jnp.dot(mid, tri, preferred_element_type=f32)
            + jnp.dot(low, tri, preferred_element_type=f32)
        ) + carry
        cum[:, span] = c
        carry = c[:, 255:256]
    q_col = carry * jnp.exp(log_col * float(FRAMES))
    positions = (px, py, pz)

    def q_copy(axis, step):
        pos = positions[axis]
        return remote(
            qbuf.at[axis, pos], qbuf.at[axis, pos], q_s.at[axis, step], q_r.at[axis, step], along(axis, step), fq)

    def q_send(axis, row):
        qbuf[axis, positions[axis]] = row
        for step in range(1, 4):
            q_copy(axis, step).start()

    def q_take(axis, jump):
        pos = positions[axis]
        for step in range(1, 4):
            slot = qbuf.at[axis, lax.rem(pos + 4 - step, 4)]
            remote(slot, slot, q_s.at[axis, step], q_r.at[axis, step], tm, fq).wait_recv()
        ahead = jnp.zeros((1, BINS), f32)
        total = jnp.zeros((1, BINS), f32)
        for j in range(4):
            ahead = jnp.where(j < pos, jump * ahead + qbuf[axis, j], ahead)
            total = jump * total + qbuf[axis, j]
        return ahead, total

    q_row = row_of(q_col)
    pl.semaphore_wait(barrier, len(peers))
    q_send(0, q_row)

    def enc_copy(i):
        return remote(enc_ref, encf.at[fq], enc_s.at[i], enc_r.at[i], tm, lax.rem(fq + i, NF))

    for i in range(1, NF):
        enc_copy(i).start()
    encf[fq] = enc_ref[...]

    boost = column(boost_ref[...].astype(f32))

    def ready_noise(slot):
        for copy in tile_loads(slot):
            copy.wait()
        ubuf[slot] = jnp.log(ubuf[slot])

    ready_noise(0)

    @pl.when(core == 0)
    def _():
        ready_noise(1)

    entry = jnp.zeros((1, BINS), f32)
    gain = jnp.ones((1, BINS), f32)
    for axis in range(3):
        frames = float(FRAMES * 4 ** axis)
        ahead, total = q_take(axis, jnp.exp(log_row * frames))
        if axis < 2:
            q_send(axis + 1, total)
        entry += gain * ahead
        gain = gain * jnp.exp(log_row * (frames * positions[axis].astype(f32)))
    entry += gain * init_ref[...]
    id_copy = remote(ids_ref.at[:, pl.ds(FRAMES - 128, 128)], idh, id_s, id_r, nxt, fq)

    @pl.when(tm < TM - 1)
    def _():
        id_copy.start()

    entry_col = column(entry)
    for t in range(TILES):
        span = slice(t * 128, t * 128 + 128)
        drop = jnp.exp(ids[:, span] * (-LOG_GAIN))
        smooth = grow[:, span] * (entry_col + cum[:, span]) * drop
        normed[t] = (spec_ref[:, span].astype(f32) * lax.rsqrt(smooth + 0.1)).astype(bf16)

    def n_copy(t):
        return remote(
            normed.at[t], nbuf.at[SLOT[t], fq], n_s.at[t], n_r.at[SLOT[t], fq], tm, OWNER[t])

    for t in (3, 4, 5, 0, 1, 2):
        @pl.when(fq != OWNER[t])
        def _(t=t):
            n_copy(t).start()

        @pl.when(fq == OWNER[t])
        def _(t=t):
            nbuf[SLOT[t], fq] = normed[t]

    for i in range(1, NF):
        src = lax.rem(fq + NF - i, NF)
        remote(enc_ref, encf.at[src], enc_s.at[i], enc_r.at[i], tm, fq).wait_recv()

    def p_copy(t, i):
        return remote(pbuf.at[1 + t], pbuf.at[1 + t], p_s.at[t, i], p_r.at[t], tm, lax.rem(fq + i, NF))

    def halo_copy(q):
        return remote(pbuf.at[TILES], pbuf.at[0], h_s.at[q], h_r, nxt, q)

    def sample(slot):
        for i in range(1, NF):
            src = lax.rem(fq + i, NF)
            remote(normed.at[0], nbuf.at[slot, src], n_s.at[0], n_r.at[slot, src], tm, fq).wait_recv()
        logits = jnp.dot(encf[0], nbuf[slot, 0], preferred_element_type=f32)
        for q in range(1, NF):
            logits += jnp.dot(encf[q], nbuf[slot, q], preferred_element_type=f32)
        conc = jnp.maximum(logits, 0.0) + jnp.log(1.0 + jnp.exp(-jnp.abs(logits))) + 0.5
        offset = conc + boost - 1.0 / 3.0
        linear = 1.0 + lax.rsqrt(9.0 * offset) * gbuf[slot]
        second = jnp.where(boost >= 1.5, ubuf[slot, 1], 0.0)
        power = ubuf[slot, 0] / conc + second / (conc + 1.0)
        draw = offset * linear * linear * linear * jnp.exp(power)
        total = jnp.sum(draw, axis=0, keepdims=True)
        pbuf[1 + first + slot] = (draw / total).astype(bf16)

    sample(0)
    for t in range(TILES):
        if SLOT[t] == 0:
            @pl.when(fq == OWNER[t])
            def _(t=t):
                for i in range(1, NF):
                    p_copy(t, i).start()

    @pl.when((fq == NF - 1) & (tm < TM - 1))
    def _():
        for q in range(NF):
            halo_copy(q).start()

    @pl.when(core == 0)
    def _():
        sample(1)

    for t in range(TILES):
        if SLOT[t] == 1:
            @pl.when(fq == OWNER[t])
            def _(t=t):
                for i in range(1, NF):
                    p_copy(t, i).start()

    @pl.when(tm == 0)
    def _():
        pbuf[0] = jnp.zeros((K, 128), bf16)
        idh[...] = jnp.full((1, 128), -1, jnp.int32)

    @pl.when(tm > 0)
    def _():
        id_copy.wait_recv()
        halo_copy(0).wait_recv()

    for t in range(TILES):
        @pl.when(fq != OWNER[t])
        def _(t=t):
            p_copy(t, 1).wait_recv()

    lane = lax.broadcasted_iota(jnp.int32, (L, 128), 1)
    lag = lax.broadcasted_iota(jnp.int32, (L, 128), 0)
    head = lane < lag

    def lagged(row):
        return pltpu.roll(jnp.broadcast_to(row, (L, 128)), 0, 1, stride=1, stride_axis=0)

    id_rows = [idh[...].astype(f32)] + [ids[:, t * 128:t * 128 + 128] for t in range(TILES)]
    rolled = [lagged(r) for r in id_rows]
    keep = []
    for t in range(TILES):
        source = jnp.where(head, rolled[t], rolled[t + 1])
        keep.append(source == jnp.broadcast_to(id_rows[t + 1], (L, 128)))

    for t in range(TILES + 1):
        pf[t] = pbuf[t].astype(f32)

    def build_row(k, carry):
        prior = lagged(pf[0, pl.ds(k, 1), :])
        for t in range(TILES):
            current = lagged(pf[t + 1, pl.ds(k, 1), :])
            value = jnp.where(keep[t], jnp.where(head, prior, current), 0.0)
            st[pl.ds(pl.multiple_of(k * L, L), L), t * 128:t * 128 + 128] = value.astype(bf16)
            prior = current
        return carry

    lax.fori_loop(0, K, build_row, 0, unroll=4)

    load_t.wait()
    for b in range(3):
        span = slice(b * 256, b * 256 + 256)
        rec = jnp.dot(tmpl[...], st[:, span], preferred_element_type=f32)
        x = spec_ref[:, span].astype(f32)
        recon[:, span] = x / rec
        sbuf[fq, 0:1, span] = jnp.sum(rec, axis=0, keepdims=True)
        sbuf[fq, 1:2, span] = jnp.sum(x, axis=0, keepdims=True)
        sbuf[fq, 2:3, span] = jnp.sum(x * jnp.log(rec), axis=0, keepdims=True)

    def s_copy(i):
        return remote(sbuf.at[fq], sbuf.at[fq], s_s.at[i], s_r.at[i], tm, lax.rem(fq + i, NF))

    for i in range(1, NF):
        s_copy(i).start()
    for i in range(1, NF):
        src = lax.rem(fq + NF - i, NF)
        remote(sbuf.at[src], sbuf.at[src], s_s.at[i], s_r.at[i], tm, fq).wait_recv()
    sums = sbuf[0, 0:3, :] + sbuf[1, 0:3, :] + sbuf[2, 0:3, :] + sbuf[3, 0:3, :]
    recon_sum, spec_sum, log_sum = sums[0:1], sums[1:2], sums[2:3]
    loss_ref[...] = jnp.log(recon_sum) - log_sum / spec_sum
    scale = F * K / TIME
    plain = scale / recon_sum
    part = scale / spec_sum
    rat[...] = (plain - part * recon[...]).astype(bf16)

    def gradient(n):
        z = lax.rem(pz + ORDER[n], 4)
        g = lax.dot_general(
            st[pl.ds(pl.multiple_of(z * 1024, 1024), 1024), :], rat[...],
            (((1,), (1,)), ((), ())), preferred_element_type=f32).reshape(4, 4, 64, 256)
        grad[n, 0] = g[..., 0:128]
        grad[n, 1] = g[..., 128:256]

    class Ring:
        def __init__(self, view, buf, send, recv, axis, staged=None):
            self.view, self.buf, self.send, self.recv, self.staged = view, buf, send, recv, staged
            self.pos = positions[axis]
            to = (along(axis, 1), along(axis, 3))
            far, right, left = (lax.rem(self.pos + i, 4) for i in (2, 1, 3))
            self.parts = (
                (far, 0, to[0]), (right, 1, to[0]), (right, 0, to[0]),
                (far, 1, to[1]), (left, 0, to[1]), (left, 1, to[1]),
            )

        def copy(self, n):
            d, h, to = self.parts[n]
            src = self.view(d, h) if self.staged is None or n % 3 == 2 else self.staged.at[n]
            return remote(src, self.buf(n), self.send.at[n], self.recv.at[n], to, fq)

        def push(self, n, more=None):
            view = self.view(self.parts[n][0], self.parts[n][1])
            if more is not None:
                view[...] = view[...] + self.buf(more)[...].astype(f32)
            elif self.staged is not None:
                self.staged[n] = view[...].astype(self.staged.dtype)
            self.copy(n).start()

        def begin(self):
            for n in (0, 3, 1, 4):
                self.push(n)

        def relay(self):
            for n in (0, 3):
                self.copy(n).wait_recv()
                self.push(n + 2, n)

        def result(self):
            for n in (1, 4, 2, 5):
                self.copy(n).wait_recv()
            return tuple(
                self.view(self.pos, h)[...] + self.buf(l)[...].astype(f32) + self.buf(r)[...].astype(f32)
                for h, l, r in ((0, 2, 4), (1, 1, 5)))

        def drain(self):
            for n in range(6):
                self.copy(n).wait_send()

    def landing(n, c):
        return lambda i: r1f.at[n, c, i // 3] if i % 3 == 2 else r1.at[n, c, i]

    s1 = [[
        Ring(lambda d, h, n=n: grad.at[n, 0, pl.ds(2 * h, 2), d], landing(n, 0), rs1_s.at[n, 0], rs1_r.at[n, 0], 0, w1.at[n, 0]),
        Ring(lambda d, h, n=n: grad.at[n, 1, d, pl.ds(2 * h, 2)], landing(n, 1), rs1_s.at[n, 1], rs1_r.at[n, 1], 1, w1.at[n, 1]),
    ] for n in range(4)]
    s2 = [[
        Ring(lambda d, h, n=n, c=c: a1.at[n, c, d, pl.ds(32 * h, 32)], lambda i, n=n, c=c: r2.at[n, c, i], rs2_s.at[n, c], rs2_r.at[n, c], 1 - c)
        for c in range(2)] for n in range(4)]
    z_to = (along(2, 1), along(2, 3))

    def z_copy(n):
        piece, half = ((0, 0), (1, 1), (1, 0), (0, 1), (2, 0), (2, 1))[n]
        return remote(c3.at[piece, half], r3.at[n], rs3_s.at[n], rs3_r.at[n], z_to[n // 3], fq)

    def begin1(n):
        for ring in s1[n]:
            ring.begin()

    def relay1(n):
        for ring in s1[n]:
            ring.relay()

    def begin2(n):
        for c in range(2):
            top, low = s1[n][c].result()
            a1[n, c, 0:2] = top
            a1[n, c, 2:4] = low
            s2[n][c].begin()

    def relay2(n):
        for ring in s2[n]:
            ring.relay()

    def done2(n):
        for c in range(2):
            top, low = s2[n][c].result()
            c3[n, c, 0:32] = top
            c3[n, c, 32:64] = low
        if n == 0:
            z_copy(0).start()
            z_copy(3).start()
        elif n < 3:
            half, plain, held = ((1, 1, 0), (0, 4, 3))[n - 1]
            z_copy(plain).start()
            z_copy(held).wait_recv()
            c3[n, 1 - half] = c3[n, 1 - half] + r3[held]
            z_copy((2, 5)[n - 1]).start()

    gradient(0)
    begin1(0)
    gradient(1)
    begin1(1)
    gradient(2)
    relay1(0)
    begin1(2)
    gradient(3)
    relay1(1)
    begin1(3)
    begin2(0)
    relay1(2)
    begin2(1)
    relay2(0)
    relay1(3)
    begin2(2)
    relay2(1)
    done2(0)
    begin2(3)
    relay2(2)
    done2(1)
    relay2(3)
    done2(2)
    done2(3)
    for n in (1, 4, 2, 5):
        z_copy(n).wait_recv()
    out_ref[:, 0:128] = c3[3, 0] + r3[2] + r3[4]
    out_ref[:, 128:256] = c3[3, 1] + r3[1] + r3[5]

    for axis in range(3):
        for step in range(1, 4):
            q_copy(axis, step).wait_send()
    for i in range(1, NF):
        enc_copy(i).wait_send()
        s_copy(i).wait_send()

    @pl.when(tm < TM - 1)
    def _():
        id_copy.wait_send()

    for t in range(TILES):
        @pl.when(fq != OWNER[t])
        def _(t=t):
            n_copy(t).wait_send()

        @pl.when(fq == OWNER[t])
        def _(t=t):
            for i in range(1, NF):
                p_copy(t, i).wait_send()

    @pl.when((fq == NF - 1) & (tm < TM - 1))
    def _():
        for q in range(NF):
            halo_copy(q).wait_send()

    for n in range(4):
        for ring in s1[n] + s2[n]:
            ring.drain()
    for n in range(6):
        z_copy(n).wait_send()


def on_device(
    spectrum, decay_rate, init_state, clip_ids, encoder, gauss_noise, uniform_noise, boost_count, templates,
):
    vmem = pl.BlockSpec(memory_space=pltpu.VMEM)
    hbm = pl.BlockSpec(memory_space=pl.ANY)
    V = pltpu.VMEM
    dma = pltpu.SemaphoreType.DMA
    loss, grad = pl.pallas_call(
        kernel,
        out_shape=(
            jax.ShapeDtypeStruct((1, FRAMES), f32),
            jax.ShapeDtypeStruct((K * L // TM, BINS), f32),
        ),
        in_specs=[vmem] * 6 + [hbm] * 3,
        out_specs=(vmem, vmem),
        scratch_shapes=[
            V((BINS, K * L), bf16), V((2, K, 128), f32), V((2, 2, K, 128), f32), V((NF, K, BINS), bf16),
            V((BINS, FRAMES), f32), V((BINS, FRAMES), f32), V((TILES, BINS, 128), bf16),
            V((2, NF, BINS, 128), bf16), V((TILES + 1, K, 128), bf16), V((TILES + 1, K, 128), f32),
            V((1, 128), jnp.int32), V((3, 4, 1, BINS), f32), V((K * L, FRAMES), bf16),
            V((BINS, FRAMES), f32), V((NF, 8, FRAMES), f32), V((BINS, FRAMES), bf16),
            V((4, 2, 4, 4, 64, 128), f32), V((4, 2, 6, 2, 64, 128), bf16), V((4, 2, 4, 64, 128), f32),
            V((4, 2, 64, 128), f32), V((4, 2, 6, 2, 64, 128), bf16), V((4, 2, 2, 2, 64, 128), f32), V((4, 2, 6, 32, 128), f32), V((6, 64, 128), f32),
            dma((5,)), dma((NF,)), dma((NF,)), dma((3, 4)), dma((3, 4)), dma, dma,
            dma((TILES,)), dma((2, NF)), dma((TILES, NF)), dma((TILES,)), dma((NF,)), dma,
            dma((NF,)), dma((NF,)),
            dma((4, 2, 6)), dma((4, 2, 6)), dma((4, 2, 6)), dma((4, 2, 6)), dma((6,)), dma((6,)),
        ],
        compiler_params=pltpu.CompilerParams(
            collective_id=0, has_side_effects=True, vmem_limit_bytes=56 * 1024 * 1024),
        name="topic_step",
    )(
        spectrum, decay_rate.reshape(1, BINS), init_state.reshape(1, BINS), clip_ids.reshape(1, FRAMES),
        encoder, boost_count.reshape(1, K), gauss_noise, uniform_noise, templates,
    )
    return loss.reshape(FRAMES), grad


def solution(mesh):
    placed = (
        P("freq", "tm"), P("freq"), P("freq"), P("tm"), P(None, "freq"), P(None, "tm"),
        P(None, None, "tm"), P(), P("freq", None),
    )
    return jax.shard_map(
        on_device, mesh=mesh, in_specs=placed, out_specs=(P("tm"), P("tm", "freq")), check_vma=False
    )
```

```python
import jax
import jax.numpy as jnp
from jax import lax
from jax.experimental import pallas as pl
from jax.experimental.pallas import tpu as pltpu
from jax.sharding import PartitionSpec as P

F = 1024
K = 256
L = 16
TIME = 49152
BINS = 256
FRAMES = 768
TILES = 6
TM = 64
NF = 4
MESH = pl.DeviceIdType.MESH
f32 = jnp.float32
bf16 = jnp.bfloat16
LOG_GAIN = 0.22314355131420976
OWNER = (0, 0, 1, 2, 2, 3)
SLOT = (0, 1, 0, 0, 1, 0)
ORDER = (2, 1, 3, 0)


def remote(src, dst, send, recv, tm, fq):
    return pltpu.make_async_remote_copy(
        src_ref=src, dst_ref=dst, send_sem=send, recv_sem=recv,
        device_id={"tm": tm, "freq": fq}, device_id_type=MESH,
    )


def take(ref, sem):
    remote(ref, ref, sem, sem, 0, 0).wait_recv()


def sent(ref, sem):
    remote(ref, ref, sem, sem, 0, 0).wait_send()


def kernel(
    decay_ref, init_ref, ids_ref, boost_ref, spec_hbm, enc_hbm, gauss_hbm, unif_hbm, tmpl_hbm,
    loss_ref, out_ref,
    spec_ref, tmpl, gbuf, ubuf, encf, grow, cum, normed, nbuf, pbuf, pf, idh, qbuf, st,
    recon, sbuf, rat, grad, w1, a1, c3, r1, r1f, r2, r3,
    load_sem, enc_s, enc_r, q_s, q_r, id_s, id_r, n_s, n_r, p_s, p_r, h_s, h_r, s_s, s_r,
    rs1_s, rs1_r, rs2_s, rs2_r, rs3_s, rs3_r,
):
    tm = lax.axis_index("tm")
    fq = lax.axis_index("freq")
    core = lax.rem(fq, 2)
    zlo = fq // 2
    barrier = pltpu.get_barrier_semaphore()
    nxt = lax.rem(tm + 1, TM)

    px = lax.rem(tm, 4)
    py = lax.rem(tm // 4, 4)
    pz = tm // 16

    def along(axis, step):
        if axis == 0:
            return tm - px + lax.rem(px + step, 4)
        if axis == 1:
            return tm - 4 * py + 4 * lax.rem(py + step, 4)
        return tm - 16 * pz + 16 * lax.rem(pz + step, 4)

    peers = [(along(axis, step), fq) for axis in range(3) for step in range(1, 4)]
    peers += [(tm, lax.rem(fq + i, NF)) for i in range(1, NF)]
    for place, other in peers:
        pl.semaphore_signal(
            barrier, inc=1, device_id={"tm": place, "freq": other}, device_id_type=MESH)

    load_x = pltpu.make_async_copy(spec_hbm, spec_ref, load_sem.at[5])
    load_x.start()
    load_e = pltpu.make_async_copy(enc_hbm, encf.at[fq], load_sem.at[6])
    load_e.start()
    first = zlo * 3 + core * 2
    load_t = pltpu.make_async_copy(tmpl_hbm, tmpl, load_sem.at[0])

    def tile_loads(slot):
        cols = pl.ds(pl.multiple_of((first + slot) * 128, 128), 128)
        return (
            pltpu.make_async_copy(gauss_hbm.at[:, cols], gbuf.at[slot], load_sem.at[1 + 2 * slot]),
            pltpu.make_async_copy(unif_hbm.at[:, :, cols], ubuf.at[slot], load_sem.at[2 + 2 * slot]),
        )

    for copy in tile_loads(0):
        copy.start()

    @pl.when(core == 0)
    def _():
        for copy in tile_loads(1):
            copy.start()

    load_t.start()

    rows = lax.broadcasted_iota(jnp.int32, (BINS, BINS), 0)
    cols = lax.broadcasted_iota(jnp.int32, (BINS, BINS), 1)
    eye = rows == cols
    tri = (rows <= cols).astype(bf16)

    def column(row):
        return jnp.sum(jnp.where(eye, jnp.broadcast_to(row, (BINS, BINS)), 0.0), axis=1, keepdims=True)

    def row_of(col):
        return jnp.sum(jnp.where(eye, jnp.broadcast_to(col, (BINS, BINS)), 0.0), axis=0, keepdims=True)

    decay_row = decay_ref[...]
    lost = 1.0 - (1.0 - decay_row)
    log_row = -lost * (1.0 + lost * (1 / 2 + lost * (1 / 3 + lost * (1 / 4 + lost * (1 / 5 + lost * (1 / 6))))))
    log_col = column(log_row)
    decay_col = column(decay_row)
    ids = ids_ref[...].astype(f32)
    lift = jnp.exp(ids * LOG_GAIN)
    load_x.wait()
    carry = jnp.zeros((BINS, 1), f32)
    for b in range(3):
        span = slice(b * 256, b * 256 + 256)
        steps = (cols + (b * 256 + 1)).astype(f32)
        power = steps * log_col
        grow[:, span] = jnp.exp(power)
        v = decay_col * (spec_ref[:, span].astype(f32) * lift[:, span]) * jnp.exp(-power)
        hi = v.astype(bf16)
        rest = v - hi.astype(f32)
        mid = rest.astype(bf16)
        low = (rest - mid.astype(f32)).astype(bf16)
        c = (
            jnp.dot(hi, tri, preferred_element_type=f32)
            + jnp.dot(mid, tri, preferred_element_type=f32)
            + jnp.dot(low, tri, preferred_element_type=f32)
        ) + carry
        cum[:, span] = c
        carry = c[:, 255:256]
    q_col = carry * jnp.exp(log_col * float(FRAMES))
    positions = (px, py, pz)

    def q_copy(axis, step):
        pos = positions[axis]
        return remote(
            qbuf.at[axis, pos], qbuf.at[axis, pos], q_s, q_r.at[axis], along(axis, step), fq)

    def q_send(axis, row):
        qbuf[axis, positions[axis]] = row
        for step in range(1, 4):
            q_copy(axis, step).start()

    def q_take(axis, jump):
        pos = positions[axis]
        take(qbuf.at[axis, pl.ds(0, 3)], q_r.at[axis])
        ahead = jnp.zeros((1, BINS), f32)
        total = jnp.zeros((1, BINS), f32)
        for j in range(4):
            ahead = jnp.where(j < pos, jump * ahead + qbuf[axis, j], ahead)
            total = jump * total + qbuf[axis, j]
        return ahead, total

    q_row = row_of(q_col)
    pl.semaphore_wait(barrier, len(peers))
    q_send(0, q_row)

    def enc_copy(i):
        return remote(encf.at[fq], encf.at[fq], enc_s, enc_r, tm, lax.rem(fq + i, NF))

    load_e.wait()
    for i in range(1, NF):
        enc_copy(i).start()
    boost = column(boost_ref[...].astype(f32))

    def ready_noise(slot):
        for copy in tile_loads(slot):
            copy.wait()
        ubuf[slot] = jnp.log(ubuf[slot])

    ready_noise(0)

    @pl.when(core == 0)
    def _():
        ready_noise(1)

    entry = jnp.zeros((1, BINS), f32)
    gain = jnp.ones((1, BINS), f32)
    for axis in range(3):
        frames = float(FRAMES * 4 ** axis)
        ahead, total = q_take(axis, jnp.exp(log_row * frames))
        if axis < 2:
            q_send(axis + 1, total)
        entry += gain * ahead
        gain = gain * jnp.exp(log_row * (frames * positions[axis].astype(f32)))
    entry += gain * init_ref[...]
    id_copy = remote(ids_ref.at[:, pl.ds(FRAMES - 128, 128)], idh, id_s, id_r, nxt, fq)

    @pl.when(tm < TM - 1)
    def _():
        id_copy.start()

    entry_col = column(entry)
    for t in range(TILES):
        span = slice(t * 128, t * 128 + 128)
        drop = jnp.exp(ids[:, span] * (-LOG_GAIN))
        smooth = grow[:, span] * (entry_col + cum[:, span]) * drop
        normed[t] = (spec_ref[:, span].astype(f32) * lax.rsqrt(smooth + 0.1)).astype(bf16)

    def n_copy(t):
        return remote(
            normed.at[t], nbuf.at[SLOT[t], fq], n_s, n_r.at[SLOT[t]], tm, OWNER[t])

    for t in (3, 4, 5, 0, 1, 2):
        @pl.when(fq != OWNER[t])
        def _(t=t):
            n_copy(t).start()

        @pl.when(fq == OWNER[t])
        def _(t=t):
            nbuf[SLOT[t], fq] = normed[t]

    take(encf.at[pl.ds(0, 3)], enc_r)

    def p_copy(t, i):
        return remote(pbuf.at[1 + t], pbuf.at[1 + t], p_s, p_r, tm, lax.rem(fq + i, NF))

    def halo_copy(q):
        return remote(pbuf.at[TILES], pbuf.at[0], h_s, h_r, nxt, q)

    def sample(slot):
        take(nbuf.at[slot, pl.ds(0, 3)], n_r.at[slot])
        logits = jnp.dot(encf[0], nbuf[slot, 0], preferred_element_type=f32)
        for q in range(1, NF):
            logits += jnp.dot(encf[q], nbuf[slot, q], preferred_element_type=f32)
        conc = jnp.maximum(logits, 0.0) + jnp.log(1.0 + jnp.exp(-jnp.abs(logits))) + 0.5
        offset = conc + boost - 1.0 / 3.0
        linear = 1.0 + lax.rsqrt(9.0 * offset) * gbuf[slot]
        second = jnp.where(boost >= 1.5, ubuf[slot, 1], 0.0)
        power = ubuf[slot, 0] / conc + second / (conc + 1.0)
        draw = offset * linear * linear * linear * jnp.exp(power)
        total = jnp.sum(draw, axis=0, keepdims=True)
        pbuf[1 + first + slot] = (draw / total).astype(bf16)

    sample(0)
    for t in range(TILES):
        if SLOT[t] == 0:
            @pl.when(fq == OWNER[t])
            def _(t=t):
                for i in range(1, NF):
                    p_copy(t, i).start()

    @pl.when((fq == NF - 1) & (tm < TM - 1))
    def _():
        for q in range(NF):
            halo_copy(q).start()

    @pl.when(core == 0)
    def _():
        sample(1)

    for t in range(TILES):
        if SLOT[t] == 1:
            @pl.when(fq == OWNER[t])
            def _(t=t):
                for i in range(1, NF):
                    p_copy(t, i).start()

    @pl.when(tm == 0)
    def _():
        pbuf[0] = jnp.zeros((K, 128), bf16)
        idh[...] = jnp.full((1, 128), -1, jnp.int32)

    @pl.when(tm > 0)
    def _():
        id_copy.wait_recv()
        halo_copy(0).wait_recv()

    @pl.when(core == 0)
    def _():
        take(pbuf.at[pl.ds(0, 4)], p_r)

    @pl.when(core == 1)
    def _():
        take(pbuf.at[pl.ds(0, 5)], p_r)

    lane = lax.broadcasted_iota(jnp.int32, (L, 128), 1)
    lag = lax.broadcasted_iota(jnp.int32, (L, 128), 0)
    head = lane < lag

    def lagged(row):
        return pltpu.roll(jnp.broadcast_to(row, (L, 128)), 0, 1, stride=1, stride_axis=0)

    id_rows = [idh[...].astype(f32)] + [ids[:, t * 128:t * 128 + 128] for t in range(TILES)]
    rolled = [lagged(r) for r in id_rows]
    keep = []
    for t in range(TILES):
        source = jnp.where(head, rolled[t], rolled[t + 1])
        keep.append(source == jnp.broadcast_to(id_rows[t + 1], (L, 128)))

    for t in range(TILES + 1):
        pf[t] = pbuf[t].astype(f32)

    def build_row(k, carry):
        prior = lagged(pf[0, pl.ds(k, 1), :])
        for t in range(TILES):
            current = lagged(pf[t + 1, pl.ds(k, 1), :])
            value = jnp.where(keep[t], jnp.where(head, prior, current), 0.0)
            st[pl.ds(pl.multiple_of(k * L, L), L), t * 128:t * 128 + 128] = value.astype(bf16)
            prior = current
        return carry

    lax.fori_loop(0, K, build_row, 0, unroll=16)

    load_t.wait()
    for b in range(3):
        span = slice(b * 256, b * 256 + 256)
        rec = jnp.dot(tmpl[...], st[:, span], preferred_element_type=f32)
        x = spec_ref[:, span].astype(f32)
        recon[:, span] = x / rec
        sbuf[fq, 0:1, span] = jnp.sum(rec, axis=0, keepdims=True)
        sbuf[fq, 1:2, span] = jnp.sum(x, axis=0, keepdims=True)
        sbuf[fq, 2:3, span] = jnp.sum(x * jnp.log(rec), axis=0, keepdims=True)

    def s_copy(i):
        return remote(sbuf.at[fq], sbuf.at[fq], s_s, s_r, tm, lax.rem(fq + i, NF))

    for i in range(1, NF):
        s_copy(i).start()
    take(sbuf.at[pl.ds(0, 3)], s_r)
    sums = sbuf[0, 0:3, :] + sbuf[1, 0:3, :] + sbuf[2, 0:3, :] + sbuf[3, 0:3, :]
    recon_sum, spec_sum, log_sum = sums[0:1], sums[1:2], sums[2:3]
    loss_ref[...] = jnp.log(recon_sum) - log_sum / spec_sum
    scale = F * K / TIME
    plain = scale / recon_sum
    part = scale / spec_sum
    rat[...] = (plain - part * recon[...]).astype(bf16)

    def gradient(n):
        z = lax.rem(pz + ORDER[n], 4)
        g = lax.dot_general(
            st[pl.ds(pl.multiple_of(z * 1024, 1024), 1024), :], rat[...],
            (((1,), (1,)), ((), ())), preferred_element_type=f32).reshape(4, 4, 64, 256)
        grad[n, 0] = g[..., 0:128]
        grad[n, 1] = g[..., 128:256]

    class Ring:
        def __init__(self, view, buf, send, recv, axis, staged=None):
            self.view, self.buf, self.send, self.recv, self.staged = view, buf, send, recv, staged
            self.pos = positions[axis]
            to = (along(axis, 1), along(axis, 3))
            far, right, left = (lax.rem(self.pos + i, 4) for i in (2, 1, 3))
            self.parts = (
                (far, 0, to[0]), (right, 1, to[0]), (right, 0, to[0]),
                (far, 1, to[1]), (left, 0, to[1]), (left, 1, to[1]),
            )

        def copy(self, n):
            d, h, to = self.parts[n]
            src = self.view(d, h) if self.staged is None or n % 3 == 2 else self.staged.at[n]
            return remote(src, self.buf(n), self.send, self.recv.at[0 if n % 3 == 0 else 1], to, fq)

        def push(self, n, more=None):
            view = self.view(self.parts[n][0], self.parts[n][1])
            if more is not None:
                view[...] = view[...] + self.buf(more)[...].astype(f32)
            elif self.staged is not None:
                self.staged[n] = view[...].astype(self.staged.dtype)
            self.copy(n).start()

        def begin(self):
            for n in (0, 3, 1, 4):
                self.push(n)

        def relay(self):
            for n in (0, 3):
                self.push(n + 2, n)

        def result(self):
            return tuple(
                self.view(self.pos, h)[...] + self.buf(l)[...].astype(f32) + self.buf(r)[...].astype(f32)
                for h, l, r in ((0, 2, 4), (1, 1, 5)))

    def landing(n, c):
        return lambda i: r1f.at[n, c, i // 3] if i % 3 == 2 else r1.at[n, c, i]

    s1 = [[
        Ring(lambda d, h, n=n: grad.at[n, 0, pl.ds(2 * h, 2), d], landing(n, 0), rs1_s, rs1_r.at[n], 0, w1.at[n, 0]),
        Ring(lambda d, h, n=n: grad.at[n, 1, d, pl.ds(2 * h, 2)], landing(n, 1), rs1_s, rs1_r.at[n], 1, w1.at[n, 1]),
    ] for n in range(4)]
    s2 = [[
        Ring(lambda d, h, n=n, c=c: a1.at[n, c, d, pl.ds(32 * h, 32)], lambda i, n=n, c=c: r2.at[n, c, i], rs2_s, rs2_r.at[n], 1 - c)
        for c in range(2)] for n in range(4)]
    z_to = (along(2, 1), along(2, 3))

    def z_copy(n):
        piece, half = ((0, 0), (1, 1), (1, 0), (0, 1), (2, 0), (2, 1))[n]
        return remote(c3.at[piece, half], r3.at[n], rs3_s, rs3_r.at[(0, 2, 2, 1, 2, 2)[n]], z_to[n // 3], fq)

    def begin1(n):
        for ring in s1[n]:
            ring.begin()

    def relay1(n):
        take(w1.at[n, 0, pl.ds(0, 4)], rs1_r.at[n, 0])
        for ring in s1[n]:
            ring.relay()

    def begin2(n):
        take(w1.at[n], rs1_r.at[n, 1])
        for c in range(2):
            top, low = s1[n][c].result()
            a1[n, c, 0:2] = top
            a1[n, c, 2:4] = low
            s2[n][c].begin()

    def relay2(n):
        take(r2.at[n, 0, pl.ds(0, 4)], rs2_r.at[n, 0])
        for ring in s2[n]:
            ring.relay()

    def done2(n):
        take(r2.at[n, :, pl.ds(0, 4)], rs2_r.at[n, 1])
        for c in range(2):
            top, low = s2[n][c].result()
            c3[n, c, 0:32] = top
            c3[n, c, 32:64] = low
        if n == 0:
            z_copy(0).start()
            z_copy(3).start()
        elif n < 3:
            half, plain, held = ((1, 1, 0), (0, 4, 3))[n - 1]
            z_copy(plain).start()
            z_copy(held).wait_recv()
            c3[n, 1 - half] = c3[n, 1 - half] + r3[held]
            z_copy((2, 5)[n - 1]).start()

    gradient(0)
    begin1(0)
    gradient(1)
    begin1(1)
    gradient(2)
    relay1(0)
    begin1(2)
    gradient(3)
    relay1(1)
    begin1(3)
    begin2(0)
    relay1(2)
    begin2(1)
    relay2(0)
    relay1(3)
    begin2(2)
    relay2(1)
    done2(0)
    begin2(3)
    relay2(2)
    done2(1)
    relay2(3)
    done2(2)
    done2(3)
    take(r3.at[pl.ds(0, 4)], rs3_r.at[2])
    out_ref[:, 0:128] = c3[3, 0] + r3[2] + r3[4]
    out_ref[:, 128:256] = c3[3, 1] + r3[1] + r3[5]

    sent(qbuf.at[:, pl.ds(0, 3)], q_s)
    sent(encf.at[pl.ds(0, 3)], enc_s)
    sent(sbuf.at[pl.ds(0, 3)], s_s)

    @pl.when(tm < TM - 1)
    def _():
        id_copy.wait_send()

    @pl.when(core == 0)
    def _():
        sent(normed.at[pl.ds(0, 4)], n_s)
        sent(pbuf.at[pl.ds(0, 6)], p_s)

    @pl.when(core == 1)
    def _():
        sent(normed.at[pl.ds(0, 5)], n_s)
        sent(pbuf.at[pl.ds(0, 3)], p_s)

    @pl.when((fq == NF - 1) & (tm < TM - 1))
    def _():
        sent(pbuf.at[pl.ds(0, 4)], h_s)

    sent(tmpl, rs1_s)
    sent(recon, rs2_s)
    sent(pbuf.at[pl.ds(0, 3)], rs3_s)


def on_device(
    spectrum, decay_rate, init_state, clip_ids, encoder, gauss_noise, uniform_noise, boost_count, templates,
):
    vmem = pl.BlockSpec(memory_space=pltpu.VMEM)
    hbm = pl.BlockSpec(memory_space=pl.ANY)
    V = pltpu.VMEM
    dma = pltpu.SemaphoreType.DMA
    loss, grad = pl.pallas_call(
        kernel,
        out_shape=(
            jax.ShapeDtypeStruct((1, FRAMES), f32),
            jax.ShapeDtypeStruct((K * L // TM, BINS), f32),
        ),
        in_specs=[vmem] * 4 + [hbm] * 5,
        out_specs=(vmem, vmem),
        scratch_shapes=[
            V((BINS, FRAMES), bf16), V((BINS, K * L), bf16), V((2, K, 128), f32), V((2, 2, K, 128), f32), V((NF, K, BINS), bf16),
            V((BINS, FRAMES), f32), V((BINS, FRAMES), f32), V((TILES, BINS, 128), bf16),
            V((2, NF, BINS, 128), bf16), V((TILES + 1, K, 128), bf16), V((TILES + 1, K, 128), f32),
            V((1, 128), jnp.int32), V((3, 4, 1, BINS), f32), V((K * L, FRAMES), bf16),
            V((BINS, FRAMES), f32), V((NF, 8, FRAMES), f32), V((BINS, FRAMES), bf16),
            V((4, 2, 4, 4, 64, 128), f32), V((4, 2, 6, 2, 64, 128), bf16), V((4, 2, 4, 64, 128), f32),
            V((4, 2, 64, 128), f32), V((4, 2, 6, 2, 64, 128), bf16), V((4, 2, 2, 2, 64, 128), f32), V((4, 2, 6, 32, 128), f32), V((6, 64, 128), f32),
            dma((7,)), dma, dma, dma, dma((3,)), dma, dma, dma, dma((2,)), dma, dma, dma, dma, dma, dma,
            dma, dma((4, 2)), dma, dma((4, 2)), dma, dma((3,)),
        ],
        compiler_params=pltpu.CompilerParams(
            collective_id=0, has_side_effects=True, vmem_limit_bytes=56 * 1024 * 1024),
        name="topic_step",
    )(
        decay_rate.reshape(1, BINS), init_state.reshape(1, BINS), clip_ids.reshape(1, FRAMES),
        boost_count.reshape(1, K), spectrum, encoder, gauss_noise, uniform_noise, templates,
    )
    return loss.reshape(FRAMES), grad


def solution(mesh):
    placed = (
        P("freq", "tm"), P("freq"), P("freq"), P("tm"), P(None, "freq"), P(None, "tm"),
        P(None, None, "tm"), P(), P("freq", None),
    )
    return jax.shard_map(
        on_device, mesh=mesh, in_specs=placed, out_specs=(P("tm"), P("tm", "freq")), check_vma=False
    )
```

```python
import jax
import jax.numpy as jnp
from jax import lax
from jax.experimental import pallas as pl
from jax.experimental.pallas import tpu as pltpu
from jax.sharding import PartitionSpec as P

F = 1024
K = 256
L = 16
TIME = 49152
BINS = 256
FRAMES = 768
TILES = 6
TM = 64
NF = 4
MESH = pl.DeviceIdType.MESH
f32 = jnp.float32
bf16 = jnp.bfloat16
LOG_GAIN = 0.22314355131420976
OWNER = (0, 0, 1, 2, 2, 3)
SLOT = (0, 1, 0, 0, 1, 0)
ORDER = (2, 1, 3, 0)


def remote(src, dst, send, recv, tm, fq):
    return pltpu.make_async_remote_copy(
        src_ref=src, dst_ref=dst, send_sem=send, recv_sem=recv,
        device_id={"tm": tm, "freq": fq}, device_id_type=MESH,
    )


def take(ref, sem):
    remote(ref, ref, sem, sem, 0, 0).wait_recv()


def sent(ref, sem):
    remote(ref, ref, sem, sem, 0, 0).wait_send()


def kernel(
    decay_ref, init_ref, ids_ref, boost_ref, spec_hbm, enc_hbm, gauss_hbm, unif_hbm, tmpl_hbm,
    loss_ref, out_ref,
    spec_ref, tmpl, gbuf, ubuf, encf, grow, cum, normed, nbuf, pbuf, pf, idsend, idh, qbuf, st,
    recon, sbuf, rat, grad, w1, a1, c3, r1, r1f, r2, r3,
    load_sem, enc_s, enc_r, q_s, q_r, id_s, id_r, n_s, n_r, p_s, p_r, h_s, h_r, s_s, s_r,
    rs1_s, rs1_r, rs2_s, rs2_r, rs3_s, rs3_r,
):
    tm = lax.axis_index("tm")
    fq = lax.axis_index("freq")
    core = lax.rem(fq, 2)
    zlo = fq // 2
    barrier = pltpu.get_barrier_semaphore()
    nxt = lax.rem(tm + 1, TM)

    px = lax.rem(tm, 4)
    py = lax.rem(tm // 4, 4)
    pz = tm // 16

    def along(axis, step):
        if axis == 0:
            return tm - px + lax.rem(px + step, 4)
        if axis == 1:
            return tm - 4 * py + 4 * lax.rem(py + step, 4)
        return tm - 16 * pz + 16 * lax.rem(pz + step, 4)

    pxy = lax.rem(tm, 16)

    def in_plane(step):
        return tm - pxy + lax.rem(pxy + step, 16)

    peers = [(in_plane(step), fq) for step in range(1, 16)] + [(along(2, step), fq) for step in range(1, 4)]
    peers += [(tm, lax.rem(fq + i, NF)) for i in range(1, NF)]
    for place, other in peers:
        pl.semaphore_signal(
            barrier, inc=1, device_id={"tm": place, "freq": other}, device_id_type=MESH)

    load_x = pltpu.make_async_copy(spec_hbm, spec_ref, load_sem.at[5])
    load_x.start()
    load_e = pltpu.make_async_copy(enc_hbm, encf.at[fq], load_sem.at[6])
    load_e.start()
    first = zlo * 3 + core * 2
    load_t = pltpu.make_async_copy(tmpl_hbm, tmpl, load_sem.at[0])

    def tile_loads(slot):
        cols = pl.ds(pl.multiple_of((first + slot) * 128, 128), 128)
        return (
            pltpu.make_async_copy(gauss_hbm.at[:, cols], gbuf.at[slot], load_sem.at[1 + 2 * slot]),
            pltpu.make_async_copy(unif_hbm.at[:, :, cols], ubuf.at[slot], load_sem.at[2 + 2 * slot]),
        )

    for copy in tile_loads(0):
        copy.start()

    @pl.when(core == 0)
    def _():
        for copy in tile_loads(1):
            copy.start()

    load_t.start()

    rows = lax.broadcasted_iota(jnp.int32, (BINS, BINS), 0)
    cols = lax.broadcasted_iota(jnp.int32, (BINS, BINS), 1)
    eye = rows == cols
    tri = (rows <= cols).astype(bf16)

    def column(row):
        return jnp.sum(jnp.where(eye, jnp.broadcast_to(row, (BINS, BINS)), 0.0), axis=1, keepdims=True)

    def row_of(col):
        return jnp.sum(jnp.where(eye, jnp.broadcast_to(col, (BINS, BINS)), 0.0), axis=0, keepdims=True)

    decay_row = decay_ref[...]
    lost = 1.0 - (1.0 - decay_row)
    log_row = -lost * (1.0 + lost * (1 / 2 + lost * (1 / 3 + lost * (1 / 4 + lost * (1 / 5 + lost * (1 / 6))))))
    log_col = column(log_row)
    decay_col = column(decay_row)
    ids_row = ids_ref[...].reshape(1, FRAMES)
    ids = ids_row.astype(f32)
    idsend[...] = ids_row[:, FRAMES - 128:]
    lift = jnp.exp(ids * LOG_GAIN)
    load_x.wait()
    carry = jnp.zeros((BINS, 1), f32)
    for b in range(3):
        span = slice(b * 256, b * 256 + 256)
        steps = (cols + (b * 256 + 1)).astype(f32)
        power = steps * log_col
        grow[:, span] = jnp.exp(power)
        v = decay_col * (spec_ref[:, span].astype(f32) * lift[:, span]) * jnp.exp(-power)
        hi = v.astype(bf16)
        rest = v - hi.astype(f32)
        mid = rest.astype(bf16)
        low = (rest - mid.astype(f32)).astype(bf16)
        c = (
            jnp.dot(hi, tri, preferred_element_type=f32)
            + jnp.dot(mid, tri, preferred_element_type=f32)
            + jnp.dot(low, tri, preferred_element_type=f32)
        ) + carry
        cum[:, span] = c
        carry = c[:, 255:256]
    q_col = carry * jnp.exp(log_col * float(FRAMES))
    positions = (px, py, pz)

    def q_send(stage, row):
        pos, count, place = ((pxy, 16, in_plane), (pz, 4, lambda step: along(2, step)))[stage]
        slot = qbuf.at[16 * stage + pos]
        slot[...] = row
        for step in range(1, count):
            remote(slot, slot, q_s, q_r.at[stage], place(step), fq).start()

    def q_take(stage, jump):
        pos, count = ((pxy, 16), (pz, 4))[stage]
        take(qbuf.at[pl.ds(0, count - 1)], q_r.at[stage])
        ahead = jnp.zeros((1, BINS), f32)
        total = jnp.zeros((1, BINS), f32)
        for j in range(count):
            row = qbuf[16 * stage + j]
            ahead = jnp.where(j < pos, jump * ahead + row, ahead)
            total = jump * total + row
        return ahead, total

    q_row = row_of(q_col)
    pl.semaphore_wait(barrier, len(peers))
    q_send(0, q_row)

    def enc_copy(i):
        return remote(encf.at[fq], encf.at[fq], enc_s, enc_r, tm, lax.rem(fq + i, NF))

    load_e.wait()
    for i in range(1, NF):
        enc_copy(i).start()
    boost = column(boost_ref[...].astype(f32))

    def ready_noise(slot):
        for copy in tile_loads(slot):
            copy.wait()
        ubuf[slot] = jnp.log(ubuf[slot])

    ready_noise(0)

    @pl.when(core == 0)
    def _():
        ready_noise(1)

    near, total = q_take(0, jnp.exp(log_row * float(FRAMES)))
    q_send(1, total)
    far, total = q_take(1, jnp.exp(log_row * float(16 * FRAMES)))
    entry = near + jnp.exp(log_row * (float(FRAMES) * pxy.astype(f32))) * (
        far + jnp.exp(log_row * (float(16 * FRAMES) * pz.astype(f32))) * init_ref[...])
    id_copy = remote(idsend, idh, id_s, id_r, nxt, fq)

    @pl.when(tm < TM - 1)
    def _():
        id_copy.start()

    entry_col = column(entry)
    for t in range(TILES):
        span = slice(t * 128, t * 128 + 128)
        drop = jnp.exp(ids[:, span] * (-LOG_GAIN))
        smooth = grow[:, span] * (entry_col + cum[:, span]) * drop
        normed[t] = (spec_ref[:, span].astype(f32) * lax.rsqrt(smooth + 0.1)).astype(bf16)

    def n_copy(t):
        return remote(
            normed.at[t], nbuf.at[SLOT[t], fq], n_s, n_r.at[SLOT[t]], tm, OWNER[t])

    for t in (3, 4, 5, 0, 1, 2):
        @pl.when(fq != OWNER[t])
        def _(t=t):
            n_copy(t).start()

        @pl.when(fq == OWNER[t])
        def _(t=t):
            nbuf[SLOT[t], fq] = normed[t]

    take(encf.at[pl.ds(0, 3)], enc_r)

    def p_copy(t, i):
        return remote(pbuf.at[1 + t], pbuf.at[1 + t], p_s, p_r, tm, lax.rem(fq + i, NF))

    def halo_copy(q):
        return remote(pbuf.at[TILES], pbuf.at[0], h_s, h_r, nxt, q)

    def sample(slot):
        take(nbuf.at[slot, pl.ds(0, 3)], n_r.at[slot])
        logits = jnp.dot(encf[0], nbuf[slot, 0], preferred_element_type=f32)
        for q in range(1, NF):
            logits += jnp.dot(encf[q], nbuf[slot, q], preferred_element_type=f32)
        conc = jnp.maximum(logits, 0.0) + jnp.log(1.0 + jnp.exp(-jnp.abs(logits))) + 0.5
        offset = conc + boost - 1.0 / 3.0
        linear = 1.0 + lax.rsqrt(9.0 * offset) * gbuf[slot]
        second = jnp.where(boost >= 1.5, ubuf[slot, 1], 0.0)
        power = ubuf[slot, 0] / conc + second / (conc + 1.0)
        draw = offset * linear * linear * linear * jnp.exp(power)
        total = jnp.sum(draw, axis=0, keepdims=True)
        pbuf[1 + first + slot] = (draw / total).astype(bf16)

    sample(0)
    for t in range(TILES):
        if SLOT[t] == 0:
            @pl.when(fq == OWNER[t])
            def _(t=t):
                for i in range(1, NF):
                    p_copy(t, i).start()

    @pl.when((fq == NF - 1) & (tm < TM - 1))
    def _():
        for q in range(NF):
            halo_copy(q).start()

    @pl.when(core == 0)
    def _():
        sample(1)

    for t in range(TILES):
        if SLOT[t] == 1:
            @pl.when(fq == OWNER[t])
            def _(t=t):
                for i in range(1, NF):
                    p_copy(t, i).start()

    @pl.when(tm == 0)
    def _():
        pbuf[0] = jnp.zeros((K, 128), bf16)
        idh[...] = jnp.full((1, 128), -1, jnp.int32)

    @pl.when(tm > 0)
    def _():
        id_copy.wait_recv()
        halo_copy(0).wait_recv()

    @pl.when(core == 0)
    def _():
        take(pbuf.at[pl.ds(0, 4)], p_r)

    @pl.when(core == 1)
    def _():
        take(pbuf.at[pl.ds(0, 5)], p_r)

    lane = lax.broadcasted_iota(jnp.int32, (L, 128), 1)
    lag = lax.broadcasted_iota(jnp.int32, (L, 128), 0)
    head = lane < lag

    def lagged(row):
        return pltpu.roll(jnp.broadcast_to(row, (L, 128)), 0, 1, stride=1, stride_axis=0)

    id_rows = [idh[...].astype(f32)] + [ids[:, t * 128:t * 128 + 128] for t in range(TILES)]
    rolled = [lagged(r) for r in id_rows]
    keep = []
    for t in range(TILES):
        source = jnp.where(head, rolled[t], rolled[t + 1])
        keep.append(source == jnp.broadcast_to(id_rows[t + 1], (L, 128)))

    for t in range(TILES + 1):
        pf[t] = pbuf[t].astype(f32)

    def build_row(k, carry):
        prior = lagged(pf[0, pl.ds(k, 1), :])
        for t in range(TILES):
            current = lagged(pf[t + 1, pl.ds(k, 1), :])
            value = jnp.where(keep[t], jnp.where(head, prior, current), 0.0)
            st[pl.ds(pl.multiple_of(k * L, L), L), t * 128:t * 128 + 128] = value.astype(bf16)
            prior = current
        return carry

    lax.fori_loop(0, K, build_row, 0, unroll=16)

    load_t.wait()
    for b in range(3):
        span = slice(b * 256, b * 256 + 256)
        rec = jnp.dot(tmpl[...], st[:, span], preferred_element_type=f32)
        x = spec_ref[:, span].astype(f32)
        recon[:, span] = x / rec
        sbuf[fq, 0:1, span] = jnp.sum(rec, axis=0, keepdims=True)
        sbuf[fq, 1:2, span] = jnp.sum(x, axis=0, keepdims=True)
        sbuf[fq, 2:3, span] = jnp.sum(x * jnp.log(rec), axis=0, keepdims=True)

    def s_copy(i):
        return remote(sbuf.at[fq], sbuf.at[fq], s_s, s_r, tm, lax.rem(fq + i, NF))

    for i in range(1, NF):
        s_copy(i).start()
    take(sbuf.at[pl.ds(0, 3)], s_r)
    sums = sbuf[0, 0:3, :] + sbuf[1, 0:3, :] + sbuf[2, 0:3, :] + sbuf[3, 0:3, :]
    recon_sum, spec_sum, log_sum = sums[0:1], sums[1:2], sums[2:3]
    loss_ref[...] = jnp.log(recon_sum) - log_sum / spec_sum
    scale = F * K / TIME
    plain = scale / recon_sum
    part = scale / spec_sum
    rat[...] = (plain - part * recon[...]).astype(bf16)

    def gradient(n):
        z = lax.rem(pz + ORDER[n], 4)
        g = lax.dot_general(
            st[pl.ds(pl.multiple_of(z * 1024, 1024), 1024), :], rat[...],
            (((1,), (1,)), ((), ())), preferred_element_type=f32).reshape(4, 4, 64, 256)
        grad[n, 0] = g[..., 0:128]
        grad[n, 1] = g[..., 128:256]

    class Ring:
        def __init__(self, view, buf, send, recv, axis, staged=None):
            self.view, self.buf, self.send, self.recv, self.staged = view, buf, send, recv, staged
            self.pos = positions[axis]
            to = (along(axis, 1), along(axis, 3))
            far, right, left = (lax.rem(self.pos + i, 4) for i in (2, 1, 3))
            self.parts = (
                (far, 0, to[0]), (right, 1, to[0]), (right, 0, to[0]),
                (far, 1, to[1]), (left, 0, to[1]), (left, 1, to[1]),
            )

        def copy(self, n):
            d, h, to = self.parts[n]
            src = self.view(d, h) if self.staged is None or n % 3 == 2 else self.staged.at[n]
            return remote(src, self.buf(n), self.send, self.recv.at[0 if n % 3 == 0 else 1], to, fq)

        def push(self, n, more=None):
            view = self.view(self.parts[n][0], self.parts[n][1])
            if more is not None:
                view[...] = view[...] + self.buf(more)[...].astype(f32)
            elif self.staged is not None:
                self.staged[n] = view[...].astype(self.staged.dtype)
            self.copy(n).start()

        def begin(self):
            for n in (0, 3, 1, 4):
                self.push(n)

        def relay(self):
            for n in (0, 3):
                self.push(n + 2, n)

        def result(self):
            return tuple(
                self.view(self.pos, h)[...] + self.buf(l)[...].astype(f32) + self.buf(r)[...].astype(f32)
                for h, l, r in ((0, 2, 4), (1, 1, 5)))

    def landing(n, c):
        return lambda i: r1f.at[n, c, i // 3] if i % 3 == 2 else r1.at[n, c, i]

    s1 = [[
        Ring(lambda d, h, n=n: grad.at[n, 0, pl.ds(2 * h, 2), d], landing(n, 0), rs1_s, rs1_r.at[n], 0, w1.at[n, 0]),
        Ring(lambda d, h, n=n: grad.at[n, 1, d, pl.ds(2 * h, 2)], landing(n, 1), rs1_s, rs1_r.at[n], 1, w1.at[n, 1]),
    ] for n in range(4)]
    s2 = [[
        Ring(lambda d, h, n=n, c=c: a1.at[n, c, d, pl.ds(32 * h, 32)], lambda i, n=n, c=c: r2.at[n, c, i], rs2_s, rs2_r.at[n], 1 - c)
        for c in range(2)] for n in range(4)]
    z_to = (along(2, 1), along(2, 3))

    def z_copy(n):
        piece, half = ((0, 0), (1, 1), (1, 0), (0, 1), (2, 0), (2, 1))[n]
        return remote(c3.at[piece, half], r3.at[n], rs3_s, rs3_r.at[(0, 2, 2, 1, 2, 2)[n]], z_to[n // 3], fq)

    def begin1(n):
        for ring in s1[n]:
            ring.begin()

    def relay1(n):
        take(w1.at[n, 0, pl.ds(0, 4)], rs1_r.at[n, 0])
        for ring in s1[n]:
            ring.relay()

    def begin2(n):
        take(w1.at[n], rs1_r.at[n, 1])
        for c in range(2):
            top, low = s1[n][c].result()
            a1[n, c, 0:2] = top
            a1[n, c, 2:4] = low
            s2[n][c].begin()

    def relay2(n):
        take(r2.at[n, 0, pl.ds(0, 4)], rs2_r.at[n, 0])
        for ring in s2[n]:
            ring.relay()

    def done2(n):
        take(r2.at[n, :, pl.ds(0, 4)], rs2_r.at[n, 1])
        for c in range(2):
            top, low = s2[n][c].result()
            c3[n, c, 0:32] = top
            c3[n, c, 32:64] = low
        if n == 0:
            z_copy(0).start()
            z_copy(3).start()
        elif n < 3:
            half, plain, held = ((1, 1, 0), (0, 4, 3))[n - 1]
            z_copy(plain).start()
            z_copy(held).wait_recv()
            c3[n, 1 - half] = c3[n, 1 - half] + r3[held]
            z_copy((2, 5)[n - 1]).start()

    gradient(0)
    begin1(0)
    gradient(1)
    begin1(1)
    gradient(2)
    relay1(0)
    begin1(2)
    gradient(3)
    relay1(1)
    begin1(3)
    begin2(0)
    relay1(2)
    begin2(1)
    relay2(0)
    relay1(3)
    begin2(2)
    relay2(1)
    done2(0)
    begin2(3)
    relay2(2)
    done2(1)
    relay2(3)
    done2(2)
    done2(3)
    take(r3.at[pl.ds(0, 4)], rs3_r.at[2])
    out_ref[:, 0:128] = c3[3, 0] + r3[2] + r3[4]
    out_ref[:, 128:256] = c3[3, 1] + r3[1] + r3[5]

    sent(qbuf.at[pl.ds(0, 18)], q_s)
    sent(encf.at[pl.ds(0, 3)], enc_s)
    sent(sbuf.at[pl.ds(0, 3)], s_s)

    @pl.when(tm < TM - 1)
    def _():
        id_copy.wait_send()

    @pl.when(core == 0)
    def _():
        sent(normed.at[pl.ds(0, 4)], n_s)
        sent(pbuf.at[pl.ds(0, 6)], p_s)

    @pl.when(core == 1)
    def _():
        sent(normed.at[pl.ds(0, 5)], n_s)
        sent(pbuf.at[pl.ds(0, 3)], p_s)

    @pl.when((fq == NF - 1) & (tm < TM - 1))
    def _():
        sent(pbuf.at[pl.ds(0, 4)], h_s)

    sent(tmpl, rs1_s)
    sent(recon, rs2_s)
    sent(pbuf.at[pl.ds(0, 3)], rs3_s)


def hand_over(loss_in, grad_in, loss_ref, grad_ref):
    loss_ref[...] = loss_in[...].reshape(FRAMES)
    grad_ref[...] = grad_in[...]


def on_device(
    spectrum, decay_rate, init_state, clip_ids, encoder, gauss_noise, uniform_noise, boost_count, templates,
):
    vmem = pl.BlockSpec(memory_space=pltpu.VMEM)
    hbm = pl.BlockSpec(memory_space=pl.ANY)
    V = pltpu.VMEM
    dma = pltpu.SemaphoreType.DMA
    loss, grad = pl.pallas_call(
        kernel,
        out_shape=(
            jax.ShapeDtypeStruct((1, FRAMES), f32),
            jax.ShapeDtypeStruct((K * L // TM, BINS), f32),
        ),
        in_specs=[vmem] * 4 + [hbm] * 5,
        out_specs=(vmem, vmem),
        scratch_shapes=[
            V((BINS, FRAMES), bf16), V((BINS, K * L), bf16), V((2, K, 128), f32), V((2, 2, K, 128), f32), V((NF, K, BINS), bf16),
            V((BINS, FRAMES), f32), V((BINS, FRAMES), f32), V((TILES, BINS, 128), bf16),
            V((2, NF, BINS, 128), bf16), V((TILES + 1, K, 128), bf16), V((TILES + 1, K, 128), f32),
            V((1, 128), jnp.int32), V((1, 128), jnp.int32), V((20, 1, BINS), f32), V((K * L, FRAMES), bf16),
            V((BINS, FRAMES), f32), V((NF, 8, FRAMES), f32), V((BINS, FRAMES), bf16),
            V((4, 2, 4, 4, 64, 128), f32), V((4, 2, 6, 2, 64, 128), bf16), V((4, 2, 4, 64, 128), f32),
            V((4, 2, 64, 128), f32), V((4, 2, 6, 2, 64, 128), bf16), V((4, 2, 2, 2, 64, 128), f32), V((4, 2, 6, 32, 128), f32), V((6, 64, 128), f32),
            dma((7,)), dma, dma, dma, dma((2,)), dma, dma, dma, dma((2,)), dma, dma, dma, dma, dma, dma,
            dma, dma((4, 2)), dma, dma((4, 2)), dma, dma((3,)),
        ],
        compiler_params=pltpu.CompilerParams(
            collective_id=0, has_side_effects=True, vmem_limit_bytes=56 * 1024 * 1024),
        name="topic_step",
    )(
        decay_rate.reshape(1, BINS), init_state.reshape(1, BINS), clip_ids,
        boost_count.reshape(1, K), spectrum, encoder, gauss_noise, uniform_noise, templates,
    )
    return pl.pallas_call(
        hand_over,
        out_shape=(jax.ShapeDtypeStruct((FRAMES,), f32), jax.ShapeDtypeStruct((K * L // TM, BINS), f32)),
        in_specs=[vmem] * 2,
        out_specs=(vmem, vmem),
        name="hand_over",
    )(loss, grad)


def solution(mesh):
    placed = (
        P("freq", "tm"), P("freq"), P("freq"), P("tm"), P(None, "freq"), P(None, "tm"),
        P(None, None, "tm"), P(), P("freq", None),
    )
    return jax.shard_map(
        on_device, mesh=mesh, in_specs=placed, out_specs=(P("tm"), P("tm", "freq")), check_vma=False
    )
```

```python
import jax
import jax.numpy as jnp
from jax import lax
from jax.experimental import pallas as pl
from jax.experimental.pallas import tpu as pltpu
from jax.sharding import PartitionSpec as P

F = 1024
K = 256
L = 16
TIME = 49152
BINS = 256
FRAMES = 768
TILES = 6
TM = 64
NF = 4
MESH = pl.DeviceIdType.MESH
f32 = jnp.float32
bf16 = jnp.bfloat16
LOG_GAIN = 0.22314355131420976
OWNER = (0, 0, 1, 2, 2, 3)
SLOT = (0, 1, 0, 0, 1, 0)
ORDER = (2, 1, 3, 0)


def remote(src, dst, send, recv, tm, fq):
    return pltpu.make_async_remote_copy(
        src_ref=src, dst_ref=dst, send_sem=send, recv_sem=recv,
        device_id={"tm": tm, "freq": fq}, device_id_type=MESH,
    )


def take(ref, sem):
    remote(ref, ref, sem, sem, 0, 0).wait_recv()


def sent(ref, sem):
    remote(ref, ref, sem, sem, 0, 0).wait_send()


def kernel(
    decay_ref, init_ref, ids_ref, boost_ref, spec_hbm, enc_hbm, gauss_hbm, unif_hbm, tmpl_hbm,
    loss_ref, out_ref,
    spec_ref, tmpl, gbuf, ubuf, encf, grow, cum, normed, nbuf, pbuf, pf, idsend, idh, qbuf, st,
    tbuf, sums, sbuf, rat, grad, w1, a1, c3, r1, r1f, r2, r3,
    load_sem, t_s, t_r, enc_s, enc_r, q_s, q_r, id_s, id_r, n_s, n_r, p_s, p_r, h_s, h_r, s_s, s_r,
    rs1_s, rs1_r, rs2_s, rs2_r, rs3_s, rs3_r,
):
    tm = lax.axis_index("tm")
    fq = lax.axis_index("freq")
    core = lax.rem(fq, 2)
    zlo = fq // 2
    barrier = pltpu.get_barrier_semaphore()
    nxt = lax.rem(tm + 1, TM)

    px = lax.rem(tm, 4)
    py = lax.rem(tm // 4, 4)
    pz = tm // 16

    def along(axis, step):
        if axis == 0:
            return tm - px + lax.rem(px + step, 4)
        if axis == 1:
            return tm - 4 * py + 4 * lax.rem(py + step, 4)
        return tm - 16 * pz + 16 * lax.rem(pz + step, 4)

    pxy = lax.rem(tm, 16)

    def in_plane(step):
        return tm - pxy + lax.rem(pxy + step, 16)

    peers = [(in_plane(step), fq) for step in range(1, 16)] + [(along(2, step), fq) for step in range(1, 4)]
    peers += [(tm, lax.rem(fq + i, NF)) for i in range(1, NF)]
    for place, other in peers:
        pl.semaphore_signal(
            barrier, inc=1, device_id={"tm": place, "freq": other}, device_id_type=MESH)

    load_x = pltpu.make_async_copy(spec_hbm, spec_ref, load_sem.at[5])
    load_x.start()
    load_e = pltpu.make_async_copy(enc_hbm, encf.at[fq], load_sem.at[6])
    load_e.start()
    first = zlo * 3 + core * 2
    load_t = pltpu.make_async_copy(tmpl_hbm, tmpl.at[pl.ds(0, BINS)], load_sem.at[0])

    def tile_loads(slot):
        cols = pl.ds(pl.multiple_of((first + slot) * 128, 128), 128)
        return (
            pltpu.make_async_copy(gauss_hbm.at[:, cols], gbuf.at[slot], load_sem.at[1 + 2 * slot]),
            pltpu.make_async_copy(unif_hbm.at[:, :, cols], ubuf.at[slot], load_sem.at[2 + 2 * slot]),
        )

    for copy in tile_loads(0):
        copy.start()

    @pl.when(core == 0)
    def _():
        for copy in tile_loads(1):
            copy.start()

    load_t.start()

    rows = lax.broadcasted_iota(jnp.int32, (BINS, BINS), 0)
    cols = lax.broadcasted_iota(jnp.int32, (BINS, BINS), 1)
    eye = rows == cols
    tri = (rows <= cols).astype(bf16)

    def column(row):
        return jnp.sum(jnp.where(eye, jnp.broadcast_to(row, (BINS, BINS)), 0.0), axis=1, keepdims=True)

    def row_of(col):
        return jnp.sum(jnp.where(eye, jnp.broadcast_to(col, (BINS, BINS)), 0.0), axis=0, keepdims=True)

    decay_row = decay_ref[...]
    lost = 1.0 - (1.0 - decay_row)
    log_row = -lost * (1.0 + lost * (1 / 2 + lost * (1 / 3 + lost * (1 / 4 + lost * (1 / 5 + lost * (1 / 6))))))
    log_col = column(log_row)
    decay_col = column(decay_row)
    ids_row = ids_ref[...].reshape(1, FRAMES)
    ids = ids_row.astype(f32)
    idsend[...] = ids_row[:, FRAMES - 128:]
    lift = jnp.exp(ids * LOG_GAIN)
    load_x.wait()
    carry = jnp.zeros((BINS, 1), f32)
    for b in range(3):
        span = slice(b * 256, b * 256 + 256)
        steps = (cols + (b * 256 + 1)).astype(f32)
        power = steps * log_col
        grow[:, span] = jnp.exp(power)
        v = decay_col * (spec_ref[:, span].astype(f32) * lift[:, span]) * jnp.exp(-power)
        hi = v.astype(bf16)
        rest = v - hi.astype(f32)
        mid = rest.astype(bf16)
        low = (rest - mid.astype(f32)).astype(bf16)
        c = (
            jnp.dot(hi, tri, preferred_element_type=f32)
            + jnp.dot(mid, tri, preferred_element_type=f32)
            + jnp.dot(low, tri, preferred_element_type=f32)
        ) + carry
        cum[:, span] = c
        carry = c[:, 255:256]
    q_col = carry * jnp.exp(log_col * float(FRAMES))
    positions = (px, py, pz)

    def q_send(stage, row):
        pos, count, place = ((pxy, 16, in_plane), (pz, 4, lambda step: along(2, step)))[stage]
        slot = qbuf.at[16 * stage + pos]
        slot[...] = row
        for step in range(1, count):
            remote(slot, slot, q_s, q_r.at[stage], place(step), fq).start()

    def q_take(stage, jump):
        pos, count = ((pxy, 16), (pz, 4))[stage]
        take(qbuf.at[pl.ds(0, count - 1)], q_r.at[stage])
        ahead = jnp.zeros((1, BINS), f32)
        total = jnp.zeros((1, BINS), f32)
        for j in range(count):
            row = qbuf[16 * stage + j]
            ahead = jnp.where(j < pos, jump * ahead + row, ahead)
            total = jump * total + row
        return ahead, total

    q_row = row_of(q_col)
    pl.semaphore_wait(barrier, len(peers))
    q_send(0, q_row)

    def enc_copy(i):
        return remote(encf.at[fq], encf.at[fq], enc_s, enc_r, tm, lax.rem(fq + i, NF))

    load_e.wait()
    for i in range(1, NF):
        enc_copy(i).start()
    load_t.wait()
    ones = jnp.ones((8, BINS), bf16)
    tbuf[fq, :, 0:K * L] = jnp.dot(ones, tmpl[0:BINS, :], preferred_element_type=f32)[0:1]
    tbuf[fq, :, K * L:] = jnp.dot(ones, spec_ref[...], preferred_element_type=f32)[0:1]
    for i in range(1, NF):
        remote(tbuf.at[fq], tbuf.at[fq], t_s, t_r, tm, lax.rem(fq + i, NF)).start()

    boost = column(boost_ref[...].astype(f32))

    def ready_noise(slot):
        for copy in tile_loads(slot):
            copy.wait()
        ubuf[slot] = jnp.log(ubuf[slot])

    ready_noise(0)

    @pl.when(core == 0)
    def _():
        ready_noise(1)

    near, total = q_take(0, jnp.exp(log_row * float(FRAMES)))
    q_send(1, total)
    take(tbuf.at[pl.ds(0, 3)], t_r)
    whole = tbuf[0] + tbuf[1] + tbuf[2] + tbuf[3]
    sums[1:2] = whole[:, K * L:]
    whole = whole[:, 0:K * L]
    hi = whole.astype(bf16).astype(f32)
    mid = (whole - hi).astype(bf16).astype(f32)
    low = whole - hi - mid
    place = lax.broadcasted_iota(jnp.int32, (16, K * L), 0)
    tmpl[BINS:, :] = jnp.where(
        place == 0, hi, jnp.where(place == 1, mid, jnp.where(place == 2, low, 0.0))).astype(bf16)
    far, total = q_take(1, jnp.exp(log_row * float(16 * FRAMES)))
    entry = near + jnp.exp(log_row * (float(FRAMES) * pxy.astype(f32))) * (
        far + jnp.exp(log_row * (float(16 * FRAMES) * pz.astype(f32))) * init_ref[...])
    id_copy = remote(idsend, idh, id_s, id_r, nxt, fq)

    @pl.when(tm < TM - 1)
    def _():
        id_copy.start()

    entry_col = column(entry)
    for t in range(TILES):
        span = slice(t * 128, t * 128 + 128)
        drop = jnp.exp(ids[:, span] * (-LOG_GAIN))
        smooth = grow[:, span] * (entry_col + cum[:, span]) * drop
        normed[t] = (spec_ref[:, span].astype(f32) * lax.rsqrt(smooth + 0.1)).astype(bf16)

    def n_copy(t):
        return remote(
            normed.at[t], nbuf.at[SLOT[t], fq], n_s, n_r.at[SLOT[t]], tm, OWNER[t])

    for t in (3, 4, 5, 0, 1, 2):
        @pl.when(fq != OWNER[t])
        def _(t=t):
            n_copy(t).start()

        @pl.when(fq == OWNER[t])
        def _(t=t):
            nbuf[SLOT[t], fq] = normed[t]

    take(encf.at[pl.ds(0, 3)], enc_r)

    def p_copy(t, i):
        return remote(pbuf.at[1 + t], pbuf.at[1 + t], p_s, p_r, tm, lax.rem(fq + i, NF))

    def halo_copy(q):
        return remote(pbuf.at[TILES], pbuf.at[0], h_s, h_r, nxt, q)

    def sample(slot):
        take(nbuf.at[slot, pl.ds(0, 3)], n_r.at[slot])
        logits = jnp.dot(encf[0], nbuf[slot, 0], preferred_element_type=f32)
        for q in range(1, NF):
            logits += jnp.dot(encf[q], nbuf[slot, q], preferred_element_type=f32)
        conc = jnp.maximum(logits, 0.0) + jnp.log(1.0 + jnp.exp(-jnp.abs(logits))) + 0.5
        offset = conc + boost - 1.0 / 3.0
        linear = 1.0 + lax.rsqrt(9.0 * offset) * gbuf[slot]
        second = jnp.where(boost >= 1.5, ubuf[slot, 1], 0.0)
        power = ubuf[slot, 0] / conc + second / (conc + 1.0)
        draw = offset * linear * linear * linear * jnp.exp(power)
        total = jnp.sum(draw, axis=0, keepdims=True)
        pbuf[1 + first + slot] = (draw / total).astype(bf16)

    sample(0)
    for t in range(TILES):
        if SLOT[t] == 0:
            @pl.when(fq == OWNER[t])
            def _(t=t):
                for i in range(1, NF):
                    p_copy(t, i).start()

    @pl.when((fq == NF - 1) & (tm < TM - 1))
    def _():
        for q in range(NF):
            halo_copy(q).start()

    @pl.when(core == 0)
    def _():
        sample(1)

    for t in range(TILES):
        if SLOT[t] == 1:
            @pl.when(fq == OWNER[t])
            def _(t=t):
                for i in range(1, NF):
                    p_copy(t, i).start()

    @pl.when(tm == 0)
    def _():
        pbuf[0] = jnp.zeros((K, 128), bf16)
        idh[...] = jnp.full((1, 128), -1, jnp.int32)

    @pl.when(tm > 0)
    def _():
        id_copy.wait_recv()
        halo_copy(0).wait_recv()

    @pl.when(core == 0)
    def _():
        take(pbuf.at[pl.ds(0, 4)], p_r)

    @pl.when(core == 1)
    def _():
        take(pbuf.at[pl.ds(0, 5)], p_r)

    lane = lax.broadcasted_iota(jnp.int32, (L, 128), 1)
    lag = lax.broadcasted_iota(jnp.int32, (L, 128), 0)
    head = lane < lag

    def lagged(row):
        return pltpu.roll(jnp.broadcast_to(row, (L, 128)), 0, 1, stride=1, stride_axis=0)

    id_rows = [idh[...].astype(f32)] + [ids[:, t * 128:t * 128 + 128] for t in range(TILES)]
    rolled = [lagged(r) for r in id_rows]
    keep = []
    for t in range(TILES):
        source = jnp.where(head, rolled[t], rolled[t + 1])
        keep.append(source == jnp.broadcast_to(id_rows[t + 1], (L, 128)))

    for t in range(TILES + 1):
        pf[t] = pbuf[t].astype(f32)

    def build_row(k, carry):
        prior = lagged(pf[0, pl.ds(k, 1), :])
        for t in range(TILES):
            current = lagged(pf[t + 1, pl.ds(k, 1), :])
            value = jnp.where(keep[t], jnp.where(head, prior, current), 0.0)
            st[pl.ds(pl.multiple_of(k * L, L), L), t * 128:t * 128 + 128] = value.astype(bf16)
            prior = current
        return carry

    lax.fori_loop(0, K, build_row, 0, unroll=16)

    scale = F * K / TIME
    for b in range(3):
        span = slice(b * 256, b * 256 + 256)
        rec = jnp.dot(tmpl[...], st[:, span], preferred_element_type=f32)
        recon_sum = rec[BINS:BINS + 1] + rec[BINS + 1:BINS + 2] + rec[BINS + 2:BINS + 3]
        rec = rec[0:BINS]
        x = spec_ref[:, span].astype(f32)
        rat[:, span] = (scale / recon_sum - (scale / sums[1:2, span]) * (x / rec)).astype(bf16)
        sums[0:1, span] = recon_sum
        sbuf[fq, :, span] = jnp.sum(x * jnp.log(rec), axis=0, keepdims=True)

    def s_copy(i):
        return remote(sbuf.at[fq], sbuf.at[fq], s_s, s_r, tm, lax.rem(fq + i, NF))

    for i in range(1, NF):
        s_copy(i).start()

    def gradient(n):
        z = lax.rem(pz + ORDER[n], 4)
        g = lax.dot_general(
            st[pl.ds(pl.multiple_of(z * 1024, 1024), 1024), :], rat[...],
            (((1,), (1,)), ((), ())), preferred_element_type=f32).reshape(4, 4, 64, 256)
        grad[n, 0] = g[..., 0:128]
        grad[n, 1] = g[..., 128:256]

    class Ring:
        def __init__(self, view, buf, send, recv, axis, staged=None):
            self.view, self.buf, self.send, self.recv, self.staged = view, buf, send, recv, staged
            self.pos = positions[axis]
            to = (along(axis, 1), along(axis, 3))
            far, right, left = (lax.rem(self.pos + i, 4) for i in (2, 1, 3))
            self.parts = (
                (far, 0, to[0]), (right, 1, to[0]), (right, 0, to[0]),
                (far, 1, to[1]), (left, 0, to[1]), (left, 1, to[1]),
            )

        def copy(self, n):
            d, h, to = self.parts[n]
            src = self.view(d, h) if self.staged is None or n % 3 == 2 else self.staged.at[n]
            return remote(src, self.buf(n), self.send, self.recv.at[0 if n % 3 == 0 else 1], to, fq)

        def push(self, n, more=None):
            view = self.view(self.parts[n][0], self.parts[n][1])
            if more is not None:
                view[...] = view[...] + self.buf(more)[...].astype(f32)
            elif self.staged is not None:
                self.staged[n] = view[...].astype(self.staged.dtype)
            self.copy(n).start()

        def begin(self):
            for n in (0, 3, 1, 4):
                self.push(n)

        def relay(self):
            for n in (0, 3):
                self.push(n + 2, n)

        def result(self):
            return tuple(
                self.view(self.pos, h)[...] + self.buf(l)[...].astype(f32) + self.buf(r)[...].astype(f32)
                for h, l, r in ((0, 2, 4), (1, 1, 5)))

    def landing(n, c):
        return lambda i: r1f.at[n, c, i // 3] if i % 3 == 2 else r1.at[n, c, i]

    s1 = [[
        Ring(lambda d, h, n=n: grad.at[n, 0, pl.ds(2 * h, 2), d], landing(n, 0), rs1_s, rs1_r.at[n], 0, w1.at[n, 0]),
        Ring(lambda d, h, n=n: grad.at[n, 1, d, pl.ds(2 * h, 2)], landing(n, 1), rs1_s, rs1_r.at[n], 1, w1.at[n, 1]),
    ] for n in range(4)]
    s2 = [[
        Ring(lambda d, h, n=n, c=c: a1.at[n, c, d, pl.ds(32 * h, 32)], lambda i, n=n, c=c: r2.at[n, c, i], rs2_s, rs2_r.at[n], 1 - c)
        for c in range(2)] for n in range(4)]
    z_to = (along(2, 1), along(2, 3))

    def z_copy(n):
        piece, half = ((0, 0), (1, 1), (1, 0), (0, 1), (2, 0), (2, 1))[n]
        return remote(c3.at[piece, half], r3.at[n], rs3_s, rs3_r.at[(0, 2, 2, 1, 2, 2)[n]], z_to[n // 3], fq)

    def begin1(n):
        for ring in s1[n]:
            ring.begin()

    def relay1(n):
        take(w1.at[n, 0, pl.ds(0, 4)], rs1_r.at[n, 0])
        for ring in s1[n]:
            ring.relay()

    def begin2(n):
        take(w1.at[n], rs1_r.at[n, 1])
        for c in range(2):
            top, low = s1[n][c].result()
            a1[n, c, 0:2] = top
            a1[n, c, 2:4] = low
            s2[n][c].begin()

    def relay2(n):
        take(r2.at[n, 0, pl.ds(0, 4)], rs2_r.at[n, 0])
        for ring in s2[n]:
            ring.relay()

    def done2(n):
        take(r2.at[n, :, pl.ds(0, 4)], rs2_r.at[n, 1])
        for c in range(2):
            top, low = s2[n][c].result()
            c3[n, c, 0:32] = top
            c3[n, c, 32:64] = low
        if n == 0:
            z_copy(0).start()
            z_copy(3).start()
        elif n < 3:
            half, plain, held = ((1, 1, 0), (0, 4, 3))[n - 1]
            z_copy(plain).start()
            z_copy(held).wait_recv()
            c3[n, 1 - half] = c3[n, 1 - half] + r3[held]
            z_copy((2, 5)[n - 1]).start()

    gradient(0)
    begin1(0)
    gradient(1)
    begin1(1)
    gradient(2)
    relay1(0)
    begin1(2)
    gradient(3)
    relay1(1)
    begin1(3)
    begin2(0)
    relay1(2)
    begin2(1)
    relay2(0)
    relay1(3)
    begin2(2)
    relay2(1)
    done2(0)
    begin2(3)
    relay2(2)
    done2(1)
    relay2(3)
    done2(2)
    done2(3)
    take(sbuf.at[pl.ds(0, 3)], s_r)
    log_sum = sbuf[0] + sbuf[1] + sbuf[2] + sbuf[3]
    loss_ref[...] = jnp.log(sums[0:1]) - log_sum / sums[1:2]
    take(r3.at[pl.ds(0, 4)], rs3_r.at[2])
    out_ref[:, 0:128] = c3[3, 0] + r3[2] + r3[4]
    out_ref[:, 128:256] = c3[3, 1] + r3[1] + r3[5]

    sent(qbuf.at[pl.ds(0, 18)], q_s)
    sent(encf.at[pl.ds(0, 3)], enc_s)
    sent(sbuf.at[pl.ds(0, 3)], s_s)
    sent(tbuf.at[pl.ds(0, 3)], t_s)

    @pl.when(tm < TM - 1)
    def _():
        id_copy.wait_send()

    @pl.when(core == 0)
    def _():
        sent(normed.at[pl.ds(0, 4)], n_s)
        sent(pbuf.at[pl.ds(0, 6)], p_s)

    @pl.when(core == 1)
    def _():
        sent(normed.at[pl.ds(0, 5)], n_s)
        sent(pbuf.at[pl.ds(0, 3)], p_s)

    @pl.when((fq == NF - 1) & (tm < TM - 1))
    def _():
        sent(pbuf.at[pl.ds(0, 4)], h_s)

    sent(tmpl.at[pl.ds(0, BINS)], rs1_s)
    sent(grow, rs2_s)
    sent(pbuf.at[pl.ds(0, 3)], rs3_s)


def hand_over(loss_in, grad_in, loss_ref, grad_ref):
    loss_ref[...] = loss_in[...].reshape(FRAMES)
    grad_ref[...] = grad_in[...]


def on_device(
    spectrum, decay_rate, init_state, clip_ids, encoder, gauss_noise, uniform_noise, boost_count, templates,
):
    vmem = pl.BlockSpec(memory_space=pltpu.VMEM)
    hbm = pl.BlockSpec(memory_space=pl.ANY)
    V = pltpu.VMEM
    dma = pltpu.SemaphoreType.DMA
    loss, grad = pl.pallas_call(
        kernel,
        out_shape=(
            jax.ShapeDtypeStruct((1, FRAMES), f32),
            jax.ShapeDtypeStruct((K * L // TM, BINS), f32),
        ),
        in_specs=[vmem] * 4 + [hbm] * 5,
        out_specs=(vmem, vmem),
        scratch_shapes=[
            V((BINS, FRAMES), bf16), V((BINS + 16, K * L), bf16), V((2, K, 128), f32), V((2, 2, K, 128), f32), V((NF, K, BINS), bf16),
            V((BINS, FRAMES), f32), V((BINS, FRAMES), f32), V((TILES, BINS, 128), bf16),
            V((2, NF, BINS, 128), bf16), V((TILES + 1, K, 128), bf16), V((TILES + 1, K, 128), f32),
            V((1, 128), jnp.int32), V((1, 128), jnp.int32), V((20, 1, BINS), f32), V((K * L, FRAMES), bf16),
            V((NF, 1, K * L + FRAMES), f32), V((2, FRAMES), f32), V((NF, 1, FRAMES), f32), V((BINS, FRAMES), bf16),
            V((4, 2, 4, 4, 64, 128), f32), V((4, 2, 6, 2, 64, 128), bf16), V((4, 2, 4, 64, 128), f32),
            V((4, 2, 64, 128), f32), V((4, 2, 6, 2, 64, 128), bf16), V((4, 2, 2, 2, 64, 128), f32), V((4, 2, 6, 32, 128), f32), V((6, 64, 128), f32),
            dma((7,)), dma, dma, dma, dma, dma, dma((2,)), dma, dma, dma, dma((2,)), dma, dma, dma, dma, dma, dma,
            dma, dma((4, 2)), dma, dma((4, 2)), dma, dma((3,)),
        ],
        compiler_params=pltpu.CompilerParams(
            collective_id=0, has_side_effects=True, vmem_limit_bytes=56 * 1024 * 1024),
        name="topic_step",
    )(
        decay_rate.reshape(1, BINS), init_state.reshape(1, BINS), clip_ids,
        boost_count.reshape(1, K), spectrum, encoder, gauss_noise, uniform_noise, templates,
    )
    return pl.pallas_call(
        hand_over,
        out_shape=(jax.ShapeDtypeStruct((FRAMES,), f32), jax.ShapeDtypeStruct((K * L // TM, BINS), f32)),
        in_specs=[vmem] * 2,
        out_specs=(vmem, vmem),
        name="hand_over",
    )(loss, grad)


def solution(mesh):
    placed = (
        P("freq", "tm"), P("freq"), P("freq"), P("tm"), P(None, "freq"), P(None, "tm"),
        P(None, None, "tm"), P(), P("freq", None),
    )
    return jax.shard_map(
        on_device, mesh=mesh, in_specs=placed, out_specs=(P("tm"), P("tm", "freq")), check_vma=False
    )
```

```python
import jax
import jax.numpy as jnp
from jax import lax
from jax.experimental import pallas as pl
from jax.experimental.pallas import tpu as pltpu
from jax.sharding import PartitionSpec as P

F = 1024
K = 256
L = 16
TIME = 49152
BINS = 256
FRAMES = 768
TILES = 6
TM = 64
NF = 4
MESH = pl.DeviceIdType.MESH
f32 = jnp.float32
bf16 = jnp.bfloat16
LOG_GAIN = 0.22314355131420976
OWNER = (0, 0, 1, 2, 2, 3)
SLOT = (0, 1, 0, 0, 1, 0)
ORDER = (2, 1, 3, 0)


def remote(src, dst, send, recv, tm, fq):
    return pltpu.make_async_remote_copy(
        src_ref=src, dst_ref=dst, send_sem=send, recv_sem=recv,
        device_id={"tm": tm, "freq": fq}, device_id_type=MESH,
    )


def take(ref, sem):
    remote(ref, ref, sem, sem, 0, 0).wait_recv()


def sent(ref, sem):
    remote(ref, ref, sem, sem, 0, 0).wait_send()


def kernel(
    decay_ref, init_ref, ids_ref, boost_ref, spec_hbm, enc_hbm, gauss_hbm, unif_hbm, tmpl_hbm,
    loss_ref, out_ref,
    spec_ref, tmpl, gbuf, ubuf, encf, grow, cum, normed, nbuf, pbuf, pf, hsend, hbuf, idsend, idh, qbuf, st,
    tbuf, sums, sbuf, rat, grad, w1, a1, c3, r1, r1f, r2, r3,
    load_sem, t_s, t_r, enc_s, enc_r, q_s, q_r, id_s, id_r, n_s, n_r, p_s, p_r, h_s, h_r, s_s, s_r,
    rs1_s, rs1_r, rs2_s, rs2_r, rs3_s, rs3_r,
):
    tm = lax.axis_index("tm")
    fq = lax.axis_index("freq")
    core = lax.rem(fq, 2)
    zlo = fq // 2
    mate = fq + 1 - 2 * core
    cross = lax.rem(fq + 2, NF)
    barrier = pltpu.get_barrier_semaphore()
    nxt = lax.rem(tm + 1, TM)

    px = lax.rem(tm, 4)
    py = lax.rem(tm // 4, 4)
    pz = tm // 16

    def along(axis, step):
        if axis == 0:
            return tm - px + lax.rem(px + step, 4)
        if axis == 1:
            return tm - 4 * py + 4 * lax.rem(py + step, 4)
        return tm - 16 * pz + 16 * lax.rem(pz + step, 4)

    pxy = lax.rem(tm, 16)

    def in_plane(step):
        return tm - pxy + lax.rem(pxy + step, 16)

    peers = [(in_plane(step), fq) for step in range(1, 16)] + [(along(2, step), fq) for step in range(1, 4)]
    peers += [(tm, lax.rem(fq + i, NF)) for i in range(1, NF)]
    for place, other in peers:
        pl.semaphore_signal(
            barrier, inc=1, device_id={"tm": place, "freq": other}, device_id_type=MESH)

    load_x = pltpu.make_async_copy(spec_hbm, spec_ref, load_sem.at[5])
    load_x.start()
    load_e = pltpu.make_async_copy(enc_hbm, encf.at[fq], load_sem.at[6])
    load_e.start()
    first = zlo * 3 + core * 2
    load_t = pltpu.make_async_copy(tmpl_hbm, tmpl.at[pl.ds(0, BINS)], load_sem.at[0])

    def tile_loads(slot):
        cols = pl.ds(pl.multiple_of((first + slot) * 128, 128), 128)
        return (
            pltpu.make_async_copy(gauss_hbm.at[:, cols], gbuf.at[slot], load_sem.at[1 + 2 * slot]),
            pltpu.make_async_copy(unif_hbm.at[:, :, cols], ubuf.at[slot], load_sem.at[2 + 2 * slot]),
        )

    for copy in tile_loads(0):
        copy.start()

    @pl.when(core == 0)
    def _():
        for copy in tile_loads(1):
            copy.start()

    load_t.start()

    rows = lax.broadcasted_iota(jnp.int32, (BINS, BINS), 0)
    cols = lax.broadcasted_iota(jnp.int32, (BINS, BINS), 1)
    eye = rows == cols
    tri = (rows <= cols).astype(bf16)

    def column(row):
        return jnp.sum(jnp.where(eye, jnp.broadcast_to(row, (BINS, BINS)), 0.0), axis=1, keepdims=True)

    def row_of(col):
        return jnp.sum(jnp.where(eye, jnp.broadcast_to(col, (BINS, BINS)), 0.0), axis=0, keepdims=True)

    decay_row = decay_ref[...]
    lost = 1.0 - (1.0 - decay_row)
    log_row = -lost * (1.0 + lost * (1 / 2 + lost * (1 / 3 + lost * (1 / 4 + lost * (1 / 5 + lost * (1 / 6))))))
    log_col = column(log_row)
    decay_col = column(decay_row)
    ids_row = ids_ref[...].reshape(1, FRAMES)
    ids = ids_row.astype(f32)
    idsend[...] = ids_row[:, FRAMES - 128:]
    lift = jnp.exp(ids * LOG_GAIN)
    load_x.wait()
    carry = jnp.zeros((BINS, 1), f32)
    for b in range(3):
        span = slice(b * 256, b * 256 + 256)
        steps = (cols + (b * 256 + 1)).astype(f32)
        power = steps * log_col
        grow[:, span] = jnp.exp(power)
        v = decay_col * (spec_ref[:, span].astype(f32) * lift[:, span]) * jnp.exp(-power)
        hi = v.astype(bf16)
        rest = v - hi.astype(f32)
        mid = rest.astype(bf16)
        low = (rest - mid.astype(f32)).astype(bf16)
        c = (
            jnp.dot(hi, tri, preferred_element_type=f32)
            + jnp.dot(mid, tri, preferred_element_type=f32)
            + jnp.dot(low, tri, preferred_element_type=f32)
        ) + carry
        cum[:, span] = c
        carry = c[:, 255:256]
    q_col = carry * jnp.exp(log_col * float(FRAMES))
    positions = (px, py, pz)

    def q_send(stage, row):
        pos, count, place = ((pxy, 16, in_plane), (pz, 4, lambda step: along(2, step)))[stage]
        slot = qbuf.at[16 * stage + pos]
        slot[...] = row
        for step in range(1, count):
            remote(slot, slot, q_s, q_r.at[stage], place(step), fq).start()

    def q_take(stage, jump):
        pos, count = ((pxy, 16), (pz, 4))[stage]
        take(qbuf.at[pl.ds(0, count - 1)], q_r.at[stage])
        ahead = jnp.zeros((1, BINS), f32)
        total = jnp.zeros((1, BINS), f32)
        for j in range(count):
            row = qbuf[16 * stage + j]
            ahead = jnp.where(j < pos, jump * ahead + row, ahead)
            total = jump * total + row
        return ahead, total

    q_row = row_of(q_col)
    pl.semaphore_wait(barrier, len(peers))
    q_send(0, q_row)

    load_e.wait()
    remote(encf.at[fq], encf.at[fq], enc_s, enc_r.at[0], tm, cross).start()
    remote(encf.at[fq], encf.at[fq], enc_s, enc_r.at[1], tm, mate).start()

    load_t.wait()
    ones = jnp.ones((8, BINS), bf16)
    tbuf[fq, :, 0:K * L] = jnp.dot(ones, tmpl[0:BINS, :], preferred_element_type=f32)[0:1]
    tbuf[fq, :, K * L:] = jnp.dot(ones, spec_ref[...], preferred_element_type=f32)[0:1]
    for i in range(1, NF):
        remote(tbuf.at[fq], tbuf.at[fq], t_s, t_r, tm, lax.rem(fq + i, NF)).start()

    boost = column(boost_ref[...].astype(f32))

    def ready_noise(slot):
        for copy in tile_loads(slot):
            copy.wait()
        ubuf[slot] = jnp.log(ubuf[slot])

    ready_noise(0)

    @pl.when(core == 0)
    def _():
        ready_noise(1)

    near, total = q_take(0, jnp.exp(log_row * float(FRAMES)))
    q_send(1, total)
    take(encf.at[0], enc_r.at[0])
    remote(encf.at[cross], encf.at[cross], enc_s, enc_r.at[1], tm, mate).start()
    take(tbuf.at[pl.ds(0, 3)], t_r)
    whole = tbuf[0] + tbuf[1] + tbuf[2] + tbuf[3]
    sums[1:2] = whole[:, K * L:]
    whole = whole[:, 0:K * L]
    hi = whole.astype(bf16).astype(f32)
    mid = (whole - hi).astype(bf16).astype(f32)
    low = whole - hi - mid
    place = lax.broadcasted_iota(jnp.int32, (16, K * L), 0)
    tmpl[BINS:, :] = jnp.where(
        place == 0, hi, jnp.where(place == 1, mid, jnp.where(place == 2, low, 0.0))).astype(bf16)
    far, total = q_take(1, jnp.exp(log_row * float(16 * FRAMES)))
    entry = near + jnp.exp(log_row * (float(FRAMES) * pxy.astype(f32))) * (
        far + jnp.exp(log_row * (float(16 * FRAMES) * pz.astype(f32))) * init_ref[...])
    id_copy = remote(idsend, idh, id_s, id_r, nxt, fq)

    @pl.when(tm < TM - 1)
    def _():
        id_copy.start()

    entry_col = column(entry)
    for t in range(TILES):
        span = slice(t * 128, t * 128 + 128)
        drop = jnp.exp(ids[:, span] * (-LOG_GAIN))
        smooth = grow[:, span] * (entry_col + cum[:, span]) * drop
        normed[t] = (spec_ref[:, span].astype(f32) * lax.rsqrt(smooth + 0.1)).astype(bf16)

    def n_copy(t):
        return remote(
            normed.at[t], nbuf.at[SLOT[t], fq], n_s, n_r.at[SLOT[t]], tm, OWNER[t])

    for t in (3, 4, 5, 0, 1, 2):
        @pl.when(fq != OWNER[t])
        def _(t=t):
            n_copy(t).start()

        @pl.when(fq == OWNER[t])
        def _(t=t):
            nbuf[SLOT[t], fq] = normed[t]

    take(encf.at[pl.ds(0, 2)], enc_r.at[1])

    def p_copy(t, sem, to):
        return remote(pbuf.at[1 + t], pbuf.at[1 + t], p_s, p_r.at[sem], tm, to)

    def halo_copy(q):
        return remote(hsend, hbuf, h_s, h_r, nxt, q)

    def sample(slot):
        take(nbuf.at[slot, pl.ds(0, 3)], n_r.at[slot])
        logits = jnp.dot(encf[0], nbuf[slot, 0], preferred_element_type=f32)
        for q in range(1, NF):
            logits += jnp.dot(encf[q], nbuf[slot, q], preferred_element_type=f32)
        conc = jnp.maximum(logits, 0.0) + jnp.log(1.0 + jnp.exp(-jnp.abs(logits))) + 0.5
        offset = conc + boost - 1.0 / 3.0
        linear = 1.0 + lax.rsqrt(9.0 * offset) * gbuf[slot]
        second = jnp.where(boost >= 1.5, ubuf[slot, 1], 0.0)
        power = ubuf[slot, 0] / conc + second / (conc + 1.0)
        draw = offset * linear * linear * linear * jnp.exp(power)
        total = jnp.sum(draw, axis=0, keepdims=True)
        pbuf[1 + first + slot] = (draw / total).astype(bf16)

    def spread(slot):
        p_copy(first + slot, slot, cross).start()
        p_copy(first + slot, 2, mate).start()

    def forward(slot):
        take(pbuf.at[0], p_r.at[slot])
        p_copy((1 - zlo) * 3 + core * 2 + slot, 2, mate).start()

    sample(0)
    spread(0)

    @pl.when((fq == NF - 1) & (tm < TM - 1))
    def _():
        hsend[...] = jnp.transpose(pbuf[TILES].astype(f32))[128 - L:].astype(bf16)
        for q in range(NF):
            halo_copy(q).start()

    @pl.when(core == 0)
    def _():
        sample(1)
        spread(1)

    forward(0)

    @pl.when(core == 0)
    def _():
        forward(1)

    @pl.when(tm == 0)
    def _():
        hbuf[...] = jnp.zeros((L, K), bf16)
        idh[...] = jnp.full((1, 128), -1, jnp.int32)

    @pl.when(tm > 0)
    def _():
        id_copy.wait_recv()
        halo_copy(0).wait_recv()

    @pl.when(core == 0)
    def _():
        take(pbuf.at[pl.ds(0, 2)], p_r.at[2])

    @pl.when(core == 1)
    def _():
        take(pbuf.at[pl.ds(0, 4)], p_r.at[2])

    lane = lax.broadcasted_iota(jnp.int32, (L, 128), 1)
    lag = lax.broadcasted_iota(jnp.int32, (L, 128), 0)
    head = lane < lag

    def lagged(row):
        return pltpu.roll(jnp.broadcast_to(row, (L, 128)), 0, 1, stride=1, stride_axis=0)

    id_rows = [idh[...].astype(f32)] + [ids[:, t * 128:t * 128 + 128] for t in range(TILES)]
    rolled = [lagged(r) for r in id_rows]
    keep = []
    for t in range(TILES):
        source = jnp.where(head, rolled[t], rolled[t + 1])
        keep.append(source == jnp.broadcast_to(id_rows[t + 1], (L, 128)))

    pf[0] = jnp.transpose(jnp.concatenate([jnp.zeros((128 - L, K), f32), hbuf[...].astype(f32)], axis=0))
    for t in range(1, TILES + 1):
        pf[t] = pbuf[t].astype(f32)

    def build_row(k, carry):
        prior = lagged(pf[0, pl.ds(k, 1), :])
        for t in range(TILES):
            current = lagged(pf[t + 1, pl.ds(k, 1), :])
            value = jnp.where(keep[t], jnp.where(head, prior, current), 0.0)
            st[pl.ds(pl.multiple_of(k * L, L), L), t * 128:t * 128 + 128] = value.astype(bf16)
            prior = current
        return carry

    lax.fori_loop(0, K, build_row, 0, unroll=16)

    scale = F * K / TIME
    for b in range(3):
        span = slice(b * 256, b * 256 + 256)
        rec = jnp.dot(tmpl[...], st[:, span], preferred_element_type=f32)
        recon_sum = rec[BINS:BINS + 1] + rec[BINS + 1:BINS + 2] + rec[BINS + 2:BINS + 3]
        rec = rec[0:BINS]
        x = spec_ref[:, span].astype(f32)
        rat[:, span] = (scale / recon_sum - (scale / sums[1:2, span]) * (x / rec)).astype(bf16)
        sums[0:1, span] = recon_sum
        sbuf[fq, :, span] = jnp.sum(x * jnp.log(rec), axis=0, keepdims=True)

    def s_copy(i):
        return remote(sbuf.at[fq], sbuf.at[fq], s_s, s_r, tm, lax.rem(fq + i, NF))

    for i in range(1, NF):
        s_copy(i).start()

    def gradient(n):
        z = lax.rem(pz + ORDER[n], 4)
        g = lax.dot_general(
            st[pl.ds(pl.multiple_of(z * 1024, 1024), 1024), :], rat[...],
            (((1,), (1,)), ((), ())), preferred_element_type=f32).reshape(4, 4, 64, 256)
        grad[n, 0] = g[..., 0:128]
        grad[n, 1] = g[..., 128:256]

    class Ring:
        def __init__(self, view, buf, send, recv, axis, staged=None):
            self.view, self.buf, self.send, self.recv, self.staged = view, buf, send, recv, staged
            self.pos = positions[axis]
            to = (along(axis, 1), along(axis, 3))
            far, right, left = (lax.rem(self.pos + i, 4) for i in (2, 1, 3))
            self.parts = (
                (far, 0, to[0]), (right, 1, to[0]), (right, 0, to[0]),
                (far, 1, to[1]), (left, 0, to[1]), (left, 1, to[1]),
            )

        def copy(self, n):
            d, h, to = self.parts[n]
            src = self.view(d, h) if self.staged is None or n % 3 == 2 else self.staged.at[n]
            return remote(src, self.buf(n), self.send, self.recv.at[0 if n % 3 == 0 else 1], to, fq)

        def push(self, n, more=None):
            view = self.view(self.parts[n][0], self.parts[n][1])
            if more is not None:
                view[...] = view[...] + self.buf(more)[...].astype(f32)
            elif self.staged is not None:
                self.staged[n] = view[...].astype(self.staged.dtype)
            self.copy(n).start()

        def begin(self):
            for n in (0, 3, 1, 4):
                self.push(n)

        def relay(self):
            for n in (0, 3):
                self.push(n + 2, n)

        def result(self):
            return tuple(
                self.view(self.pos, h)[...] + self.buf(l)[...].astype(f32) + self.buf(r)[...].astype(f32)
                for h, l, r in ((0, 2, 4), (1, 1, 5)))

    def landing(n, c):
        return lambda i: r1f.at[n, c, i // 3] if i % 3 == 2 else r1.at[n, c, i]

    s1 = [[
        Ring(lambda d, h, n=n: grad.at[n, 0, pl.ds(2 * h, 2), d], landing(n, 0), rs1_s, rs1_r.at[n], 0, w1.at[n, 0]),
        Ring(lambda d, h, n=n: grad.at[n, 1, d, pl.ds(2 * h, 2)], landing(n, 1), rs1_s, rs1_r.at[n], 1, w1.at[n, 1]),
    ] for n in range(4)]
    s2 = [[
        Ring(lambda d, h, n=n, c=c: a1.at[n, c, d, pl.ds(32 * h, 32)], lambda i, n=n, c=c: r2.at[n, c, i], rs2_s, rs2_r.at[n], 1 - c)
        for c in range(2)] for n in range(4)]
    z_to = (along(2, 1), along(2, 3))

    def z_copy(n):
        piece, half = ((0, 0), (1, 1), (1, 0), (0, 1), (2, 0), (2, 1))[n]
        return remote(c3.at[piece, half], r3.at[n], rs3_s, rs3_r.at[(0, 2, 2, 1, 2, 2)[n]], z_to[n // 3], fq)

    def begin1(n):
        for ring in s1[n]:
            ring.begin()

    def relay1(n):
        take(w1.at[n, 0, pl.ds(0, 4)], rs1_r.at[n, 0])
        for ring in s1[n]:
            ring.relay()

    def begin2(n):
        take(w1.at[n], rs1_r.at[n, 1])
        for c in range(2):
            top, low = s1[n][c].result()
            a1[n, c, 0:2] = top
            a1[n, c, 2:4] = low
            s2[n][c].begin()

    def relay2(n):
        take(r2.at[n, 0, pl.ds(0, 4)], rs2_r.at[n, 0])
        for ring in s2[n]:
            ring.relay()

    def done2(n):
        take(r2.at[n, :, pl.ds(0, 4)], rs2_r.at[n, 1])
        for c in range(2):
            top, low = s2[n][c].result()
            c3[n, c, 0:32] = top
            c3[n, c, 32:64] = low
        if n == 0:
            z_copy(0).start()
            z_copy(3).start()
        elif n < 3:
            half, plain, held = ((1, 1, 0), (0, 4, 3))[n - 1]
            z_copy(plain).start()
            z_copy(held).wait_recv()
            c3[n, 1 - half] = c3[n, 1 - half] + r3[held]
            z_copy((2, 5)[n - 1]).start()

    gradient(0)
    begin1(0)
    gradient(1)
    begin1(1)
    gradient(2)
    relay1(0)
    begin1(2)
    gradient(3)
    relay1(1)
    begin1(3)
    begin2(0)
    relay1(2)
    begin2(1)
    relay2(0)
    relay1(3)
    begin2(2)
    relay2(1)
    done2(0)
    begin2(3)
    relay2(2)
    done2(1)
    relay2(3)
    done2(2)
    done2(3)
    take(sbuf.at[pl.ds(0, 3)], s_r)
    log_sum = sbuf[0] + sbuf[1] + sbuf[2] + sbuf[3]
    loss_ref[...] = jnp.log(sums[0:1]) - log_sum / sums[1:2]
    take(r3.at[pl.ds(0, 4)], rs3_r.at[2])
    out_ref[:, 0:128] = c3[3, 0] + r3[2] + r3[4]
    out_ref[:, 128:256] = c3[3, 1] + r3[1] + r3[5]

    sent(qbuf.at[pl.ds(0, 18)], q_s)
    sent(encf.at[pl.ds(0, 3)], enc_s)
    sent(sbuf.at[pl.ds(0, 3)], s_s)
    sent(tbuf.at[pl.ds(0, 3)], t_s)

    @pl.when(tm < TM - 1)
    def _():
        id_copy.wait_send()

    @pl.when(core == 0)
    def _():
        sent(normed.at[pl.ds(0, 4)], n_s)
        sent(pbuf.at[pl.ds(0, 6)], p_s)

    @pl.when(core == 1)
    def _():
        sent(normed.at[pl.ds(0, 5)], n_s)
        sent(pbuf.at[pl.ds(0, 3)], p_s)

    @pl.when((fq == NF - 1) & (tm < TM - 1))
    def _():
        sent(encf.at[0, pl.ds(0, 64)], h_s)

    sent(tmpl.at[pl.ds(0, BINS)], rs1_s)
    sent(grow, rs2_s)
    sent(pbuf.at[pl.ds(0, 3)], rs3_s)


def hand_over(loss_in, grad_in, loss_ref, grad_ref):
    loss_ref[...] = loss_in[...].reshape(FRAMES)
    grad_ref[...] = grad_in[...]


def on_device(
    spectrum, decay_rate, init_state, clip_ids, encoder, gauss_noise, uniform_noise, boost_count, templates,
):
    vmem = pl.BlockSpec(memory_space=pltpu.VMEM)
    hbm = pl.BlockSpec(memory_space=pl.ANY)
    V = pltpu.VMEM
    dma = pltpu.SemaphoreType.DMA
    loss, grad = pl.pallas_call(
        kernel,
        out_shape=(
            jax.ShapeDtypeStruct((1, FRAMES), f32),
            jax.ShapeDtypeStruct((K * L // TM, BINS), f32),
        ),
        in_specs=[vmem] * 4 + [hbm] * 5,
        out_specs=(vmem, vmem),
        scratch_shapes=[
            V((BINS, FRAMES), bf16), V((BINS + 16, K * L), bf16), V((2, K, 128), f32), V((2, 2, K, 128), f32), V((NF, K, BINS), bf16),
            V((BINS, FRAMES), f32), V((BINS, FRAMES), f32), V((TILES, BINS, 128), bf16),
            V((2, NF, BINS, 128), bf16), V((TILES + 1, K, 128), bf16), V((TILES + 1, K, 128), f32),
            V((L, K), bf16), V((L, K), bf16), V((1, 128), jnp.int32), V((1, 128), jnp.int32), V((20, 1, BINS), f32), V((K * L, FRAMES), bf16),
            V((NF, 1, K * L + FRAMES), f32), V((2, FRAMES), f32), V((NF, 1, FRAMES), f32), V((BINS, FRAMES), bf16),
            V((4, 2, 4, 4, 64, 128), f32), V((4, 2, 6, 2, 64, 128), bf16), V((4, 2, 4, 64, 128), f32),
            V((4, 2, 64, 128), f32), V((4, 2, 6, 2, 64, 128), bf16), V((4, 2, 2, 2, 64, 128), f32), V((4, 2, 6, 32, 128), f32), V((6, 64, 128), f32),
            dma((7,)), dma, dma, dma, dma((2,)), dma, dma((2,)), dma, dma, dma, dma((2,)), dma, dma((3,)), dma, dma, dma, dma,
            dma, dma((4, 2)), dma, dma((4, 2)), dma, dma((3,)),
        ],
        compiler_params=pltpu.CompilerParams(
            collective_id=0, has_side_effects=True, vmem_limit_bytes=56 * 1024 * 1024),
        name="topic_step",
    )(
        decay_rate.reshape(1, BINS), init_state.reshape(1, BINS), clip_ids,
        boost_count.reshape(1, K), spectrum, encoder, gauss_noise, uniform_noise, templates,
    )
    return pl.pallas_call(
        hand_over,
        out_shape=(jax.ShapeDtypeStruct((FRAMES,), f32), jax.ShapeDtypeStruct((K * L // TM, BINS), f32)),
        in_specs=[vmem] * 2,
        out_specs=(vmem, vmem),
        name="hand_over",
    )(loss, grad)


def solution(mesh):
    placed = (
        P("freq", "tm"), P("freq"), P("freq"), P("tm"), P(None, "freq"), P(None, "tm"),
        P(None, None, "tm"), P(), P("freq", None),
    )
    return jax.shard_map(
        on_device, mesh=mesh, in_specs=placed, out_specs=(P("tm"), P("tm", "freq")), check_vma=False
    )
```

```python
import jax
import jax.numpy as jnp
from jax import lax
from jax.experimental import pallas as pl
from jax.experimental.pallas import tpu as pltpu
from jax.sharding import PartitionSpec as P

F = 1024
K = 256
L = 16
TIME = 49152
BINS = 256
FRAMES = 768
TILES = 6
TM = 64
NF = 4
MESH = pl.DeviceIdType.MESH
f32 = jnp.float32
bf16 = jnp.bfloat16
LOG_GAIN = 0.22314355131420976
ORDER = (2, 1, 3, 0)


def remote(src, dst, send, recv, tm, fq):
    return pltpu.make_async_remote_copy(
        src_ref=src, dst_ref=dst, send_sem=send, recv_sem=recv,
        device_id={"tm": tm, "freq": fq}, device_id_type=MESH,
    )


def take(ref, sem):
    remote(ref, ref, sem, sem, 0, 0).wait_recv()


def sent(ref, sem):
    remote(ref, ref, sem, sem, 0, 0).wait_send()


def kernel(
    decay_ref, init_ref, ids_ref, boost_ref, spec_hbm, enc_hbm, gauss_hbm, unif_hbm, tmpl_hbm,
    loss_ref, out_ref,
    spec_ref, tmpl, gbuf, ubuf, encf, grow, cum, normed, nbuf, pbuf, pf, hsend, hbuf, idsend, idh, qbuf, st,
    tbuf, sums, sbuf, rat, grad, w1, a1, c3, r1, r1f, r2, r3,
    load_sem, t_s, t_r, enc_s, enc_r, q_s, q_r, id_s, id_r, n_s, n_r, p_s, p_r, h_s, h_r, s_s, s_r,
    rs1_s, rs1_r, rs2_s, rs2_r, rs3_s, rs3_r,
):
    tm = lax.axis_index("tm")
    fq = lax.axis_index("freq")
    core = lax.rem(fq, 2)
    zlo = fq // 2
    mate = fq + 1 - 2 * core
    cross = lax.rem(fq + 2, NF)
    barrier = pltpu.get_barrier_semaphore()
    nxt = lax.rem(tm + 1, TM)

    px = lax.rem(tm, 4)
    py = lax.rem(tm // 4, 4)
    pz = tm // 16

    def along(axis, step):
        if axis == 0:
            return tm - px + lax.rem(px + step, 4)
        if axis == 1:
            return tm - 4 * py + 4 * lax.rem(py + step, 4)
        return tm - 16 * pz + 16 * lax.rem(pz + step, 4)

    pxy = lax.rem(tm, 16)

    def in_plane(step):
        return tm - pxy + lax.rem(pxy + step, 16)

    peers = [(in_plane(step), fq) for step in range(1, 16)] + [(along(2, step), fq) for step in range(1, 4)]
    peers += [(tm, lax.rem(fq + i, NF)) for i in range(1, NF)]
    for place, other in peers:
        pl.semaphore_signal(
            barrier, inc=1, device_id={"tm": place, "freq": other}, device_id_type=MESH)

    load_x = pltpu.make_async_copy(spec_hbm, spec_ref, load_sem.at[5])
    load_x.start()
    load_e = pltpu.make_async_copy(enc_hbm, encf.at[fq], load_sem.at[6])
    load_e.start()
    first = zlo * 3 + core * 2
    load_t = pltpu.make_async_copy(tmpl_hbm, tmpl.at[pl.ds(0, BINS)], load_sem.at[0])

    def tile_loads(slot):
        cols = pl.ds(pl.multiple_of((first + slot) * 128, 128), 128)
        return (
            pltpu.make_async_copy(gauss_hbm.at[:, cols], gbuf.at[slot], load_sem.at[1 + 2 * slot]),
            pltpu.make_async_copy(unif_hbm.at[:, :, cols], ubuf.at[slot], load_sem.at[2 + 2 * slot]),
        )

    for copy in tile_loads(0):
        copy.start()

    @pl.when(core == 0)
    def _():
        for copy in tile_loads(1):
            copy.start()

    load_t.start()

    rows = lax.broadcasted_iota(jnp.int32, (BINS, BINS), 0)
    cols = lax.broadcasted_iota(jnp.int32, (BINS, BINS), 1)
    eye = rows == cols
    tri = (rows <= cols).astype(bf16)

    def column(row):
        return jnp.sum(jnp.where(eye, jnp.broadcast_to(row, (BINS, BINS)), 0.0), axis=1, keepdims=True)

    def row_of(col):
        return jnp.sum(jnp.where(eye, jnp.broadcast_to(col, (BINS, BINS)), 0.0), axis=0, keepdims=True)

    decay_row = decay_ref[...]
    lost = 1.0 - (1.0 - decay_row)
    log_row = -lost * (1.0 + lost * (1 / 2 + lost * (1 / 3 + lost * (1 / 4 + lost * (1 / 5 + lost * (1 / 6))))))
    log_col = column(log_row)
    decay_col = column(decay_row)
    ids_row = ids_ref[...].reshape(1, FRAMES)
    ids = ids_row.astype(f32)
    idsend[...] = ids_row[:, FRAMES - 128:]
    lift = jnp.exp(ids * LOG_GAIN)
    load_x.wait()
    carry = jnp.zeros((BINS, 1), f32)
    for b in range(3):
        span = slice(b * 256, b * 256 + 256)
        steps = (cols + (b * 256 + 1)).astype(f32)
        power = steps * log_col
        grow[:, span] = jnp.exp(power)
        v = decay_col * (spec_ref[:, span].astype(f32) * lift[:, span]) * jnp.exp(-power)
        hi = v.astype(bf16)
        rest = v - hi.astype(f32)
        mid = rest.astype(bf16)
        low = (rest - mid.astype(f32)).astype(bf16)
        c = (
            jnp.dot(hi, tri, preferred_element_type=f32)
            + jnp.dot(mid, tri, preferred_element_type=f32)
            + jnp.dot(low, tri, preferred_element_type=f32)
        ) + carry
        cum[:, span] = c
        carry = c[:, 255:256]
    q_col = carry * jnp.exp(log_col * float(FRAMES))
    positions = (px, py, pz)

    def q_send(stage, row):
        pos, count, place = ((pxy, 16, in_plane), (pz, 4, lambda step: along(2, step)))[stage]
        slot = qbuf.at[16 * stage + pos]
        slot[...] = row
        for step in range(1, count):
            remote(slot, slot, q_s, q_r.at[stage], place(step), fq).start()

    def q_take(stage, jump):
        pos, count = ((pxy, 16), (pz, 4))[stage]
        take(qbuf.at[pl.ds(0, count - 1)], q_r.at[stage])
        ahead = jnp.zeros((1, BINS), f32)
        total = jnp.zeros((1, BINS), f32)
        for j in range(count):
            row = qbuf[16 * stage + j]
            ahead = jnp.where(j < pos, jump * ahead + row, ahead)
            total = jump * total + row
        return ahead, total

    q_row = row_of(q_col)
    pl.semaphore_wait(barrier, len(peers))
    q_send(0, q_row)

    load_e.wait()
    remote(encf.at[fq], encf.at[fq], enc_s, enc_r.at[0], tm, cross).start()
    remote(encf.at[fq], encf.at[fq], enc_s, enc_r.at[1], tm, mate).start()

    load_t.wait()
    ones = jnp.ones((8, BINS), bf16)
    tbuf[fq, :, 0:K * L] = jnp.dot(ones, tmpl[0:BINS, :], preferred_element_type=f32)[0:1]
    tbuf[fq, :, K * L:] = jnp.dot(ones, spec_ref[...], preferred_element_type=f32)[0:1]
    for i in range(1, NF):
        remote(tbuf.at[fq], tbuf.at[fq], t_s, t_r, tm, lax.rem(fq + i, NF)).start()

    boost = column(boost_ref[...].astype(f32))

    def ready_noise(slot):
        for copy in tile_loads(slot):
            copy.wait()
        ubuf[slot] = jnp.log(ubuf[slot])

    ready_noise(0)

    @pl.when(core == 0)
    def _():
        ready_noise(1)

    near, total = q_take(0, jnp.exp(log_row * float(FRAMES)))
    q_send(1, total)
    take(encf.at[0], enc_r.at[0])
    remote(encf.at[cross], encf.at[cross], enc_s, enc_r.at[1], tm, mate).start()
    take(tbuf.at[pl.ds(0, 3)], t_r)
    whole = tbuf[0] + tbuf[1] + tbuf[2] + tbuf[3]
    sums[1:2] = whole[:, K * L:]
    whole = whole[:, 0:K * L]
    hi = whole.astype(bf16).astype(f32)
    mid = (whole - hi).astype(bf16).astype(f32)
    low = whole - hi - mid
    place = lax.broadcasted_iota(jnp.int32, (16, K * L), 0)
    tmpl[BINS:, :] = jnp.where(
        place == 0, hi, jnp.where(place == 1, mid, jnp.where(place == 2, low, 0.0))).astype(bf16)
    far, total = q_take(1, jnp.exp(log_row * float(16 * FRAMES)))
    entry = near + jnp.exp(log_row * (float(FRAMES) * pxy.astype(f32))) * (
        far + jnp.exp(log_row * (float(16 * FRAMES) * pz.astype(f32))) * init_ref[...])
    id_copy = remote(idsend, idh, id_s, id_r, nxt, fq)

    @pl.when(tm < TM - 1)
    def _():
        id_copy.start()

    entry_col = column(entry)
    def normalise(t):
        span = pl.ds(pl.multiple_of(t * 128, 128), 128)
        drop = jnp.exp(ids_ref[span].reshape(1, 128).astype(f32) * (-LOG_GAIN))
        smooth = grow[:, span] * (entry_col + cum[:, span]) * drop
        normed[t] = (spec_ref[:, span].astype(f32) * lax.rsqrt(smooth + 0.1)).astype(bf16)

    def n_copy(t, slot, to):
        return remote(normed.at[t], nbuf.at[slot, fq], n_s, n_r.at[slot], tm, to)

    for r, slot, owner in ((0, 0, 0), (2, 0, 1), (1, 1, 0)):
        t = 3 * (1 - zlo) + r
        normalise(t)
        n_copy(t, slot, 2 * (1 - zlo) + owner).start()
    for r, slot, owner in ((0, 0, 0), (2, 0, 1), (1, 1, 0)):
        t = 3 * zlo + r
        normalise(t)

        @pl.when(core != owner)
        def _(t=t, slot=slot):
            n_copy(t, slot, mate).start()

        @pl.when(core == owner)
        def _(t=t, slot=slot):
            nbuf[slot, fq] = normed[t]

    take(encf.at[pl.ds(0, 2)], enc_r.at[1])

    def p_copy(t, sem, to):
        return remote(pbuf.at[1 + t], pbuf.at[1 + t], p_s, p_r.at[sem], tm, to)

    def halo_copy(q):
        return remote(hsend, hbuf, h_s, h_r, nxt, q)

    def sample(slot):
        take(nbuf.at[slot, pl.ds(0, 3)], n_r.at[slot])
        logits = jnp.dot(encf[0], nbuf[slot, 0], preferred_element_type=f32)
        for q in range(1, NF):
            logits += jnp.dot(encf[q], nbuf[slot, q], preferred_element_type=f32)
        conc = jnp.maximum(logits, 0.0) + jnp.log(1.0 + jnp.exp(-jnp.abs(logits))) + 0.5
        offset = conc + boost - 1.0 / 3.0
        linear = 1.0 + lax.rsqrt(9.0 * offset) * gbuf[slot]
        second = jnp.where(boost >= 1.5, ubuf[slot, 1], 0.0)
        power = ubuf[slot, 0] / conc + second / (conc + 1.0)
        draw = offset * linear * linear * linear * jnp.exp(power)
        total = jnp.sum(draw, axis=0, keepdims=True)
        pbuf[1 + first + slot] = (draw / total).astype(bf16)

    def spread(slot):
        p_copy(first + slot, slot, cross).start()
        p_copy(first + slot, 2, mate).start()

    def forward(slot):
        take(pbuf.at[0], p_r.at[slot])
        p_copy((1 - zlo) * 3 + core * 2 + slot, 2, mate).start()

    sample(0)
    spread(0)

    @pl.when((fq == NF - 1) & (tm < TM - 1))
    def _():
        hsend[...] = jnp.transpose(pbuf[TILES].astype(f32))[128 - L:].astype(bf16)
        for q in range(NF):
            halo_copy(q).start()

    @pl.when(core == 0)
    def _():
        sample(1)
        spread(1)

    forward(0)

    @pl.when(core == 0)
    def _():
        forward(1)

    @pl.when(tm == 0)
    def _():
        hbuf[...] = jnp.zeros((L, K), bf16)
        idh[...] = jnp.full((1, 128), -1, jnp.int32)

    @pl.when(tm > 0)
    def _():
        id_copy.wait_recv()
        halo_copy(0).wait_recv()

    @pl.when(core == 0)
    def _():
        take(pbuf.at[pl.ds(0, 2)], p_r.at[2])

    @pl.when(core == 1)
    def _():
        take(pbuf.at[pl.ds(0, 4)], p_r.at[2])

    lane = lax.broadcasted_iota(jnp.int32, (L, 128), 1)
    lag = lax.broadcasted_iota(jnp.int32, (L, 128), 0)
    head = lane < lag

    def lagged(row):
        return pltpu.roll(jnp.broadcast_to(row, (L, 128)), 0, 1, stride=1, stride_axis=0)

    id_rows = [idh[...].astype(f32)] + [ids[:, t * 128:t * 128 + 128] for t in range(TILES)]
    rolled = [lagged(r) for r in id_rows]
    keep = []
    for t in range(TILES):
        source = jnp.where(head, rolled[t], rolled[t + 1])
        keep.append(source == jnp.broadcast_to(id_rows[t + 1], (L, 128)))

    pf[0] = jnp.transpose(jnp.concatenate([jnp.zeros((128 - L, K), f32), hbuf[...].astype(f32)], axis=0))
    for t in range(1, TILES + 1):
        pf[t] = pbuf[t].astype(f32)

    def build_row(k, carry):
        prior = lagged(pf[0, pl.ds(k, 1), :])
        for t in range(TILES):
            current = lagged(pf[t + 1, pl.ds(k, 1), :])
            value = jnp.where(keep[t], jnp.where(head, prior, current), 0.0)
            st[pl.ds(pl.multiple_of(k * L, L), L), t * 128:t * 128 + 128] = value.astype(bf16)
            prior = current
        return carry

    lax.fori_loop(0, K, build_row, 0, unroll=16)

    scale = F * K / TIME
    for b in range(3):
        span = slice(b * 256, b * 256 + 256)
        rec = jnp.dot(tmpl[...], st[:, span], preferred_element_type=f32)
        recon_sum = rec[BINS:BINS + 1] + rec[BINS + 1:BINS + 2] + rec[BINS + 2:BINS + 3]
        rec = rec[0:BINS]
        x = spec_ref[:, span].astype(f32)
        rat[:, span] = (scale / recon_sum - (scale / sums[1:2, span]) * (x / rec)).astype(bf16)
        sums[0:1, span] = recon_sum
        sbuf[fq, :, span] = jnp.sum(x * jnp.log(rec), axis=0, keepdims=True)

    def s_copy(i):
        return remote(sbuf.at[fq], sbuf.at[fq], s_s, s_r, tm, lax.rem(fq + i, NF))

    for i in range(1, NF):
        s_copy(i).start()

    def gradient(n):
        z = lax.rem(pz + ORDER[n], 4)
        g = lax.dot_general(
            st[pl.ds(pl.multiple_of(z * 1024, 1024), 1024), :], rat[...],
            (((1,), (1,)), ((), ())), preferred_element_type=f32).reshape(4, 4, 64, 256)
        grad[n, 0] = g[..., 0:128]
        grad[n, 1] = g[..., 128:256]

    class Ring:
        def __init__(self, view, buf, send, recv, axis, staged=None):
            self.view, self.buf, self.send, self.recv, self.staged = view, buf, send, recv, staged
            self.pos = positions[axis]
            to = (along(axis, 1), along(axis, 3))
            far, right, left = (lax.rem(self.pos + i, 4) for i in (2, 1, 3))
            self.parts = (
                (far, 0, to[0]), (right, 1, to[0]), (right, 0, to[0]),
                (far, 1, to[1]), (left, 0, to[1]), (left, 1, to[1]),
            )

        def copy(self, n):
            d, h, to = self.parts[n]
            src = self.view(d, h) if self.staged is None or n % 3 == 2 else self.staged.at[n]
            return remote(src, self.buf(n), self.send, self.recv.at[0 if n % 3 == 0 else 1], to, fq)

        def push(self, n, more=None):
            view = self.view(self.parts[n][0], self.parts[n][1])
            if more is not None:
                view[...] = view[...] + self.buf(more)[...].astype(f32)
            elif self.staged is not None:
                self.staged[n] = view[...].astype(self.staged.dtype)
            self.copy(n).start()

        def begin(self):
            for n in (0, 3, 1, 4):
                self.push(n)

        def relay(self):
            for n in (0, 3):
                self.push(n + 2, n)

        def result(self):
            return tuple(
                self.view(self.pos, h)[...] + self.buf(l)[...].astype(f32) + self.buf(r)[...].astype(f32)
                for h, l, r in ((0, 2, 4), (1, 1, 5)))

    def landing(n, c):
        return lambda i: r1f.at[n, c, i // 3] if i % 3 == 2 else r1.at[n, c, i]

    s1 = [[
        Ring(lambda d, h, n=n: grad.at[n, 0, pl.ds(2 * h, 2), d], landing(n, 0), rs1_s, rs1_r.at[n], 0, w1.at[n, 0]),
        Ring(lambda d, h, n=n: grad.at[n, 1, d, pl.ds(2 * h, 2)], landing(n, 1), rs1_s, rs1_r.at[n], 1, w1.at[n, 1]),
    ] for n in range(4)]
    s2 = [[
        Ring(lambda d, h, n=n, c=c: a1.at[n, c, d, pl.ds(32 * h, 32)], lambda i, n=n, c=c: r2.at[n, c, i], rs2_s, rs2_r.at[n], 1 - c)
        for c in range(2)] for n in range(4)]
    z_to = (along(2, 1), along(2, 3))

    def z_copy(n):
        piece, half = ((0, 0), (1, 1), (1, 0), (0, 1), (2, 0), (2, 1))[n]
        return remote(c3.at[piece, half], r3.at[n], rs3_s, rs3_r.at[(0, 2, 2, 1, 2, 2)[n]], z_to[n // 3], fq)

    def begin1(n):
        for ring in s1[n]:
            ring.begin()

    def relay1(n):
        take(w1.at[n, 0, pl.ds(0, 4)], rs1_r.at[n, 0])
        for ring in s1[n]:
            ring.relay()

    def begin2(n):
        take(w1.at[n], rs1_r.at[n, 1])
        for c in range(2):
            top, low = s1[n][c].result()
            a1[n, c, 0:2] = top
            a1[n, c, 2:4] = low
            s2[n][c].begin()

    def relay2(n):
        take(r2.at[n, 0, pl.ds(0, 4)], rs2_r.at[n, 0])
        for ring in s2[n]:
            ring.relay()

    def done2(n):
        take(r2.at[n, :, pl.ds(0, 4)], rs2_r.at[n, 1])
        for c in range(2):
            top, low = s2[n][c].result()
            c3[n, c, 0:32] = top
            c3[n, c, 32:64] = low
        if n == 0:
            z_copy(0).start()
            z_copy(3).start()
        elif n < 3:
            half, plain, held = ((1, 1, 0), (0, 4, 3))[n - 1]
            z_copy(plain).start()
            z_copy(held).wait_recv()
            c3[n, 1 - half] = c3[n, 1 - half] + r3[held]
            z_copy((2, 5)[n - 1]).start()

    gradient(0)
    begin1(0)
    gradient(1)
    begin1(1)
    gradient(2)
    relay1(0)
    begin1(2)
    gradient(3)
    relay1(1)
    begin1(3)
    begin2(0)
    relay1(2)
    begin2(1)
    relay2(0)
    relay1(3)
    begin2(2)
    relay2(1)
    done2(0)
    begin2(3)
    relay2(2)
    done2(1)
    relay2(3)
    done2(2)
    done2(3)
    take(sbuf.at[pl.ds(0, 3)], s_r)
    log_sum = sbuf[0] + sbuf[1] + sbuf[2] + sbuf[3]
    loss_ref[...] = jnp.log(sums[0:1]) - log_sum / sums[1:2]
    take(r3.at[pl.ds(0, 4)], rs3_r.at[2])
    out_ref[:, 0:128] = c3[3, 0] + r3[2] + r3[4]
    out_ref[:, 128:256] = c3[3, 1] + r3[1] + r3[5]

    sent(qbuf.at[pl.ds(0, 18)], q_s)
    sent(encf.at[pl.ds(0, 3)], enc_s)
    sent(sbuf.at[pl.ds(0, 3)], s_s)
    sent(tbuf.at[pl.ds(0, 3)], t_s)

    @pl.when(tm < TM - 1)
    def _():
        id_copy.wait_send()

    @pl.when(core == 0)
    def _():
        sent(normed.at[pl.ds(0, 4)], n_s)
        sent(pbuf.at[pl.ds(0, 6)], p_s)

    @pl.when(core == 1)
    def _():
        sent(normed.at[pl.ds(0, 5)], n_s)
        sent(pbuf.at[pl.ds(0, 3)], p_s)

    @pl.when((fq == NF - 1) & (tm < TM - 1))
    def _():
        sent(encf.at[0, pl.ds(0, 64)], h_s)

    sent(tmpl.at[pl.ds(0, BINS)], rs1_s)
    sent(grow, rs2_s)
    sent(pbuf.at[pl.ds(0, 3)], rs3_s)


def hand_over(loss_in, grad_in, loss_ref, grad_ref):
    loss_ref[...] = loss_in[...].reshape(FRAMES)
    grad_ref[...] = grad_in[...]


def on_device(
    spectrum, decay_rate, init_state, clip_ids, encoder, gauss_noise, uniform_noise, boost_count, templates,
):
    vmem = pl.BlockSpec(memory_space=pltpu.VMEM)
    hbm = pl.BlockSpec(memory_space=pl.ANY)
    V = pltpu.VMEM
    dma = pltpu.SemaphoreType.DMA
    loss, grad = pl.pallas_call(
        kernel,
        out_shape=(
            V((1, FRAMES), f32),
            V((K * L // TM, BINS), f32),
        ),
        in_specs=[vmem] * 4 + [hbm] * 5,
        out_specs=(vmem, vmem),
        scratch_shapes=[
            V((BINS, FRAMES), bf16), V((BINS + 16, K * L), bf16), V((2, K, 128), f32), V((2, 2, K, 128), f32), V((NF, K, BINS), bf16),
            V((BINS, FRAMES), f32), V((BINS, FRAMES), f32), V((TILES, BINS, 128), bf16),
            V((2, NF, BINS, 128), bf16), V((TILES + 1, K, 128), bf16), V((TILES + 1, K, 128), f32),
            V((L, K), bf16), V((L, K), bf16), V((1, 128), jnp.int32), V((1, 128), jnp.int32), V((20, 1, BINS), f32), V((K * L, FRAMES), bf16),
            V((NF, 1, K * L + FRAMES), f32), V((2, FRAMES), f32), V((NF, 1, FRAMES), f32), V((BINS, FRAMES), bf16),
            V((4, 2, 4, 4, 64, 128), f32), V((4, 2, 6, 2, 64, 128), bf16), V((4, 2, 4, 64, 128), f32),
            V((4, 2, 64, 128), f32), V((4, 2, 6, 2, 64, 128), bf16), V((4, 2, 2, 2, 64, 128), f32), V((4, 2, 6, 32, 128), f32), V((6, 64, 128), f32),
            dma((7,)), dma, dma, dma, dma((2,)), dma, dma((2,)), dma, dma, dma, dma((2,)), dma, dma((3,)), dma, dma, dma, dma,
            dma, dma((4, 2)), dma, dma((4, 2)), dma, dma((3,)),
        ],
        compiler_params=pltpu.CompilerParams(
            collective_id=0, has_side_effects=True, vmem_limit_bytes=56 * 1024 * 1024),
        name="topic_step",
    )(
        decay_rate.reshape(1, BINS), init_state.reshape(1, BINS), clip_ids,
        boost_count.reshape(1, K), spectrum, encoder, gauss_noise, uniform_noise, templates,
    )
    return pl.pallas_call(
        hand_over,
        out_shape=(jax.ShapeDtypeStruct((FRAMES,), f32), jax.ShapeDtypeStruct((K * L // TM, BINS), f32)),
        in_specs=[vmem] * 2,
        out_specs=(vmem, vmem),
        name="hand_over",
    )(loss, grad)


def solution(mesh):
    placed = (
        P("freq", "tm"), P("freq"), P("freq"), P("tm"), P(None, "freq"), P(None, "tm"),
        P(None, None, "tm"), P(), P("freq", None),
    )
    return jax.shard_map(
        on_device, mesh=mesh, in_specs=placed, out_specs=(P("tm"), P("tm", "freq")), check_vma=False
    )
```

```python
import jax
import jax.numpy as jnp
from jax import lax
from jax.experimental import pallas as pl
from jax.experimental.pallas import tpu as pltpu
from jax.sharding import PartitionSpec as P

F = 1024
K = 256
L = 16
TIME = 49152
BINS = 256
FRAMES = 768
TILES = 6
TM = 64
NF = 4
MESH = pl.DeviceIdType.MESH
f32 = jnp.float32
bf16 = jnp.bfloat16
LOG_GAIN = 0.22314355131420976
FAR_FIRST = (10, 9, 11, 6, 14, 2, 8, 5, 7, 13, 15, 1, 3, 4, 12)
ORDER = (2, 1, 3, 0)


def remote(src, dst, send, recv, tm, fq):
    return pltpu.make_async_remote_copy(
        src_ref=src, dst_ref=dst, send_sem=send, recv_sem=recv,
        device_id={"tm": tm, "freq": fq}, device_id_type=MESH,
    )


def take(ref, sem):
    remote(ref, ref, sem, sem, 0, 0).wait_recv()


def sent(ref, sem):
    remote(ref, ref, sem, sem, 0, 0).wait_send()


def kernel(
    decay_ref, init_ref, ids_ref, boost_ref, spec_hbm, enc_hbm, gauss_hbm, unif_hbm, tmpl_hbm,
    loss_ref, out_ref,
    spec_ref, tmpl, gbuf, ubuf, encf, grow, cum, normed, nbuf, pbuf, pf, hsend, hbuf, idsend, idh, qbuf, st,
    tbuf, sums, sbuf, rat, grad, w1, a1, c3, r1, r1f, r2, r3,
    load_sem, t_s, t_r, enc_s, enc_r, q_s, q_r, id_s, id_r, n_s, n_r, p_s, p_r, h_s, h_r, s_s, s_r,
    rs1_s, rs1_r, rs2_s, rs2_r, rs3_s, rs3_r,
):
    tm = lax.axis_index("tm")
    fq = lax.axis_index("freq")
    core = lax.rem(fq, 2)
    zlo = fq // 2
    mate = fq + 1 - 2 * core
    cross = lax.rem(fq + 2, NF)
    barrier = pltpu.get_barrier_semaphore()
    nxt = lax.rem(tm + 1, TM)

    px = lax.rem(tm, 4)
    py = lax.rem(tm // 4, 4)
    pz = tm // 16

    def along(axis, step):
        if axis == 0:
            return tm - px + lax.rem(px + step, 4)
        if axis == 1:
            return tm - 4 * py + 4 * lax.rem(py + step, 4)
        return tm - 16 * pz + 16 * lax.rem(pz + step, 4)

    pxy = lax.rem(tm, 16)

    def in_plane(step):
        return tm - pxy + lax.rem(pxy + step, 16)

    peers = [(along(2, step), fq) for step in ORDER[:3]] + [(in_plane(step), fq) for step in FAR_FIRST]
    peers += [(tm, lax.rem(fq + i, NF)) for i in range(1, NF)]
    for place, other in peers:
        pl.semaphore_signal(
            barrier, inc=1, device_id={"tm": place, "freq": other}, device_id_type=MESH)

    load_x = pltpu.make_async_copy(spec_hbm, spec_ref, load_sem.at[5])
    load_x.start()
    load_e = pltpu.make_async_copy(enc_hbm, encf.at[fq], load_sem.at[6])
    load_e.start()
    first = zlo * 3 + core * 2
    load_t = pltpu.make_async_copy(tmpl_hbm, tmpl.at[pl.ds(0, BINS)], load_sem.at[0])

    def tile_loads(slot):
        cols = pl.ds(pl.multiple_of((first + slot) * 128, 128), 128)
        return (
            pltpu.make_async_copy(gauss_hbm.at[:, cols], gbuf.at[slot], load_sem.at[1 + 2 * slot]),
            pltpu.make_async_copy(unif_hbm.at[:, :, cols], ubuf.at[slot], load_sem.at[2 + 2 * slot]),
        )

    for copy in tile_loads(0):
        copy.start()

    @pl.when(core == 0)
    def _():
        for copy in tile_loads(1):
            copy.start()

    load_t.start()

    rows = lax.broadcasted_iota(jnp.int32, (BINS, BINS), 0)
    cols = lax.broadcasted_iota(jnp.int32, (BINS, BINS), 1)
    eye = rows == cols
    tri = (rows <= cols).astype(bf16)

    def column(row):
        return jnp.sum(jnp.where(eye, jnp.broadcast_to(row, (BINS, BINS)), 0.0), axis=1, keepdims=True)

    def row_of(col):
        return jnp.sum(jnp.where(eye, jnp.broadcast_to(col, (BINS, BINS)), 0.0), axis=0, keepdims=True)

    decay_row = decay_ref[...]
    lost = 1.0 - (1.0 - decay_row)
    log_row = -lost * (1.0 + lost * (1 / 2 + lost * (1 / 3 + lost * (1 / 4 + lost * (1 / 5 + lost * (1 / 6))))))
    log_col = column(log_row)
    decay_col = column(decay_row)
    ids_row = ids_ref[...].reshape(1, FRAMES)
    ids = ids_row.astype(f32)
    idsend[...] = ids_row[:, FRAMES - 128:]
    lift = jnp.exp(ids * LOG_GAIN)
    load_x.wait()
    carry = jnp.zeros((BINS, 1), f32)
    for b in range(3):
        span = slice(b * 256, b * 256 + 256)
        steps = (cols + (b * 256 + 1)).astype(f32)
        power = steps * log_col
        grow[:, span] = jnp.exp(power)
        v = decay_col * (spec_ref[:, span].astype(f32) * lift[:, span]) * jnp.exp(-power)
        hi = v.astype(bf16)
        rest = v - hi.astype(f32)
        mid = rest.astype(bf16)
        low = (rest - mid.astype(f32)).astype(bf16)
        c = (
            jnp.dot(hi, tri, preferred_element_type=f32)
            + jnp.dot(mid, tri, preferred_element_type=f32)
            + jnp.dot(low, tri, preferred_element_type=f32)
        ) + carry
        cum[:, span] = c
        carry = c[:, 255:256]
    q_col = carry * jnp.exp(log_col * float(FRAMES))
    positions = (px, py, pz)

    def q_send(stage, row):
        pos, steps, place = ((pxy, FAR_FIRST, in_plane), (pz, ORDER[:3], lambda step: along(2, step)))[stage]
        slot = qbuf.at[16 * stage + pos]
        slot[...] = row
        for step in steps:
            remote(slot, slot, q_s, q_r.at[stage], place(step), fq).start()

    def q_take(stage, jump):
        pos, count = ((pxy, 16), (pz, 4))[stage]
        take(qbuf.at[pl.ds(0, count - 1)], q_r.at[stage])
        ahead = jnp.zeros((1, BINS), f32)
        total = jnp.zeros((1, BINS), f32)
        for j in range(count):
            row = qbuf[16 * stage + j]
            ahead = jnp.where(j < pos, jump * ahead + row, ahead)
            total = jump * total + row
        return ahead, total

    q_row = row_of(q_col)
    pl.semaphore_wait(barrier, len(peers))
    q_send(0, q_row)

    load_e.wait()
    remote(encf.at[fq], encf.at[fq], enc_s, enc_r.at[0], tm, cross).start()
    remote(encf.at[fq], encf.at[fq], enc_s, enc_r.at[1], tm, mate).start()

    load_t.wait()
    ones = jnp.ones((8, BINS), bf16)
    tbuf[fq, :, 0:K * L] = jnp.dot(ones, tmpl[0:BINS, :], preferred_element_type=f32)[0:1]
    tbuf[fq, :, K * L:] = jnp.dot(ones, spec_ref[...], preferred_element_type=f32)[0:1]
    for i in range(1, NF):
        remote(tbuf.at[fq], tbuf.at[fq], t_s, t_r, tm, lax.rem(fq + i, NF)).start()

    boost = column(boost_ref[...].astype(f32))

    def ready_noise(slot):
        for copy in tile_loads(slot):
            copy.wait()
        ubuf[slot] = jnp.log(ubuf[slot])

    ready_noise(0)

    @pl.when(core == 0)
    def _():
        ready_noise(1)

    near, total = q_take(0, jnp.exp(log_row * float(FRAMES)))
    q_send(1, total)
    take(encf.at[0], enc_r.at[0])
    remote(encf.at[cross], encf.at[cross], enc_s, enc_r.at[1], tm, mate).start()
    take(tbuf.at[pl.ds(0, 3)], t_r)
    whole = tbuf[0] + tbuf[1] + tbuf[2] + tbuf[3]
    sums[1:2] = whole[:, K * L:]
    whole = whole[:, 0:K * L]
    hi = whole.astype(bf16).astype(f32)
    mid = (whole - hi).astype(bf16).astype(f32)
    low = whole - hi - mid
    place = lax.broadcasted_iota(jnp.int32, (16, K * L), 0)
    tmpl[BINS:, :] = jnp.where(
        place == 0, hi, jnp.where(place == 1, mid, jnp.where(place == 2, low, 0.0))).astype(bf16)
    far, total = q_take(1, jnp.exp(log_row * float(16 * FRAMES)))
    entry = near + jnp.exp(log_row * (float(FRAMES) * pxy.astype(f32))) * (
        far + jnp.exp(log_row * (float(16 * FRAMES) * pz.astype(f32))) * init_ref[...])
    id_copy = remote(idsend, idh, id_s, id_r, nxt, fq)

    @pl.when(tm < TM - 1)
    def _():
        id_copy.start()

    entry_col = column(entry)
    def normalise(t):
        span = pl.ds(pl.multiple_of(t * 128, 128), 128)
        drop = jnp.exp(ids_ref[span].reshape(1, 128).astype(f32) * (-LOG_GAIN))
        smooth = grow[:, span] * (entry_col + cum[:, span]) * drop
        normed[t] = (spec_ref[:, span].astype(f32) * lax.rsqrt(smooth + 0.1)).astype(bf16)

    def n_copy(t, slot, to):
        return remote(normed.at[t], nbuf.at[slot, fq], n_s, n_r.at[slot], tm, to)

    for r, slot, owner in ((0, 0, 0), (2, 0, 1), (1, 1, 0)):
        t = 3 * (1 - zlo) + r
        normalise(t)
        n_copy(t, slot, 2 * (1 - zlo) + owner).start()
    for r, slot, owner in ((0, 0, 0), (2, 0, 1), (1, 1, 0)):
        t = 3 * zlo + r
        normalise(t)

        @pl.when(core != owner)
        def _(t=t, slot=slot):
            n_copy(t, slot, mate).start()

        @pl.when(core == owner)
        def _(t=t, slot=slot):
            nbuf[slot, fq] = normed[t]

    take(encf.at[pl.ds(0, 2)], enc_r.at[1])

    def p_copy(t, sem, to):
        return remote(pbuf.at[1 + t], pbuf.at[1 + t], p_s, p_r.at[sem], tm, to)

    def halo_copy(q):
        return remote(hsend, hbuf, h_s, h_r, nxt, q)

    def sample(slot):
        take(nbuf.at[slot, pl.ds(0, 3)], n_r.at[slot])
        logits = jnp.dot(encf[0], nbuf[slot, 0], preferred_element_type=f32)
        for q in range(1, NF):
            logits += jnp.dot(encf[q], nbuf[slot, q], preferred_element_type=f32)
        conc = jnp.maximum(logits, 0.0) + jnp.log(1.0 + jnp.exp(-jnp.abs(logits))) + 0.5
        offset = conc + boost - 1.0 / 3.0
        linear = 1.0 + lax.rsqrt(9.0 * offset) * gbuf[slot]
        second = jnp.where(boost >= 1.5, ubuf[slot, 1], 0.0)
        power = ubuf[slot, 0] / conc + second / (conc + 1.0)
        draw = offset * linear * linear * linear * jnp.exp(power)
        total = jnp.sum(draw, axis=0, keepdims=True)
        pbuf[1 + first + slot] = (draw / total).astype(bf16)

    def spread(slot):
        p_copy(first + slot, slot, cross).start()
        p_copy(first + slot, 2, mate).start()

    def forward(slot):
        take(pbuf.at[0], p_r.at[slot])
        p_copy((1 - zlo) * 3 + core * 2 + slot, 2, mate).start()

    sample(0)
    spread(0)

    @pl.when((fq == NF - 1) & (tm < TM - 1))
    def _():
        hsend[...] = jnp.transpose(pbuf[TILES].astype(f32))[128 - L:].astype(bf16)
        for q in range(NF):
            halo_copy(q).start()

    @pl.when(core == 0)
    def _():
        sample(1)
        spread(1)

    forward(0)

    @pl.when(core == 0)
    def _():
        forward(1)

    @pl.when(tm == 0)
    def _():
        hbuf[...] = jnp.zeros((L, K), bf16)
        idh[...] = jnp.full((1, 128), -1, jnp.int32)

    @pl.when(tm > 0)
    def _():
        id_copy.wait_recv()
        halo_copy(0).wait_recv()

    @pl.when(core == 0)
    def _():
        take(pbuf.at[pl.ds(0, 2)], p_r.at[2])

    @pl.when(core == 1)
    def _():
        take(pbuf.at[pl.ds(0, 4)], p_r.at[2])

    lane = lax.broadcasted_iota(jnp.int32, (L, 128), 1)
    lag = lax.broadcasted_iota(jnp.int32, (L, 128), 0)
    head = lane < lag

    def lagged(row):
        return pltpu.roll(jnp.broadcast_to(row, (L, 128)), 0, 1, stride=1, stride_axis=0)

    id_rows = [idh[...].astype(f32)] + [ids[:, t * 128:t * 128 + 128] for t in range(TILES)]
    rolled = [lagged(r) for r in id_rows]
    keep = []
    for t in range(TILES):
        source = jnp.where(head, rolled[t], rolled[t + 1])
        keep.append(source == jnp.broadcast_to(id_rows[t + 1], (L, 128)))

    pf[0] = jnp.transpose(jnp.concatenate([jnp.zeros((128 - L, K), f32), hbuf[...].astype(f32)], axis=0))
    for t in range(1, TILES + 1):
        pf[t] = pbuf[t].astype(f32)

    def build_row(k, carry):
        prior = lagged(pf[0, pl.ds(k, 1), :])
        for t in range(TILES):
            current = lagged(pf[t + 1, pl.ds(k, 1), :])
            value = jnp.where(keep[t], jnp.where(head, prior, current), 0.0)
            st[pl.ds(pl.multiple_of(k * L, L), L), t * 128:t * 128 + 128] = value.astype(bf16)
            prior = current
        return carry

    lax.fori_loop(0, K, build_row, 0, unroll=16)

    scale = F * K / TIME
    for b in range(3):
        span = slice(b * 256, b * 256 + 256)
        rec = jnp.dot(tmpl[...], st[:, span], preferred_element_type=f32)
        recon_sum = rec[BINS:BINS + 1] + rec[BINS + 1:BINS + 2] + rec[BINS + 2:BINS + 3]
        rec = rec[0:BINS]
        x = spec_ref[:, span].astype(f32)
        rat[:, span] = (scale / recon_sum - (scale / sums[1:2, span]) * (x / rec)).astype(bf16)
        sums[0:1, span] = recon_sum
        sbuf[fq, :, span] = jnp.sum(x * jnp.log(rec), axis=0, keepdims=True)

    def s_copy(i):
        return remote(sbuf.at[fq], sbuf.at[fq], s_s, s_r, tm, lax.rem(fq + i, NF))

    for i in range(1, NF):
        s_copy(i).start()

    def gradient(n):
        z = lax.rem(pz + ORDER[n], 4)
        g = lax.dot_general(
            st[pl.ds(pl.multiple_of(z * 1024, 1024), 1024), :], rat[...],
            (((1,), (1,)), ((), ())), preferred_element_type=f32).reshape(4, 4, 64, 256)
        grad[n, 0] = g[..., 0:128]
        grad[n, 1] = g[..., 128:256]

    class Ring:
        def __init__(self, view, buf, send, recv, axis, staged=None):
            self.view, self.buf, self.send, self.recv, self.staged = view, buf, send, recv, staged
            self.pos = positions[axis]
            to = (along(axis, 1), along(axis, 3))
            far, right, left = (lax.rem(self.pos + i, 4) for i in (2, 1, 3))
            self.parts = (
                (far, 0, to[0]), (right, 1, to[0]), (right, 0, to[0]),
                (far, 1, to[1]), (left, 0, to[1]), (left, 1, to[1]),
            )

        def copy(self, n):
            d, h, to = self.parts[n]
            src = self.view(d, h) if self.staged is None or n % 3 == 2 else self.staged.at[n]
            return remote(src, self.buf(n), self.send, self.recv.at[0 if n % 3 == 0 else 1], to, fq)

        def push(self, n, more=None):
            view = self.view(self.parts[n][0], self.parts[n][1])
            if more is not None:
                view[...] = view[...] + self.buf(more)[...].astype(f32)
            elif self.staged is not None:
                self.staged[n] = view[...].astype(self.staged.dtype)
            self.copy(n).start()

        def begin(self):
            for n in (0, 3, 1, 4):
                self.push(n)

        def relay(self):
            for n in (0, 3):
                self.push(n + 2, n)

        def result(self):
            return tuple(
                self.view(self.pos, h)[...] + self.buf(l)[...].astype(f32) + self.buf(r)[...].astype(f32)
                for h, l, r in ((0, 2, 4), (1, 1, 5)))

    def landing(n, c):
        return lambda i: r1f.at[n, c, i // 3] if i % 3 == 2 else r1.at[n, c, i]

    s1 = [[
        Ring(lambda d, h, n=n: grad.at[n, 0, pl.ds(2 * h, 2), d], landing(n, 0), rs1_s, rs1_r.at[n], 0, w1.at[n, 0]),
        Ring(lambda d, h, n=n: grad.at[n, 1, d, pl.ds(2 * h, 2)], landing(n, 1), rs1_s, rs1_r.at[n], 1, w1.at[n, 1]),
    ] for n in range(4)]
    s2 = [[
        Ring(lambda d, h, n=n, c=c: a1.at[n, c, d, pl.ds(32 * h, 32)], lambda i, n=n, c=c: r2.at[n, c, i], rs2_s, rs2_r.at[n], 1 - c)
        for c in range(2)] for n in range(4)]
    z_to = (along(2, 1), along(2, 3))

    def z_copy(n):
        piece, half = ((0, 0), (1, 1), (1, 0), (0, 1), (2, 0), (2, 1))[n]
        return remote(c3.at[piece, half], r3.at[n], rs3_s, rs3_r.at[(0, 2, 2, 1, 2, 2)[n]], z_to[n // 3], fq)

    def begin1(n):
        for ring in s1[n]:
            ring.begin()

    def relay1(n):
        take(w1.at[n, 0, pl.ds(0, 4)], rs1_r.at[n, 0])
        for ring in s1[n]:
            ring.relay()

    def begin2(n):
        take(w1.at[n], rs1_r.at[n, 1])
        for c in range(2):
            top, low = s1[n][c].result()
            a1[n, c, 0:2] = top
            a1[n, c, 2:4] = low
            s2[n][c].begin()

    def relay2(n):
        take(r2.at[n, 0, pl.ds(0, 4)], rs2_r.at[n, 0])
        for ring in s2[n]:
            ring.relay()

    def done2(n):
        take(r2.at[n, :, pl.ds(0, 4)], rs2_r.at[n, 1])
        for c in range(2):
            top, low = s2[n][c].result()
            c3[n, c, 0:32] = top
            c3[n, c, 32:64] = low
        if n == 0:
            z_copy(0).start()
            z_copy(3).start()
        elif n < 3:
            half, plain, held = ((1, 1, 0), (0, 4, 3))[n - 1]
            z_copy(plain).start()
            z_copy(held).wait_recv()
            c3[n, 1 - half] = c3[n, 1 - half] + r3[held]
            z_copy((2, 5)[n - 1]).start()

    gradient(0)
    begin1(0)
    gradient(1)
    begin1(1)
    gradient(2)
    relay1(0)
    begin1(2)
    gradient(3)
    relay1(1)
    begin1(3)
    begin2(0)
    relay1(2)
    begin2(1)
    relay2(0)
    relay1(3)
    begin2(2)
    relay2(1)
    done2(0)
    begin2(3)
    relay2(2)
    done2(1)
    relay2(3)
    done2(2)
    done2(3)
    take(sbuf.at[pl.ds(0, 3)], s_r)
    log_sum = sbuf[0] + sbuf[1] + sbuf[2] + sbuf[3]
    loss_ref[...] = jnp.log(sums[0:1]) - log_sum / sums[1:2]
    take(r3.at[pl.ds(0, 4)], rs3_r.at[2])
    out_ref[:, 0:128] = c3[3, 0] + r3[2] + r3[4]
    out_ref[:, 128:256] = c3[3, 1] + r3[1] + r3[5]

    sent(qbuf.at[pl.ds(0, 18)], q_s)
    sent(encf.at[pl.ds(0, 3)], enc_s)
    sent(sbuf.at[pl.ds(0, 3)], s_s)
    sent(tbuf.at[pl.ds(0, 3)], t_s)

    @pl.when(tm < TM - 1)
    def _():
        id_copy.wait_send()

    @pl.when(core == 0)
    def _():
        sent(normed.at[pl.ds(0, 4)], n_s)
        sent(pbuf.at[pl.ds(0, 6)], p_s)

    @pl.when(core == 1)
    def _():
        sent(normed.at[pl.ds(0, 5)], n_s)
        sent(pbuf.at[pl.ds(0, 3)], p_s)

    @pl.when((fq == NF - 1) & (tm < TM - 1))
    def _():
        sent(encf.at[0, pl.ds(0, 64)], h_s)

    sent(tmpl.at[pl.ds(0, BINS)], rs1_s)
    sent(grow, rs2_s)
    sent(pbuf.at[pl.ds(0, 3)], rs3_s)


def hand_over(loss_in, grad_in, loss_ref, grad_ref):
    loss_ref[...] = loss_in[...].reshape(FRAMES)
    grad_ref[...] = grad_in[...]


def on_device(
    spectrum, decay_rate, init_state, clip_ids, encoder, gauss_noise, uniform_noise, boost_count, templates,
):
    vmem = pl.BlockSpec(memory_space=pltpu.VMEM)
    hbm = pl.BlockSpec(memory_space=pl.ANY)
    V = pltpu.VMEM
    dma = pltpu.SemaphoreType.DMA
    loss, grad = pl.pallas_call(
        kernel,
        out_shape=(
            V((1, FRAMES), f32),
            V((K * L // TM, BINS), f32),
        ),
        in_specs=[vmem] * 4 + [hbm] * 5,
        out_specs=(vmem, vmem),
        scratch_shapes=[
            V((BINS, FRAMES), bf16), V((BINS + 16, K * L), bf16), V((2, K, 128), f32), V((2, 2, K, 128), f32), V((NF, K, BINS), bf16),
            V((BINS, FRAMES), f32), V((BINS, FRAMES), f32), V((TILES, BINS, 128), bf16),
            V((2, NF, BINS, 128), bf16), V((TILES + 1, K, 128), bf16), V((TILES + 1, K, 128), f32),
            V((L, K), bf16), V((L, K), bf16), V((1, 128), jnp.int32), V((1, 128), jnp.int32), V((20, 1, BINS), f32), V((K * L, FRAMES), bf16),
            V((NF, 1, K * L + FRAMES), f32), V((2, FRAMES), f32), V((NF, 1, FRAMES), f32), V((BINS, FRAMES), bf16),
            V((4, 2, 4, 4, 64, 128), f32), V((4, 2, 6, 2, 64, 128), bf16), V((4, 2, 4, 64, 128), f32),
            V((4, 2, 64, 128), f32), V((4, 2, 6, 2, 64, 128), bf16), V((4, 2, 2, 2, 64, 128), f32), V((4, 2, 6, 32, 128), f32), V((6, 64, 128), f32),
            dma((7,)), dma, dma, dma, dma((2,)), dma, dma((2,)), dma, dma, dma, dma((2,)), dma, dma((3,)), dma, dma, dma, dma,
            dma, dma((4, 2)), dma, dma((4, 2)), dma, dma((3,)),
        ],
        compiler_params=pltpu.CompilerParams(
            collective_id=0, has_side_effects=True, vmem_limit_bytes=56 * 1024 * 1024),
        name="topic_step",
    )(
        decay_rate.reshape(1, BINS), init_state.reshape(1, BINS), clip_ids,
        boost_count.reshape(1, K), spectrum, encoder, gauss_noise, uniform_noise, templates,
    )
    return pl.pallas_call(
        hand_over,
        out_shape=(jax.ShapeDtypeStruct((FRAMES,), f32), jax.ShapeDtypeStruct((K * L // TM, BINS), f32)),
        in_specs=[vmem] * 2,
        out_specs=(vmem, vmem),
        name="hand_over",
    )(loss, grad)


def solution(mesh):
    placed = (
        P("freq", "tm"), P("freq"), P("freq"), P("tm"), P(None, "freq"), P(None, "tm"),
        P(None, None, "tm"), P(), P("freq", None),
    )
    return jax.shard_map(
        on_device, mesh=mesh, in_specs=placed, out_specs=(P("tm"), P("tm", "freq")), check_vma=False
    )
```
